32 devices in a mesh: wide: 8 (over z, x), narrow: 4 (over y, core).
Axes of the slice: x: 2, y: 2, z: 4, core: 2. Of those that a mesh axis runs over, the one named last changes fastest.
Arguments:
- block_input: bfloat16 [32, 1024, 768], P(('wide', 'narrow')), may hold values from -6 to 6
- segments: int32 [32, 1024], P(('wide', 'narrow')), may hold values from 0 to 3, never falling along the last dimension, each value on 1 to 512 neighbouring positions
- real_mask: int32 [32, 1024], P(('wide', 'narrow')), may hold values from 0 to 1, as said below
- qkv_weight: bfloat16 [768, 2304], replicated, may hold values from -0.21875 to 0.21875
- attn_out_weight: bfloat16 [768, 768], replicated, may hold values from -1.75 to 1.75
- ffn_in_weight: bfloat16 [768, 3072], replicated, may hold values from -0.21875 to 0.21875
- ffn_bias: float32 [3072], replicated, may hold values from -3 to 3
- ffn_out_weight: bfloat16 [3072, 768], replicated, may hold values from -0.109375 to 0.109375
- first_gain: float32 [768], replicated, may hold values from 0.25 to 1.75
- first_shift: float32 [768], replicated, may hold values from -2 to 2
- second_gain: float32 [768], replicated, may hold values from 0.25 to 1.75
- second_shift: float32 [768], replicated, may hold values from -2 to 2
- adapter_down: bfloat16 [768, 16, 48], P(None, None, 'narrow'), may hold values from -0.21875 to 0.21875
- adapter_up: bfloat16 [16, 48, 768], P(None, 'narrow'), may hold values from -0.875 to 0.875
- joining_query: bfloat16 [768, 768], replicated, may hold values from -0.4375 to 0.4375
- joining_key: bfloat16 [768, 768], replicated, may hold values from -0.21875 to 0.21875
- joining_value: bfloat16 [768, 768], replicated, may hold values from -0.21875 to 0.21875
- cotangent: bfloat16 [32, 1024, 768], P(('wide', 'narrow')), may hold values from -6 to 6
Outputs:
- block_output: bfloat16 [32, 1024, 768], P(('wide', 'narrow'))
- input_grad: bfloat16 [32, 1024, 768], P(('wide', 'narrow'))
- query_grad: float32 [768, 768], replicated
- key_grad: float32 [768, 768], replicated
- value_grad: float32 [768, 768], replicated
- ffn_bias_grad: float32 [3072], replicated
- first_gain_grad: float32 [768], replicated
- first_shift_grad: float32 [768], replicated
- second_gain_grad: float32 [768], replicated
- second_shift_grad: float32 [768], replicated
- entropy: float32 [], replicated
The draws below stay inside these ranges and needn't reach their ends.
Inputs may be any that keep to these rules, and one draw needn't show every extreme that they name: `segments`: within a row the ids never fall; a row holds at most 4 documents of 1 to 512 tokens, and one of them has exactly 512. `real_mask`: in each row the real tokens form a leading run, and every row has at least one.
All inputs are finite; a program needn't handle non-finite values.
Results may differ from the reference program's by a relative error of at most 0.02.
Values may be sent and summed in bfloat16 or wider, within the bound.
A program may use at most 256 MiB of HBM per device.

```python
import math
import jax
import jax.numpy as jnp
import numpy as np
from jax import lax

D = 768
HEADS = 12
HEAD_DIM = 64
FF = 3072
ADAPTERS = 16
BOTTLE = 48
SEQ = 1024
DOCS = 4
ROWS = 32
DOC_MOST = 512


def draw_real_mask(key, part):
    row_ids = jnp.arange(ROWS, dtype=jnp.int32)
    least_count = SEQ // 3
    base_count = least_count + (SEQ - least_count) * row_ids // max(ROWS - 1, 1)
    jitter = jax.random.randint(key, (ROWS,), 0, max(SEQ // 16, 1), dtype=jnp.int32)
    real_count = jnp.maximum(base_count - jitter, 1)
    positions = jnp.arange(SEQ, dtype=jnp.int32)
    return (positions[None, :] < real_count[:, None]).astype(jnp.int32)


def block_scale(rng, dims, split, low, largest):
    def one(dim, blocks):
        draws = jax.random.uniform(jax.random.fold_in(jax.random.fold_in(rng, 6), dim), (blocks,), jnp.float32, low / len(split), largest / len(split))
        return jnp.repeat(jnp.exp(draws), dims[dim] // blocks).reshape((-1,) + (1,) * (len(dims) - dim - 1))

    factor_of = one(*split[0])
    for cut in split[1:]:
        factor_of = factor_of * one(*cut)
    return factor_of


def profile(number_of, total, reach, lean):
    weights = [(1 << 20) // math.isqrt(rank ** lean) + 1 for rank in range(2, number_of + 1)]
    surplus, counts = total - reach - (number_of - 1), [1] * (number_of - 1)
    while surplus > 0:
        candidates = [i for i in range(number_of - 1) if counts[i] < reach]
        mass, budget = sum([weights[i] for i in candidates]), surplus
        for i in candidates:
            extra = min(reach - counts[i], max(1, budget * weights[i] // mass), surplus)
            counts[i] = counts[i] + extra
            surplus = surplus - extra
    return np.array([reach] + counts)


def ragged_sizes(own_key, amount, total, bound, skew):
    if amount == 2:
        one = jax.random.randint(own_key, (), max(1, total - bound), min(bound, total - 1) + 1)
        return jnp.stack([one, total - one])
    tallies = jnp.asarray(profile(amount, total, bound, skew), jnp.int32)
    twos = (amount - 1) // 2
    source_of, receiver = tallies[1:1 + 2 * twos:2], tallies[2:2 + 2 * twos:2]
    margin = jnp.minimum(source_of - 1, bound - receiver)
    shifted = jax.random.randint(jax.random.fold_in(own_key, 1), (twos,), 0, 1 << 20) % (margin + 1)
    tallies = tallies.at[1:1 + 2 * twos:2].set(source_of - shifted).at[2:2 + 2 * twos:2].set(receiver + shifted)
    return tallies[jax.random.permutation(jax.random.fold_in(own_key, 2), amount)]


def centred(key, extent, deviation, bound, split=(), held_as=jnp.bfloat16):
    entries = deviation * jax.random.normal(key, extent, jnp.float32)
    if split:
        entries = entries * block_scale(key, extent, split, -0.22, 0.18)
    return jnp.clip(entries, -bound, bound).astype(held_as)


def setup_inputs(seed: int = 0) -> dict:
    keys = jax.random.split(jax.random.key(seed), 19)
    return {
        "block_input": centred(keys[0], (ROWS, SEQ, D), 1.0, 6.0, ((0, 32),)),
        "segments": jax.vmap(lambda own: jnp.searchsorted(jnp.cumsum(ragged_sizes(own, DOCS, SEQ, DOC_MOST, 0)), jnp.arange(SEQ), side="right"))(jax.random.split(keys[1], ROWS)).reshape((ROWS, SEQ)).astype(jnp.int32),
        "real_mask": draw_real_mask(jax.random.fold_in(keys[18], 71), 0),
        "qkv_weight": centred(keys[3], (D, 3 * D), D ** -0.5, 0.21875),
        "attn_out_weight": centred(keys[4], (D, D), (D // 64) ** -0.5, 1.75),
        "ffn_in_weight": centred(keys[5], (D, FF), D ** -0.5, 0.21875),
        "ffn_bias": centred(keys[6], (FF,), 0.5, 3.0, (), jnp.float32),
        "ffn_out_weight": centred(keys[7], (FF, D), FF ** -0.5, 0.109375),
        "first_gain": jnp.clip(1.0 + 0.15 * jax.random.normal(keys[8], (D,), jnp.float32), 0.25, 1.75),
        "first_shift": centred(keys[9], (D,), 0.3, 2.0, (), jnp.float32),
        "second_gain": jnp.clip(1.0 + 0.15 * jax.random.normal(keys[10], (D,), jnp.float32), 0.25, 1.75),
        "second_shift": centred(keys[11], (D,), 0.3, 2.0, (), jnp.float32),
        "adapter_down": centred(keys[12], (D, ADAPTERS, BOTTLE), D ** -0.5, 0.21875, ((2, 4),)),
        "adapter_up": centred(keys[13], (ADAPTERS, BOTTLE, D), BOTTLE ** -0.5, 0.875, ((1, 4),)),
        "joining_query": centred(keys[14], (D, D), (D // 4) ** -0.5, 0.4375),
        "joining_key": centred(keys[15], (D, D), D ** -0.5, 0.21875),
        "joining_value": centred(keys[16], (D, D), D ** -0.5, 0.21875),
        "cotangent": centred(keys[17], (ROWS, SEQ, D), 1.0, 6.0, ((0, 32),)),
    }


@jax.custom_vjp
def low(v):
    return lax.optimization_barrier(v.astype(jnp.bfloat16)).astype(jnp.float32)

@jax.custom_vjp
def low_back(v):
    return v

def low_keep(v):
    return (low(v), None)

def low_pass(kept, grad):
    return (grad,)

def back_keep(v):
    return (v, None)

def back_low(kept, grad):
    return (low(grad),)
low.defvjp(low_keep, low_pass)
low_back.defvjp(back_keep, back_low)
highest = lax.Precision.HIGHEST

def matmul(left_op, right_op):
    return jnp.dot(left_op, right_op, precision=highest, preferred_element_type=jnp.float32)

def layer_norm(values, gain_vec, shift_vec):
    centre = values - lax.optimization_barrier(jnp.mean(values, axis=-1, keepdims=True))
    factor = lax.rsqrt(lax.optimization_barrier(jnp.mean(centre * centre, axis=-1, keepdims=True)) + 1e-06)
    return centre * factor * gain_vec + shift_vec

def row_forward(trained, frozen, row_input, seg_row, real_row):
    query_w, key_w, value_w, bias_vec, gain_one, shift_one, gain_two, shift_two = trained
    qkv_w, attn_w, in_w, out_w, down_w, up_w = frozen
    seq_len = row_input.shape[0]
    packed = low_back(low(matmul(row_input, qkv_w)))
    head_view = packed.reshape(seq_len, 3, HEADS, HEAD_DIM)
    queries = head_view[:, 0]
    key_heads = head_view[:, 1]
    value_heads = head_view[:, 2]
    raw_scores = jnp.einsum('qhd,khd->hqk', queries, key_heads, precision=highest) * (1.0 / math.sqrt(HEAD_DIM))
    same_doc = seg_row[:, None] == seg_row[None, :]
    logits = jnp.where(same_doc[None], raw_scores, -1e+30)
    probs_full = jax.nn.softmax(logits, axis=-1)
    context = jnp.einsum('hqk,khd->qhd', low(probs_full), value_heads, precision=highest)
    context = low_back(low(context.reshape(seq_len, D)))
    attn_out = low_back(matmul(context, attn_w))
    h_one = layer_norm(row_input + attn_out, gain_one, shift_one)
    ffn_pre = low_back(matmul(low(h_one), in_w) + bias_vec)
    ffn_out = low_back(matmul(low(jax.nn.gelu(ffn_pre, approximate=False)), out_w))
    h_two = layer_norm(h_one + ffn_out, gain_two, shift_two)
    h_low = low(h_two)
    query_rows = low_back(low(matmul(h_low, query_w)))
    probe = low_back(low(matmul(query_rows, key_w.T)))
    down_pre = matmul(h_low, down_w)
    bottle = jax.nn.gelu(down_pre, approximate=False)
    guide = matmul(probe, up_w.T)
    scores = lax.optimization_barrier(jnp.sum((bottle * guide).reshape(seq_len, ADAPTERS, BOTTLE), axis=-1)) * (1.0 / math.sqrt(D))
    joining_weights = jax.nn.softmax(scores, axis=-1)
    mixed_rows = joining_weights[:, :, None] * bottle.reshape(seq_len, ADAPTERS, BOTTLE)
    mixed_rows = low(mixed_rows.reshape(seq_len, ADAPTERS * BOTTLE))
    update = low_back(matmul(mixed_rows, up_w))
    block_out = h_two + matmul(low(h_two + update), value_w)
    log_weights = scores - jax.nn.logsumexp(scores, axis=-1, keepdims=True)
    ent_row = jnp.sum(-lax.optimization_barrier(jnp.sum(joining_weights * log_weights, axis=-1)) * real_row)
    return (block_out, ent_row)

def reference(block_input, segments, real_mask, qkv_weight, attn_out_weight, ffn_in_weight, ffn_bias, ffn_out_weight, first_gain, first_shift, second_gain, second_shift, adapter_down, adapter_up, joining_query, joining_key, joining_value, cotangent):
    trained = (joining_query.astype(jnp.float32), joining_key.astype(jnp.float32), joining_value.astype(jnp.float32), ffn_bias, first_gain, first_shift, second_gain, second_shift)
    frozen = (qkv_weight.astype(jnp.float32), attn_out_weight.astype(jnp.float32), ffn_in_weight.astype(jnp.float32), ffn_out_weight.astype(jnp.float32), adapter_down.astype(jnp.float32).reshape(D, ADAPTERS * BOTTLE), adapter_up.astype(jnp.float32).reshape(ADAPTERS * BOTTLE, D))

    def one_row(carried, row_item):
        grad_sums, ent_total = carried
        row_input, seg_row, real_row, cot_row = row_item

        def forward_fn(params, inputs):
            return row_forward(params, frozen, inputs, seg_row, real_row)
        (row_out, ent_row), pullback = jax.vjp(forward_fn, trained, row_input)
        param_grads, row_grad = pullback((cot_row, jnp.zeros((), jnp.float32)))
        grad_sums = jax.tree.map(jnp.add, grad_sums, param_grads)
        return ((grad_sums, ent_total + ent_row), (row_out.astype(jnp.bfloat16), row_grad.astype(jnp.bfloat16)))
    zero_sums = jax.tree.map(jnp.zeros_like, trained)
    (grad_sums, ent_total), (block_output, input_grad) = lax.scan(one_row, (zero_sums, jnp.zeros((), jnp.float32)), (block_input.astype(jnp.float32), segments, real_mask.astype(jnp.float32), cotangent.astype(jnp.float32)))
    count_real = jnp.sum(real_mask.astype(jnp.float32))
    entropy = ent_total / count_real
    return (block_output, input_grad, grad_sums[0], grad_sums[1], grad_sums[2], grad_sums[3], grad_sums[4], grad_sums[5], grad_sums[6], grad_sums[7], entropy)
```

```python
import math

import jax
import jax.numpy as jnp
import functools

from jax import lax
from jax.experimental import pallas as pl
from jax.experimental.pallas import tpu as pltpu
from jax.sharding import PartitionSpec as P

D = 768
HEADS = 12
HEAD_DIM = 64
ADAPTERS = 16
BOTTLE = 48

AUG = 16
BF = jnp.bfloat16
F32 = jnp.float32
BLOCK_Q = 256
BLOCK_K = 128


def dot_on(left_op, right_op, left_dim, right_dim):
    return lax.dot_general(
        left_op,
        right_op,
        (((left_dim,), (right_dim,)), ((), ())),
        preferred_element_type=F32,
    )


def head_rows(part, head):
    return pl.ds(pl.multiple_of(part * D + head * HEAD_DIM, HEAD_DIM), HEAD_DIM)


def attend_kernel(bounds, x, w, seg, packed, ctx, lse, xt, qa, kt, m_s, l_s, o_s):
    seq = x.shape[0]
    xt[...] = x[...].T

    def project(step, unused):
        rows = pl.ds(pl.multiple_of(step * 256, 256), 256)
        packed[rows, :] = dot_on(w[:, rows], xt[...], 0, 0).astype(BF)
        return 0

    lax.fori_loop(0, w.shape[1] // 256, project, 0)
    row = lax.broadcasted_iota(jnp.int32, (AUG, seq), 0)
    same = row == seg[...]
    aug_q = jnp.where(same, 1.0, 0.0).astype(BF)
    aug_k = jnp.where((row < 4) & (~same), -1e30, 0.0).astype(BF)

    def prepare(head, unused):
        qa[head, :HEAD_DIM, :] = packed[head_rows(0, head), :] * jnp.asarray(0.125, BF)
        qa[head, HEAD_DIM:, :] = aug_q
        kt[head] = jnp.concatenate([packed[head_rows(1, head), :], aug_k], axis=0).T
        return 0

    lax.fori_loop(0, HEADS, prepare, 0)

    def query_block(i, unused):
        qs = pl.ds(pl.multiple_of(i * BLOCK_Q, BLOCK_Q), BLOCK_Q)
        for h in range(HEADS):
            m_s[h] = jnp.full((8, BLOCK_Q), -1e30, F32)
            l_s[h] = jnp.zeros((8, BLOCK_Q), F32)
            o_s[h] = jnp.zeros((HEAD_DIM, BLOCK_Q), F32)

        def key_block(j, unused):
            ks = pl.ds(pl.multiple_of(j * BLOCK_K, BLOCK_K), BLOCK_K)
            logits = [dot_on(kt[h, ks, :], qa[h, :, qs], 1, 0) for h in range(HEADS)]
            probs = []
            for h in range(HEADS):
                tile = logits[h].reshape(BLOCK_K // 8, 8, BLOCK_Q)
                top = jnp.max(jnp.max(tile, axis=0), axis=0, keepdims=True)
                old = m_s[h]
                new = jnp.maximum(old, jnp.broadcast_to(top, (8, BLOCK_Q)))
                decay = jnp.exp(old - new)
                prob = jnp.exp(tile - new[None])
                l_s[h] = l_s[h] * decay + jnp.sum(prob, axis=0)
                m_s[h] = new
                probs.append((prob.reshape(BLOCK_K, BLOCK_Q).astype(BF), decay))
            for h in range(HEADS):
                prob, decay = probs[h]
                part = dot_on(packed[2 * D + h * HEAD_DIM : 2 * D + (h + 1) * HEAD_DIM, ks], prob, 1, 0)
                kept = o_s[h].reshape(8, 8, BLOCK_Q) * decay[None]
                o_s[h] = kept.reshape(HEAD_DIM, BLOCK_Q) + part
            return 0

        lax.fori_loop(bounds[0, i], bounds[1, i], key_block, 0)
        for h in range(HEADS):
            total = jnp.sum(l_s[h], axis=0, keepdims=True)
            ctx[h * HEAD_DIM : (h + 1) * HEAD_DIM, qs] = (o_s[h] * (1.0 / total)).astype(BF)
            lse[h, :, qs] = m_s[h][:1] + jnp.log(total)
        return 0

    lax.fori_loop(0, seq // BLOCK_Q, query_block, 0)


def attend_back_kernel(bounds, packed, ctx, lse, gctx, seg, gp, qa, kt, da, vt, dq_s, dk_s, dv_s):
    seq = packed.shape[1]
    row = lax.broadcasted_iota(jnp.int32, (AUG, seq), 0)
    same = row == seg[...]
    aug_q = jnp.where(same, 1.0, 0.0)
    aug_k = jnp.where(row < 4, jnp.where(same, 0.0, -1e30), jnp.where(row < 7, 1.0, 0.0)).astype(BF)
    aug_v = jnp.where(row < 3, 1.0, 0.0).astype(BF)

    def minus_rows(value, base):
        rest = -value
        rows = jnp.zeros((AUG, seq), F32)
        for step in range(3):
            piece = rest.astype(BF).astype(F32)
            rows = jnp.where(row == base + step, jnp.broadcast_to(piece, (AUG, seq)), rows)
            rest = rest - piece
        return rows

    def prepare(head, unused):
        rows = head_rows(0, head)
        qa[head, :HEAD_DIM, :] = packed[rows, :] * jnp.asarray(0.125, BF)
        qa[head, HEAD_DIM:, :] = (aug_q + minus_rows(lse[head], 4)).astype(BF)
        kt[head] = jnp.concatenate([packed[head_rows(1, head), :], aug_k], axis=0).T
        vt[head] = jnp.concatenate([packed[head_rows(2, head), :], aug_v], axis=0).T
        grad = gctx[rows, :]
        inner = jnp.sum(grad.astype(F32) * ctx[rows, :].astype(F32), axis=0, keepdims=True)
        da[head, :HEAD_DIM, :] = grad
        da[head, HEAD_DIM:, :] = minus_rows(inner, 0).astype(BF)
        dk_s[head] = jnp.zeros((HEAD_DIM, seq), F32)
        dv_s[head] = jnp.zeros((HEAD_DIM, seq), F32)
        return 0

    lax.fori_loop(0, HEADS, prepare, 0)

    def query_block(i, unused):
        qs = pl.ds(pl.multiple_of(i * BLOCK_Q, BLOCK_Q), BLOCK_Q)
        for h in range(HEADS):
            dq_s[h] = jnp.zeros((HEAD_DIM, BLOCK_Q), F32)

        def key_block(j, unused):
            ks = pl.ds(pl.multiple_of(j * BLOCK_K, BLOCK_K), BLOCK_K)
            first, second = {}, {}
            lag = 4
            for t in range(HEADS + 2 * lag):
                if t < HEADS:
                    first[t] = (
                        dot_on(kt[t, ks, :], qa[t, :, qs], 1, 0),
                        dot_on(vt[t, ks, :], da[t, :, qs], 1, 0),
                    )
                h = t - lag
                if 0 <= h < HEADS:
                    logits, grad = first.pop(h)
                    prob = jnp.exp(logits)
                    second[h] = (prob.astype(BF), (prob * grad).astype(BF))
                h = t - 2 * lag
                if 0 <= h < HEADS:
                    prob, grad = second.pop(h)
                    dv_s[h, :, ks] += dot_on(da[h, :HEAD_DIM, qs], prob, 1, 1)
                    dk_s[h, :, ks] += dot_on(qa[h, :HEAD_DIM, qs], grad, 1, 1)
                    dq_s[h] += dot_on(packed[D + h * HEAD_DIM : D + (h + 1) * HEAD_DIM, ks], grad, 1, 0)
            return 0

        lax.fori_loop(bounds[0, i], bounds[1, i], key_block, 0)
        for h in range(HEADS):
            gp[h * HEAD_DIM : (h + 1) * HEAD_DIM, qs] = (dq_s[h] * 0.125).astype(BF)
        return 0

    lax.fori_loop(0, seq // BLOCK_Q, query_block, 0)

    def finish(head, unused):
        gp[head_rows(1, head), :] = dk_s[head].astype(BF)
        gp[head_rows(2, head), :] = dv_s[head].astype(BF)
        return 0

    lax.fori_loop(0, HEADS, finish, 0)


def key_bounds(seg):
    first = seg[::BLOCK_Q]
    last = seg[BLOCK_Q - 1 :: BLOCK_Q]
    low = jnp.sum((seg[None, :] < first[:, None]).astype(jnp.int32), axis=1)
    high = jnp.sum((seg[None, :] <= last[:, None]).astype(jnp.int32), axis=1)
    return jnp.stack([low // BLOCK_K, (high + BLOCK_K - 1) // BLOCK_K])


def in_vmem():
    return pl.BlockSpec(memory_space=pltpu.VMEM)


def attend(x, w, seg, bounds):
    seq = x.shape[0]
    return pl.pallas_call(
        attend_kernel,
        in_specs=[pl.BlockSpec(memory_space=pltpu.SMEM), in_vmem(), in_vmem(), in_vmem()],
        out_specs=[in_vmem(), in_vmem(), in_vmem()],
        out_shape=(
            jax.ShapeDtypeStruct((3 * D, seq), BF),
            jax.ShapeDtypeStruct((D, seq), BF),
            jax.ShapeDtypeStruct((HEADS, 1, seq), F32),
        ),
        scratch_shapes=[
            pltpu.VMEM((D, seq), BF),
            pltpu.VMEM((HEADS, HEAD_DIM + AUG, seq), BF),
            pltpu.VMEM((HEADS, seq, HEAD_DIM + AUG), BF),
            pltpu.VMEM((HEADS, 8, BLOCK_Q), F32),
            pltpu.VMEM((HEADS, 8, BLOCK_Q), F32),
            pltpu.VMEM((HEADS, HEAD_DIM, BLOCK_Q), F32),
        ],
        name="attend",
        compiler_params=pltpu.CompilerParams(vmem_limit_bytes=60 << 20),
    )(bounds, x, w, seg)


def attend_back(packed, ctx, lse, gctx, seg, bounds):
    seq = packed.shape[1]
    aug = HEAD_DIM + AUG
    return pl.pallas_call(
        attend_back_kernel,
        in_specs=[pl.BlockSpec(memory_space=pltpu.SMEM)] + [in_vmem() for _ in range(5)],
        out_specs=in_vmem(),
        out_shape=jax.ShapeDtypeStruct((3 * D, seq), BF),
        scratch_shapes=[
            pltpu.VMEM((HEADS, aug, seq), BF),
            pltpu.VMEM((HEADS, seq, aug), BF),
            pltpu.VMEM((HEADS, aug, seq), BF),
            pltpu.VMEM((HEADS, seq, aug), BF),
            pltpu.VMEM((HEADS, HEAD_DIM, BLOCK_Q), F32),
            pltpu.VMEM((HEADS, HEAD_DIM, seq), F32),
            pltpu.VMEM((HEADS, HEAD_DIM, seq), F32),
        ],
        name="attend_back",
        compiler_params=pltpu.CompilerParams(vmem_limit_bytes=62 << 20),
    )(bounds, packed, ctx, lse, gctx, seg)


def matmul(left_op, right_op):
    return jnp.dot(left_op, right_op, preferred_element_type=jnp.float32)


def contract_rows(left_op, right_op):
    return lax.dot_general(
        left_op, right_op, (((0,), (0,)), ((), ())), preferred_element_type=jnp.float32
    )


def contract_cols(left_op, right_op):
    return lax.dot_general(
        left_op, right_op, (((1,), (1,)), ((), ())), preferred_element_type=jnp.float32
    )


def normalize(values):
    centre = values - jnp.mean(values, axis=-1, keepdims=True)
    factor = lax.rsqrt(jnp.mean(centre * centre, axis=-1, keepdims=True) + 1e-06)
    return (centre * factor, factor)


def norm_back(grad_out, unit_vals, factor, gain_vec):
    scaled = grad_out * gain_vec
    return factor * (
        scaled
        - jnp.mean(scaled, axis=-1, keepdims=True)
        - unit_vals * jnp.mean(scaled * unit_vals, axis=-1, keepdims=True)
    )


def gelu_slope(values):
    return 0.5 * (1.0 + lax.erf(values * (1.0 / math.sqrt(2.0)))) + values * jnp.exp(
        -0.5 * values * values
    ) * (1.0 / math.sqrt(2.0 * math.pi))


def per_device(
    block_input,
    segments,
    real_mask,
    qkv_weight,
    attn_out_weight,
    ffn_in_weight,
    ffn_bias,
    ffn_out_weight,
    first_gain,
    first_shift,
    second_gain,
    second_shift,
    adapter_down,
    adapter_up,
    joining_query,
    joining_key,
    joining_value,
    cotangent,
):
    row_count, seq_len, width = block_input.shape
    token_count = row_count * seq_len
    mix_scale = 1.0 / math.sqrt(D)
    bank_width = ADAPTERS * BOTTLE
    down_full, up_full = (
        lax.all_gather(adapter_down, "narrow", axis=2, tiled=True),
        lax.all_gather(adapter_up, "narrow", axis=1, tiled=True),
    )
    down_flat = down_full.reshape(width, bank_width)
    up_flat = up_full.reshape(bank_width, width)

    tokens = block_input.reshape(token_count, width)
    seg_row = segments.reshape(1, token_count)
    bounds = key_bounds(segments.reshape(token_count))
    packed, context, log_total = attend(tokens, qkv_weight, seg_row, bounds)
    attn_out = contract_rows(context, attn_out_weight)
    unit_one, factor_one = normalize(tokens.astype(jnp.float32) + attn_out)
    h_one = unit_one * first_gain + first_shift
    ffn_pre = matmul(h_one.astype(jnp.bfloat16), ffn_in_weight) + ffn_bias
    act_low = jax.nn.gelu(ffn_pre, approximate=False).astype(jnp.bfloat16)
    ffn_out = matmul(act_low, ffn_out_weight)
    unit_two, factor_two = normalize(h_one + ffn_out)
    h_two = unit_two * second_gain + second_shift
    h_low = h_two.astype(jnp.bfloat16)
    query_low = matmul(h_low, joining_query).astype(jnp.bfloat16)
    probe_low = contract_cols(query_low, joining_key).astype(jnp.bfloat16)
    down_pre = matmul(h_low, down_flat)
    bottle = jax.nn.gelu(down_pre, approximate=False).reshape(token_count, ADAPTERS, BOTTLE)
    guide = contract_cols(probe_low, up_flat).reshape(token_count, ADAPTERS, BOTTLE)
    scores = jnp.sum(bottle * guide, axis=-1) * mix_scale
    shifted = scores - jnp.max(scores, axis=-1, keepdims=True)
    log_weights = shifted - jnp.log(jnp.sum(jnp.exp(shifted), axis=-1, keepdims=True))
    mix_weights = jnp.exp(log_weights)
    mixed_low = (
        (mix_weights[:, :, None] * bottle).reshape(token_count, bank_width).astype(jnp.bfloat16)
    )
    update = matmul(mixed_low, up_flat)
    blend_low = (h_two + update).astype(jnp.bfloat16)
    block_output = (h_two + matmul(blend_low, joining_value)).astype(jnp.bfloat16)
    real_rows = real_mask.reshape(token_count).astype(jnp.float32)
    ent_local = jnp.sum(-jnp.sum(mix_weights * log_weights, axis=-1) * real_rows)
    count_local = jnp.sum(real_rows)
    ent_total = lax.psum(ent_local, ("wide", "narrow"))
    grad_out = cotangent.reshape(token_count, width)
    value_grad = contract_rows(blend_low, grad_out)
    grad_blend = contract_cols(grad_out, joining_value)
    grad_update = grad_blend.astype(jnp.bfloat16)
    grad_mixed = contract_cols(grad_update, up_flat).reshape(token_count, ADAPTERS, BOTTLE)
    grad_weights = jnp.sum(grad_mixed * bottle, axis=-1)
    grad_scores = mix_weights * (
        grad_weights - jnp.sum(grad_weights * mix_weights, axis=-1, keepdims=True)
    )
    score_term = (grad_scores * mix_scale)[:, :, None]
    grad_guide = (score_term * bottle).reshape(token_count, bank_width)
    grad_bottle = (grad_mixed * mix_weights[:, :, None] + score_term * guide).reshape(
        token_count, bank_width
    )
    grad_down = grad_bottle * gelu_slope(down_pre)
    grad_probe = matmul(grad_guide.astype(BF), up_flat).astype(BF)
    key_grad = contract_rows(grad_probe, query_low)
    grad_query = matmul(grad_probe, joining_key).astype(jnp.bfloat16)
    query_grad = contract_rows(h_low, grad_query)
    adapter_back = contract_cols(grad_down.astype(BF), down_flat)
    grad_h_two = (
        grad_out.astype(jnp.float32)
        + grad_blend
        + adapter_back
        + contract_cols(grad_query, joining_query)
    )
    gain_two_grad = jnp.sum(grad_h_two * unit_two, axis=0)
    shift_two_grad = jnp.sum(grad_h_two, axis=0)
    grad_r_two = norm_back(grad_h_two, unit_two, factor_two, second_gain)
    grad_ffn = grad_r_two.astype(jnp.bfloat16)
    grad_pre = (contract_cols(grad_ffn, ffn_out_weight) * gelu_slope(ffn_pre)).astype(jnp.bfloat16)
    bias_grad = jnp.sum(grad_pre.astype(jnp.float32), axis=0)
    grad_h_one = grad_r_two + contract_cols(grad_pre, ffn_in_weight)
    gain_one_grad = jnp.sum(grad_h_one * unit_one, axis=0)
    shift_one_grad = jnp.sum(grad_h_one, axis=0)
    grad_r_one = norm_back(grad_h_one, unit_one, factor_one, first_gain)
    grad_attn = grad_r_one.astype(jnp.bfloat16)
    grad_context = contract_cols(attn_out_weight, grad_attn).astype(BF)
    grad_packed = attend_back(packed, context, log_total, grad_context, seg_row, bounds)
    input_grad = (grad_r_one + lax.dot_general(grad_packed, qkv_weight, (((0,), (1,)), ((), ())), preferred_element_type=F32)).astype(jnp.bfloat16)
    summed_all = lax.psum(
        (
            query_grad,
            key_grad,
            value_grad,
            bias_grad,
            gain_one_grad,
            shift_one_grad,
            gain_two_grad,
            shift_two_grad,
            count_local,
        ),
        ("wide", "narrow"),
    )
    summed = summed_all[:8]
    count_total = summed_all[8]
    entropy = ent_total / count_total
    return (
        block_output.reshape(row_count, seq_len, width),
        input_grad.reshape(row_count, seq_len, width),
        summed[0],
        summed[1],
        summed[2],
        summed[3],
        summed[4],
        summed[5],
        summed[6],
        summed[7],
        entropy,
    )


def solution(mesh):
    placed = (
        P(("wide", "narrow"), None, None),
        P(("wide", "narrow"), None),
        P(("wide", "narrow"), None),
        P(),
        P(),
        P(),
        P(),
        P(),
        P(),
        P(),
        P(),
        P(),
        P(None, None, "narrow"),
        P(None, "narrow", None),
        P(),
        P(),
        P(),
        P(("wide", "narrow"), None, None),
    )
    return jax.shard_map(
        per_device,
        mesh=mesh,
        in_specs=placed,
        out_specs=(
            P(("wide", "narrow"), None, None),
            P(("wide", "narrow"), None, None),
            P(),
            P(),
            P(),
            P(),
            P(),
            P(),
            P(),
            P(),
            P(),
        ),
        check_vma=False,
    )
```

```python
import math

import jax
import jax.numpy as jnp
import functools

from jax import lax
from jax.experimental import pallas as pl
from jax.experimental.pallas import tpu as pltpu
from jax.sharding import PartitionSpec as P

D = 768
HEADS = 12
HEAD_DIM = 64
ADAPTERS = 16
BOTTLE = 48

AUG = 16
BF = jnp.bfloat16
F32 = jnp.float32
BLOCK_Q = 256
BLOCK_K = 128
VMEM_BYTES = 64 << 20


def dot_on(left_op, right_op, left_dim, right_dim):
    return lax.dot_general(
        left_op,
        right_op,
        (((left_dim,), (right_dim,)), ((), ())),
        preferred_element_type=F32,
    )


def head_rows(part, head):
    return pl.ds(pl.multiple_of(part * D + head * HEAD_DIM, HEAD_DIM), HEAD_DIM)


def attend_kernel(bounds, x, w, seg, packed, ctx, lse, xt, qa, kt, m_s, l_s, o_s):
    seq = x.shape[0]
    xt[...] = x[...].T

    def project(step, unused):
        rows = pl.ds(pl.multiple_of(step * 256, 256), 256)
        packed[rows, :] = dot_on(w[:, rows], xt[...], 0, 0).astype(BF)
        return 0

    lax.fori_loop(0, w.shape[1] // 256, project, 0)
    row = lax.broadcasted_iota(jnp.int32, (AUG, seq), 0)
    same = row == seg[...]
    aug_q = jnp.where(same, 1.0, 0.0).astype(BF)
    aug_k = jnp.where((row < 4) & (~same), -1e30, 0.0).astype(BF)

    def prepare(head, unused):
        qa[head, :HEAD_DIM, :] = packed[head_rows(0, head), :] * jnp.asarray(0.125, BF)
        qa[head, HEAD_DIM:, :] = aug_q
        kt[head] = jnp.concatenate([packed[head_rows(1, head), :], aug_k], axis=0).T
        return 0

    lax.fori_loop(0, HEADS, prepare, 0)

    def query_block(i, unused):
        qs = pl.ds(pl.multiple_of(i * BLOCK_Q, BLOCK_Q), BLOCK_Q)
        for h in range(HEADS):
            m_s[h] = jnp.full((8, BLOCK_Q), -1e30, F32)
            l_s[h] = jnp.zeros((8, BLOCK_Q), F32)
            o_s[h] = jnp.zeros((HEAD_DIM, BLOCK_Q), F32)

        def key_block(j, unused):
            ks = pl.ds(pl.multiple_of(j * BLOCK_K, BLOCK_K), BLOCK_K)
            logits = [dot_on(kt[h, ks, :], qa[h, :, qs], 1, 0) for h in range(HEADS)]
            probs = []
            for h in range(HEADS):
                tile = logits[h].reshape(BLOCK_K // 8, 8, BLOCK_Q)
                top = jnp.max(jnp.max(tile, axis=0), axis=0, keepdims=True)
                old = m_s[h]
                new = jnp.maximum(old, jnp.broadcast_to(top, (8, BLOCK_Q)))
                decay = jnp.exp(old - new)
                prob = jnp.exp(tile - new[None])
                l_s[h] = l_s[h] * decay + jnp.sum(prob, axis=0)
                m_s[h] = new
                probs.append((prob.reshape(BLOCK_K, BLOCK_Q).astype(BF), decay))
            for h in range(HEADS):
                prob, decay = probs[h]
                part = dot_on(packed[2 * D + h * HEAD_DIM : 2 * D + (h + 1) * HEAD_DIM, ks], prob, 1, 0)
                kept = o_s[h].reshape(8, 8, BLOCK_Q) * decay[None]
                o_s[h] = kept.reshape(HEAD_DIM, BLOCK_Q) + part
            return 0

        lax.fori_loop(bounds[0, i], bounds[1, i], key_block, 0)
        for h in range(HEADS):
            total = jnp.sum(l_s[h], axis=0, keepdims=True)
            ctx[h * HEAD_DIM : (h + 1) * HEAD_DIM, qs] = (o_s[h] * (1.0 / total)).astype(BF)
            lse[h, :, qs] = m_s[h][:1] + jnp.log(total)
        return 0

    lax.fori_loop(0, seq // BLOCK_Q, query_block, 0)


def attend_back_kernel(bounds, packed, ctx, lse, gctx, seg, gp, qa, kt, da, vt, dq_s, dk_s, dv_s):
    seq = packed.shape[1]
    row = lax.broadcasted_iota(jnp.int32, (AUG, seq), 0)
    same = row == seg[...]
    aug_q = jnp.where(same, 1.0, 0.0)
    aug_k = jnp.where(row < 4, jnp.where(same, 0.0, -1e30), jnp.where(row < 7, 1.0, 0.0)).astype(BF)
    aug_v = jnp.where(row < 3, 1.0, 0.0).astype(BF)

    def minus_rows(value, base):
        rest = -value
        rows = jnp.zeros((AUG, seq), F32)
        for step in range(3):
            piece = rest.astype(BF).astype(F32)
            rows = jnp.where(row == base + step, jnp.broadcast_to(piece, (AUG, seq)), rows)
            rest = rest - piece
        return rows

    def prepare(head, unused):
        rows = head_rows(0, head)
        qa[head, :HEAD_DIM, :] = packed[rows, :] * jnp.asarray(0.125, BF)
        qa[head, HEAD_DIM:, :] = (aug_q + minus_rows(lse[head], 4)).astype(BF)
        kt[head] = jnp.concatenate([packed[head_rows(1, head), :], aug_k], axis=0).T
        vt[head] = jnp.concatenate([packed[head_rows(2, head), :], aug_v], axis=0).T
        grad = gctx[rows, :]
        inner = jnp.sum(grad.astype(F32) * ctx[rows, :].astype(F32), axis=0, keepdims=True)
        da[head, :HEAD_DIM, :] = grad
        da[head, HEAD_DIM:, :] = minus_rows(inner, 0).astype(BF)
        dk_s[head] = jnp.zeros((HEAD_DIM, seq), F32)
        dv_s[head] = jnp.zeros((HEAD_DIM, seq), F32)
        return 0

    lax.fori_loop(0, HEADS, prepare, 0)

    def query_block(i, unused):
        qs = pl.ds(pl.multiple_of(i * BLOCK_Q, BLOCK_Q), BLOCK_Q)
        for h in range(HEADS):
            dq_s[h] = jnp.zeros((HEAD_DIM, BLOCK_Q), F32)

        def key_block(j, unused):
            ks = pl.ds(pl.multiple_of(j * BLOCK_K, BLOCK_K), BLOCK_K)
            first, second = {}, {}
            lag = 4
            for t in range(HEADS + 2 * lag):
                if t < HEADS:
                    first[t] = (
                        dot_on(kt[t, ks, :], qa[t, :, qs], 1, 0),
                        dot_on(vt[t, ks, :], da[t, :, qs], 1, 0),
                    )
                h = t - lag
                if 0 <= h < HEADS:
                    logits, grad = first.pop(h)
                    prob = jnp.exp(logits)
                    second[h] = (prob.astype(BF), (prob * grad).astype(BF))
                h = t - 2 * lag
                if 0 <= h < HEADS:
                    prob, grad = second.pop(h)
                    dv_s[h, :, ks] += dot_on(da[h, :HEAD_DIM, qs], prob, 1, 1)
                    dk_s[h, :, ks] += dot_on(qa[h, :HEAD_DIM, qs], grad, 1, 1)
                    dq_s[h] += dot_on(packed[D + h * HEAD_DIM : D + (h + 1) * HEAD_DIM, ks], grad, 1, 0)
            return 0

        lax.fori_loop(bounds[0, i], bounds[1, i], key_block, 0)
        for h in range(HEADS):
            gp[h * HEAD_DIM : (h + 1) * HEAD_DIM, qs] = (dq_s[h] * 0.125).astype(BF)
        return 0

    lax.fori_loop(0, seq // BLOCK_Q, query_block, 0)

    def finish(head, unused):
        gp[head_rows(1, head), :] = dk_s[head].astype(BF)
        gp[head_rows(2, head), :] = dv_s[head].astype(BF)
        return 0

    lax.fori_loop(0, HEADS, finish, 0)


def key_bounds(seg):
    first = seg[::BLOCK_Q]
    last = seg[BLOCK_Q - 1 :: BLOCK_Q]
    low = jnp.sum((seg[None, :] < first[:, None]).astype(jnp.int32), axis=1)
    high = jnp.sum((seg[None, :] <= last[:, None]).astype(jnp.int32), axis=1)
    return jnp.stack([low // BLOCK_K, (high + BLOCK_K - 1) // BLOCK_K])


def in_vmem():
    return pl.BlockSpec(memory_space=pltpu.VMEM)


def attend(x, w, seg, bounds):
    seq = x.shape[0]
    return pl.pallas_call(
        attend_kernel,
        in_specs=[pl.BlockSpec(memory_space=pltpu.SMEM), in_vmem(), in_vmem(), in_vmem()],
        out_specs=[in_vmem(), in_vmem(), in_vmem()],
        out_shape=(
            jax.ShapeDtypeStruct((3 * D, seq), BF),
            jax.ShapeDtypeStruct((D, seq), BF),
            jax.ShapeDtypeStruct((HEADS, 1, seq), F32),
        ),
        scratch_shapes=[
            pltpu.VMEM((D, seq), BF),
            pltpu.VMEM((HEADS, HEAD_DIM + AUG, seq), BF),
            pltpu.VMEM((HEADS, seq, HEAD_DIM + AUG), BF),
            pltpu.VMEM((HEADS, 8, BLOCK_Q), F32),
            pltpu.VMEM((HEADS, 8, BLOCK_Q), F32),
            pltpu.VMEM((HEADS, HEAD_DIM, BLOCK_Q), F32),
        ],
        name="attend",
        compiler_params=pltpu.CompilerParams(vmem_limit_bytes=60 << 20),
    )(bounds, x, w, seg)


def attend_back(packed, ctx, lse, gctx, seg, bounds):
    seq = packed.shape[1]
    aug = HEAD_DIM + AUG
    return pl.pallas_call(
        attend_back_kernel,
        in_specs=[pl.BlockSpec(memory_space=pltpu.SMEM)] + [in_vmem() for _ in range(5)],
        out_specs=in_vmem(),
        out_shape=jax.ShapeDtypeStruct((3 * D, seq), BF),
        scratch_shapes=[
            pltpu.VMEM((HEADS, aug, seq), BF),
            pltpu.VMEM((HEADS, seq, aug), BF),
            pltpu.VMEM((HEADS, aug, seq), BF),
            pltpu.VMEM((HEADS, seq, aug), BF),
            pltpu.VMEM((HEADS, HEAD_DIM, BLOCK_Q), F32),
            pltpu.VMEM((HEADS, HEAD_DIM, seq), F32),
            pltpu.VMEM((HEADS, HEAD_DIM, seq), F32),
        ],
        name="attend_back",
        compiler_params=pltpu.CompilerParams(vmem_limit_bytes=62 << 20),
    )(bounds, packed, ctx, lse, gctx, seg)


def pieces(value):
    high = value.astype(BF)
    return high, (value - high.astype(F32)).astype(BF)


def normalize(values):
    centre = values - jnp.mean(values, axis=-1, keepdims=True)
    factor = lax.rsqrt(jnp.mean(centre * centre, axis=-1, keepdims=True) + 1e-06)
    return centre * factor, factor


def norm_back(scaled, unit_vals, factor):
    return factor * (
        scaled
        - jnp.mean(scaled, axis=-1, keepdims=True)
        - unit_vals * jnp.mean(scaled * unit_vals, axis=-1, keepdims=True)
    )


def gelu_parts(values):
    rising = 0.5 * (1.0 + lax.erf(values * (1.0 / math.sqrt(2.0))))
    bell = jnp.exp(-0.5 * values * values) * (1.0 / math.sqrt(2.0 * math.pi))
    return values * rising, rising + values * bell


def fold_rows(values):
    rows, columns = values.shape
    return jnp.sum(values.reshape(rows // 8, 8, columns), axis=0)


def staged(count, product, finish):
    held = {}
    for step in range(count + 1):
        if step < count:
            held[step] = product(step)
        if step >= 1:
            finish(step - 1, held.pop(step - 1))


MESH = pl.DeviceIdType.MESH
PLANE = 4
DEPTH = 4
OWN_ROWS = 24
PLANE_ROWS = 96
CORE_ROWS = 384


def place():
    wide, narrow = lax.axis_index("wide"), lax.axis_index("narrow")
    return wide // 2, lax.rem(wide, 2), narrow // 2, lax.rem(narrow, 2)


def device(z, x, y, core):
    return (z * 2 + x, y * 2 + core)


def plane_mate(step):
    z, x, y, core = place()
    return device(z, jnp.bitwise_xor(x, step // 2), jnp.bitwise_xor(y, step % 2), core)


def depth_mate(step):
    z, x, y, core = place()
    return device(lax.rem(z + step, DEPTH), x, y, core)


def core_mate():
    z, x, y, core = place()
    return device(z, x, y, 1 - core)


def remote(source, target, sems, slot, mate):
    return pltpu.make_async_remote_copy(
        src_ref=source,
        dst_ref=target,
        send_sem=sems.at[0, slot],
        recv_sem=sems.at[1, slot],
        device_id=mate,
        device_id_type=MESH,
    )


def greet(mates):
    barrier = pltpu.get_barrier_semaphore()
    for mate in mates:
        pl.semaphore_signal(barrier, inc=1, device_id=mate, device_id_type=MESH)
    return lambda: pl.semaphore_wait(barrier, len(mates))


class Scatter:
    def __init__(self, which, square, send, near, plane, small_send, small, gathered, sems):
        self.which, self.square, self.send, self.near, self.plane = which, square, send, near, plane
        self.small_send, self.small, self.gathered, self.sems = small_send, small, gathered, sems
        z, x, y, core = place()
        self.z, self.spot, self.core = z, x * 2 + y, core
        self.copies = []

    def rows(self, start, count):
        return pl.ds(pl.multiple_of(start, 8), count)

    def finish(self):
        for copy in self.copies:
            copy.wait()
        self.copies = []

    def go(self, source, target, slot, mate):
        copy = remote(source, target, self.sems, self.which * 10 + slot, mate)
        copy.start()
        self.copies.append(copy)

    def to_core(self):
        self.go(self.send.at[self.which], self.near.at[self.which], 0, core_mate())

    def to_plane(self):
        self.finish()
        for q in range(PLANE):
            rows = pl.ds(q * PLANE_ROWS, PLANE_ROWS)
            total = self.square[rows, :] + self.near[self.which, q].astype(F32)
            self.square[rows, :] = total
            self.send[self.which, q] = total.astype(BF)
        for step in range(1, PLANE):
            spot = jnp.bitwise_xor(self.spot, step)
            self.go(self.send.at[self.which, spot], self.plane.at[self.which, step - 1], step, plane_mate(step))

    def to_depth(self):
        self.finish()
        rows = self.rows(self.spot * PLANE_ROWS, PLANE_ROWS)
        total = self.square[rows, :]
        for step in range(1, PLANE):
            total = total + self.plane[self.which, step - 1].astype(F32)
        self.square[rows, :] = total
        for k in range(DEPTH):
            self.small_send[self.which, k] = total[k * OWN_ROWS : (k + 1) * OWN_ROWS, :].astype(BF)
        for step in range(1, DEPTH):
            spot = lax.rem(self.z + step, DEPTH)
            self.go(
                self.small_send.at[self.which, spot],
                self.small.at[self.which, step - 1],
                PLANE - 1 + step,
                depth_mate(step),
            )

    def share(self):
        self.finish()
        start = self.spot * PLANE_ROWS + self.z * OWN_ROWS
        total = self.square[self.rows(start, OWN_ROWS), :]
        for step in range(1, DEPTH):
            total = total + self.small[self.which, step - 1].astype(F32)
        self.gathered[self.which, self.z] = total.astype(BF)
        mine = self.gathered.at[self.which, self.z]
        for step in range(1, DEPTH):
            self.go(mine, mine, PLANE + DEPTH - 2 + step, depth_mate(step))


ROWS_AT_ONCE = 256
HIDDEN_AT_ONCE = 512


def middle_kernel(
    shard_units, joined, x_h, g_h, ctx_h, wo_h, win_h, wout_h, bank_h, wq_h, wk_h, wv_h,
    bias, gain_one, shift_one, gain_two, shift_two, mask,
    out_h, gr_h, gctx_h, v_h, gg_h, sums_out,
    x, g, ctx, wo, win, wout, bank, wq, wk, wv,
    unit_one, unit_two, bottle, guide, total, act, slope, low, factor, mix,
    v_s, gg_s, sums, sums_part, in_sem, out_sem, *links,
):
    seq, width = x.shape
    blocks = seq // ROWS_AT_ONCE
    mix_scale = 1.0 / math.sqrt(D)
    loads = {}
    names = ("ctx", "wo", "x", "win", "wout", "wq", "wk", "bank", "g", "wv")
    sources = (ctx_h, wo_h, x_h, win_h, wout_h, wq_h, wk_h, bank_h, g_h, wv_h)
    targets = (ctx, wo, x, win, wout, wq, wk, bank, g, wv)
    if joined:
        send, near, plane, small_send, small, gathered, sums_near, sums_plane, link_sems, bank_sems, sums_sems = links
        arrived = greet(
            [core_mate()]
            + [plane_mate(step) for step in range(1, PLANE)]
            + [depth_mate(step) for step in range(1, DEPTH)]
        )
        spot = lax.axis_index("narrow")
        shard = bank_h.shape[1]

        def bank_rows(index):
            return bank.at[:, pl.ds(pl.multiple_of(index * shard, 16), shard), :]

        targets = targets[:7] + (bank_rows(spot),) + targets[8:]
    for number, name in enumerate(names):
        loads[name] = pltpu.make_async_copy(sources[number], targets[number], in_sem.at[number])
    for name in (("bank",) + names[:7] + names[8:]) if joined else names:
        loads[name].start()

    def rows_of(step):
        return pl.ds(step * ROWS_AT_ONCE, ROWS_AT_ONCE)

    t_one, t_two, t_three, t_four = (pl.ds(k * width, width) for k in range(4))
    down, up = 0, 1
    column = lax.broadcasted_iota(jnp.int32, (ADAPTERS, width), 1)
    owner = lax.rem(column, ADAPTERS * shard_units) // shard_units
    chosen = jnp.where(
        owner == lax.broadcasted_iota(jnp.int32, (ADAPTERS, width), 0), 1.0, 0.0
    ).astype(BF)

    def per_adapter(values):
        high, rest = pieces(values)
        return dot_on(chosen, high, 1, 1) + dot_on(chosen, rest, 1, 1)

    def per_unit(values):
        high, rest = pieces(values)
        return dot_on(high, chosen, 0, 0) + dot_on(rest, chosen, 0, 0)

    loads["ctx"].wait()
    loads["wo"].wait()
    loads["x"].wait()

    def finish_first(step, part):
        rows = rows_of(step)
        unit, scale = normalize(x[rows, :].astype(F32) + part)
        unit_one[rows, :] = unit
        factor[rows, 0:1] = scale
        low[rows, :] = (unit * gain_one[...] + shift_one[...]).astype(BF)

    if joined:
        arrived()
        loads["bank"].wait()
        bank_copies = [
            remote(bank_rows(spot), bank_rows(spot), bank_sems, 0, core_mate()),
            remote(bank_rows(spot), bank_rows(spot), bank_sems, 1, plane_mate(1)),
        ]
        for copy in bank_copies:
            copy.start()
    staged(blocks, lambda step: dot_on(ctx[:, rows_of(step)], wo[...], 0, 0), finish_first)

    loads["win"].wait()

    def hidden(chunk, unused):
        columns = pl.ds(pl.multiple_of(chunk * HIDDEN_AT_ONCE, HIDDEN_AT_ONCE), HIDDEN_AT_ONCE)

        def finish(step, part):
            rows = rows_of(step)
            value, rising = gelu_parts(part + bias[:, columns])
            act[rows, columns] = value.astype(BF)
            slope[rows, columns] = rising.astype(BF)

        staged(blocks, lambda step: dot_on(low[rows_of(step), :], win[:, columns], 1, 0), finish)
        return 0

    lax.fori_loop(0, win.shape[1] // HIDDEN_AT_ONCE, hidden, 0)
    loads["wout"].wait()

    def second(half, unused):
        def rows_in(step):
            start = half * (seq // 2) + step * ROWS_AT_ONCE
            return pl.ds(pl.multiple_of(start, ROWS_AT_ONCE), ROWS_AT_ONCE)

        def finish(step, part):
            rows = rows_in(step)
            unit, scale = normalize(unit_one[rows, :] * gain_one[...] + shift_one[...] + part)
            unit_two[rows, :] = unit
            factor[rows, 1:2] = scale
            low[rows, :] = (unit * gain_two[...] + shift_two[...]).astype(BF)

        staged(blocks // 2, lambda step: dot_on(act[rows_in(step), :], wout[...], 1, 0), finish)
        return 0

    lax.fori_loop(0, 2, second, 0)

    def h_two(rows):
        return unit_two[rows, :] * gain_two[...] + shift_two[...]

    if joined:
        bank_copies[1].wait()
        other = jnp.bitwise_xor(spot, 2)
        bank_copies[1] = remote(bank_rows(other), bank_rows(other), bank_sems, 2, core_mate())
        bank_copies[1].start()
    loads["wq"].wait()

    def keep(place):
        def finish(step, part):
            act[rows_of(step), place] = part.astype(BF)

        return finish

    staged(blocks, lambda step: dot_on(low[rows_of(step), :], wq[...], 1, 0), keep(t_one))
    loads["wk"].wait()
    staged(blocks, lambda step: dot_on(act[rows_of(step), t_one], wk[...], 1, 1), keep(t_two))
    if joined:
        for copy in bank_copies:
            copy.wait()
    else:
        loads["bank"].wait()

    def finish_down(step, part):
        rows = rows_of(step)
        value, rising = gelu_parts(part)
        bottle[rows, :] = value
        act[rows, t_four] = rising.astype(BF)

    staged(blocks, lambda step: dot_on(low[rows_of(step), :], bank[down], 1, 1), finish_down)

    def finish_guide(step, part):
        rows = rows_of(step)
        guide[rows, :] = part
        value = bottle[rows, :]
        scores = per_adapter(value * part) * mix_scale
        shifted = scores - jnp.max(scores, axis=0, keepdims=True)
        log_weights = shifted - jnp.log(jnp.sum(jnp.exp(shifted), axis=0, keepdims=True))
        weights = jnp.exp(log_weights)
        mix[:, rows] = weights
        sums[step : step + 1, :ROWS_AT_ONCE] = -jnp.sum(weights * log_weights, axis=0, keepdims=True)
        act[rows, t_one] = (per_unit(weights) * value).astype(BF)

    staged(blocks, lambda step: dot_on(act[rows_of(step), t_two], bank[up], 1, 1), finish_guide)
    real = mask[...].astype(F32)
    ent = jnp.zeros((1, 1), F32)
    for step in range(blocks):
        part = sums[step : step + 1, :ROWS_AT_ONCE] * real[:, step * ROWS_AT_ONCE : (step + 1) * ROWS_AT_ONCE]
        ent = ent + jnp.sum(part, axis=1, keepdims=True)
    sums_out[8:9, :] = jnp.broadcast_to(ent, (1, width))
    sums_out[9:10, :] = jnp.broadcast_to(jnp.sum(real, axis=1, keepdims=True), (1, width))
    sums_out[10:16, :] = jnp.zeros((6, width), F32)

    def finish_update(step, part):
        rows = rows_of(step)
        act[rows, t_two] = (h_two(rows) + part).astype(BF)

    staged(blocks, lambda step: dot_on(act[rows_of(step), t_one], bank[up], 1, 0), finish_update)

    loads["g"].wait()
    third = width // 3

    def over_tokens(left, right, target):
        def product(step):
            return dot_on(left(pl.ds(step * third, third)), right, 0, 0)

        def finish(step, part):
            target[pl.ds(step * third, third), :] = part

        staged(3, product, finish)

    def halves(left, base, right, target, which):
        core = place()[3]

        def product(step):
            start = base + (core if step else 1 - core) * CORE_ROWS
            return dot_on(left[:, pl.ds(pl.multiple_of(start, 128), CORE_ROWS)], right, 0, 0)

        def finish(step, part):
            if step:
                target[...] = part
            else:
                for q in range(PLANE):
                    send[which, q] = part[q * PLANE_ROWS : (q + 1) * PLANE_ROWS, :].astype(BF)

        staged(2, product, finish)

    if joined:
        halves(act, width, g[...], v_s, 0)
    else:
        over_tokens(lambda cols: act[:, pl.ds(width + cols.start, third)], g[...], v_s)
    if joined:
        value_sum, joint_sum = (
            Scatter(k, square, send, near, plane, small_send, small, gathered, link_sems)
            for k, square in enumerate((v_s, gg_s))
        )
        value_sum.to_core()
    else:
        v_out = pltpu.make_async_copy(v_s, v_h, out_sem.at[0])
        v_out.start()

    loads["wv"].wait()

    def finish_out(step, part):
        rows = rows_of(step)
        x[rows, :] = (h_two(rows) + part).astype(BF)

    staged(blocks, lambda step: dot_on(act[rows_of(step), t_two], wv[...], 1, 0), finish_out)
    out_copy = pltpu.make_async_copy(x, out_h, out_sem.at[1])
    out_copy.start()

    def finish_blend(step, part):
        rows = rows_of(step)
        total[rows, :] = g[rows, :].astype(F32) + part
        act[rows, t_one] = part.astype(BF)

    staged(blocks, lambda step: dot_on(g[rows_of(step), :], wv[...], 1, 1), finish_blend)

    if joined:
        value_sum.to_plane()

    def finish_mixed(step, part):
        rows = rows_of(step)
        value = bottle[rows, :]
        weights = mix[:, rows]
        grad_weights = per_adapter(part * value)
        grad_scores = weights * (grad_weights - jnp.sum(grad_weights * weights, axis=0, keepdims=True))
        score_term = per_unit(grad_scores * mix_scale)
        act[rows, t_one] = (score_term * value).astype(BF)
        grad_bottle = part * per_unit(weights) + score_term * guide[rows, :]
        act[rows, t_three] = (grad_bottle * act[rows, t_four].astype(F32)).astype(BF)

    staged(blocks, lambda step: dot_on(act[rows_of(step), t_one], bank[up], 1, 1), finish_mixed)
    staged(blocks, lambda step: dot_on(act[rows_of(step), t_one], bank[up], 1, 0), keep(t_two))
    if joined:
        halves(low, 0, act[:, t_two], gg_s, 1)
    else:
        over_tokens(lambda cols: low[:, cols], act[:, t_two], gg_s)
    if joined:
        joint_sum.to_core()
    else:
        gg_out = pltpu.make_async_copy(gg_s, gg_h, out_sem.at[2])
        gg_out.start()
    staged(blocks, lambda step: dot_on(act[rows_of(step), t_two], wk[...], 1, 0), keep(t_one))
    partial = [jnp.zeros((8, width), F32) for unused in range(4)]

    def finish_two(step, part):
        rows = rows_of(step)
        grad = total[rows, :] + part
        unit = unit_two[rows, :]
        partial[0] = partial[0] + fold_rows(grad * unit)
        partial[1] = partial[1] + fold_rows(grad)
        back = norm_back(grad * gain_two[...], unit, factor[rows, 1:2])
        total[rows, :] = back
        low[rows, :] = back.astype(BF)

    staged(
        blocks,
        lambda step: dot_on(act[rows_of(step), t_three], bank[down], 1, 0)
        + dot_on(act[rows_of(step), t_one], wq[...], 1, 1),
        finish_two,
    )

    if joined:
        joint_sum.to_plane()
        value_sum.to_depth()

    def hidden_back(chunk, unused):
        columns = pl.ds(pl.multiple_of(chunk * HIDDEN_AT_ONCE, HIDDEN_AT_ONCE), HIDDEN_AT_ONCE)
        held = [jnp.zeros((8, HIDDEN_AT_ONCE), F32)]

        def finish(step, part):
            rows = rows_of(step)
            grad = (part * slope[rows, columns].astype(F32)).astype(BF)
            act[rows, columns] = grad
            held[0] = held[0] + fold_rows(grad.astype(F32))

        staged(blocks, lambda step: dot_on(low[rows_of(step), :], wout[columns, :], 1, 1), finish)
        for piece in range(HIDDEN_AT_ONCE // 256):
            lanes = slice(piece * 256, (piece + 1) * 256)
            sums_part[chunk * (HIDDEN_AT_ONCE // 256) + piece] = held[0][:, lanes]
        return 0

    lax.fori_loop(0, win.shape[1] // HIDDEN_AT_ONCE, hidden_back, 0)
    for number in range(win.shape[1] // 256):
        lanes = pl.ds((number % 3) * 256, 256)
        sums_out[number // 3 : number // 3 + 1, lanes] = jnp.sum(sums_part[number], axis=0, keepdims=True)
    sums_out[4:5, :] = jnp.sum(partial[0], axis=0, keepdims=True)
    sums_out[5:6, :] = jnp.sum(partial[1], axis=0, keepdims=True)
    if joined:
        value_sum.share()
        joint_sum.to_depth()

    def first_back(half, carried):
        def rows_in(step):
            start = half * (seq // 2) + step * ROWS_AT_ONCE
            return pl.ds(pl.multiple_of(start, ROWS_AT_ONCE), ROWS_AT_ONCE)

        held = list(carried)

        def finish(step, part):
            rows = rows_in(step)
            grad = total[rows, :] + part
            unit = unit_one[rows, :]
            held[0] = held[0] + fold_rows(grad * unit)
            held[1] = held[1] + fold_rows(grad)
            back = norm_back(grad * gain_one[...], unit, factor[rows, 0:1])
            total[rows, :] = back
            low[rows, :] = back.astype(BF)

        staged(blocks // 2, lambda step: dot_on(act[rows_in(step), :], win[...], 1, 1), finish)
        return tuple(held)

    zero = jnp.zeros((8, width), F32)
    gain_sum, shift_sum = lax.fori_loop(0, 2, first_back, (zero, zero))
    sums_out[6:7, :] = jnp.sum(gain_sum, axis=0, keepdims=True)
    sums_out[7:8, :] = jnp.sum(shift_sum, axis=0, keepdims=True)
    if joined:
        near_copy = remote(sums_out, sums_near, sums_sems, 0, core_mate())
        near_copy.start()
        joint_sum.share()
    gr_copy = pltpu.make_async_copy(total, gr_h, out_sem.at[3])
    gr_copy.start()

    def finish_ctx(step, part):
        ctx[pl.ds(step * third, third), :] = part.astype(BF)

    staged(3, lambda step: dot_on(wo[pl.ds(step * third, third), :], low[...], 1, 1), finish_ctx)
    gctx_copy = pltpu.make_async_copy(ctx, gctx_h, out_sem.at[4])
    gctx_copy.start()
    if joined:
        near_copy.wait()
        sums_out[...] = sums_out[...] + sums_near[...]
        plane_copies = [
            remote(sums_out, sums_plane.at[step - 1], sums_sems, step, plane_mate(step)) for step in range(1, PLANE)
        ]
        for copy in plane_copies:
            copy.start()
        value_sum.finish()
        joint_sum.finish()
        v_out = pltpu.make_async_copy(gathered, v_h, out_sem.at[0])
        v_out.start()
        for copy in plane_copies:
            copy.wait()
        sums_out[...] = sums_out[...] + sums_plane[0] + sums_plane[1] + sums_plane[2]
    else:
        gg_out.wait()
    v_out.wait()
    out_copy.wait()
    gr_copy.wait()
    gctx_copy.wait()


def middle(joined, units, x, g, ctx, wo, win, wout, bank, wq, wk, wv, bias, gain_one, shift_one, gain_two, shift_two, mask):
    seq, width = x.shape
    hidden = win.shape[1]
    anywhere = pl.BlockSpec(memory_space=pl.ANY)
    token_low = pltpu.VMEM((seq, width), BF)
    token_wide = pltpu.VMEM((seq, width), F32)
    square = pltpu.VMEM((width, width), BF)
    sum_square = pltpu.VMEM((CORE_ROWS if joined else width, width), F32)
    links = [
        pltpu.VMEM((2, PLANE, PLANE_ROWS, width), BF),
        pltpu.VMEM((2, PLANE, PLANE_ROWS, width), BF),
        pltpu.VMEM((2, PLANE - 1, PLANE_ROWS, width), BF),
        pltpu.VMEM((2, DEPTH, OWN_ROWS, width), BF),
        pltpu.VMEM((2, DEPTH - 1, OWN_ROWS, width), BF),
        pltpu.VMEM((2, DEPTH, OWN_ROWS, width), BF),
        pltpu.VMEM((16, width), F32),
        pltpu.VMEM((PLANE - 1, 16, width), F32),
        pltpu.SemaphoreType.DMA((2, 20)),
        pltpu.SemaphoreType.DMA((2, 3)),
        pltpu.SemaphoreType.DMA((2, PLANE)),
    ]
    return pl.pallas_call(
        functools.partial(middle_kernel, units, joined),
        in_specs=[anywhere] * 10 + [in_vmem() for unused in range(6)],
        out_specs=[anywhere] * 5 + [in_vmem()],
        out_shape=(
            jax.ShapeDtypeStruct((seq, width), BF),
            jax.ShapeDtypeStruct((seq, width), F32),
            jax.ShapeDtypeStruct((width, seq), BF),
            jax.ShapeDtypeStruct((2, DEPTH, OWN_ROWS, width), BF)
            if joined
            else jax.ShapeDtypeStruct((width, width), F32),
            jax.ShapeDtypeStruct((8, 128) if joined else (width, width), F32),
            jax.ShapeDtypeStruct((16, width), F32),
        ),
        scratch_shapes=[
            token_low, token_low, pltpu.VMEM((width, seq), BF),
            square, pltpu.VMEM((width, hidden), BF), pltpu.VMEM((hidden, width), BF),
            pltpu.VMEM((2, width, width), BF), square, square, square,
            token_wide, token_wide, token_wide, token_wide, token_wide,
            pltpu.VMEM((seq, hidden), BF), pltpu.VMEM((seq, hidden), BF), token_low,
            pltpu.VMEM((seq, 2), F32), pltpu.VMEM((ADAPTERS, seq), F32),
            sum_square, sum_square,
            pltpu.VMEM((8, ROWS_AT_ONCE), F32), pltpu.VMEM((hidden // 256, 8, 256), F32),
            pltpu.SemaphoreType.DMA((10,)), pltpu.SemaphoreType.DMA((5,)),
        ]
        + (links if joined else []),
        name="middle",
        compiler_params=pltpu.CompilerParams(
            vmem_limit_bytes=VMEM_BYTES, **(dict(collective_id=0, has_side_effects=True) if joined else {})
        ),
    )(x, g, ctx, wo, win, wout, bank, wq, wk, wv, bias, gain_one, shift_one, gain_two, shift_two, mask)

def close_kernel(
    grad_row, grad_packed, w_h, mine_h, first_h, second_h, third_h, sums_in,
    input_grad, held_h, sums_out,
    w, held, sums_depth, w_sem, held_sems, out_sem, core_sems, sums_sems,
):
    z, x, y, core = place()
    spot = x * 2 + y
    arrived = greet([core_mate()] + [depth_mate(step) for step in range(1, DEPTH)])
    w_copy = pltpu.make_async_copy(w_h, w, w_sem)
    w_copy.start()
    arrived()
    sums_copies = [
        remote(sums_in, sums_depth.at[step - 1], sums_sems, step - 1, depth_mate(step)) for step in range(1, DEPTH)
    ]
    for copy in sums_copies:
        copy.start()
    fills = []
    for step, source in enumerate((mine_h, first_h, second_h, third_h)):
        fills.append(
            pltpu.make_async_copy(source, held.at[core, jnp.bitwise_xor(spot, step)], held_sems.at[step])
        )
        fills[-1].start()
    for fill in fills:
        fill.wait()
    across = remote(held.at[core], held.at[core], core_sems, 0, core_mate())
    across.start()
    w_copy.wait()
    blocks = grad_row.shape[0] // ROWS_AT_ONCE

    def finish(step, part):
        rows = pl.ds(step * ROWS_AT_ONCE, ROWS_AT_ONCE)
        input_grad[rows, :] = (grad_row[rows, :] + part).astype(BF)

    staged(
        blocks,
        lambda step: dot_on(grad_packed[:, pl.ds(step * ROWS_AT_ONCE, ROWS_AT_ONCE)], w[...], 0, 1),
        finish,
    )
    across.wait()
    out = pltpu.make_async_copy(held, held_h, out_sem)
    out.start()
    for copy in sums_copies:
        copy.wait()
    sums_out[...] = sums_in[...] + sums_depth[0] + sums_depth[1] + sums_depth[2]
    out.wait()


def close(grad_row, grad_packed, w, pieces_held, sums):
    seq, width = grad_row.shape
    anywhere = pl.BlockSpec(memory_space=pl.ANY)
    held = (2, PLANE, 2, DEPTH, OWN_ROWS, width)
    return pl.pallas_call(
        close_kernel,
        in_specs=[in_vmem(), in_vmem()] + [anywhere] * 5 + [in_vmem()],
        out_specs=[in_vmem(), anywhere, in_vmem()],
        out_shape=(
            jax.ShapeDtypeStruct((seq, width), BF),
            jax.ShapeDtypeStruct(held, BF),
            jax.ShapeDtypeStruct((16, width), F32),
        ),
        scratch_shapes=[
            pltpu.VMEM(w.shape, BF),
            pltpu.VMEM(held, BF),
            pltpu.VMEM((DEPTH - 1, 16, width), F32),
            pltpu.SemaphoreType.DMA,
            pltpu.SemaphoreType.DMA((PLANE,)),
            pltpu.SemaphoreType.DMA,
            pltpu.SemaphoreType.DMA((2, 1)),
            pltpu.SemaphoreType.DMA((2, DEPTH - 1)),
        ],
        name="close",
        compiler_params=pltpu.CompilerParams(
            vmem_limit_bytes=VMEM_BYTES, collective_id=1, has_side_effects=True
        ),
    )(grad_row, grad_packed, w, *pieces_held, sums)


def products_kernel(held, wk, wq, value_grad, query_grad, key_grad, joint):
    for core in range(2):
        for spot in range(PLANE):
            for z in range(DEPTH):
                start = core * CORE_ROWS + spot * PLANE_ROWS + z * OWN_ROWS
                rows = pl.ds(start, OWN_ROWS)
                value_grad[rows, :] = held[core, spot, 0, z].astype(F32)
                joint[rows, :] = held[core, spot, 1, z].astype(F32)
    low = joint[...].astype(BF)
    query_grad[...] = dot_on(low, wk[...], 1, 0)
    key_grad[...] = dot_on(low, wq[...], 0, 0)


def products(held, wk, wq):
    width = wk.shape[0]
    square = jax.ShapeDtypeStruct((width, width), F32)
    return pl.pallas_call(
        products_kernel,
        in_specs=[in_vmem() for unused in range(3)],
        out_specs=[in_vmem() for unused in range(3)],
        out_shape=(square, square, square),
        scratch_shapes=[pltpu.VMEM((width, width), F32)],
        name="products",
        compiler_params=pltpu.CompilerParams(vmem_limit_bytes=VMEM_BYTES),
    )(held, wk, wq)


def plane_order(step):
    order = []
    for index in range(32):
        wide, narrow = index // 4, index % 4
        wide, narrow = wide ^ (step // 2), narrow ^ (2 * (step % 2))
        order.append((index, wide * 4 + narrow))
    return order

def per_device(
    joined,
    block_input, segments, real_mask, qkv_weight, attn_out_weight, ffn_in_weight, ffn_bias, ffn_out_weight,
    first_gain, first_shift, second_gain, second_shift, adapter_down, adapter_up,
    joining_query, joining_key, joining_value, cotangent,
):
    row_count, seq_len, width = block_input.shape
    tokens = block_input.reshape(seq_len, width)
    units = adapter_down.shape[2]
    bank = jnp.stack(
        [
            jnp.transpose(adapter_down, (1, 2, 0)).reshape(ADAPTERS * units, width),
            adapter_up.reshape(ADAPTERS * units, width),
        ]
    )
    if not joined:
        bank = lax.all_gather(bank, "narrow", axis=1, tiled=True)
    seg_row = segments.reshape(1, seq_len)
    bounds = key_bounds(segments.reshape(seq_len))
    packed, context, log_total = attend(tokens, qkv_weight, seg_row, bounds)
    row = lambda vector: vector.reshape(1, vector.shape[0])
    out, grad_row, grad_context, value_sum, joint_sum, sums = middle(
        joined, units,
        tokens, cotangent.reshape(seq_len, width), context, attn_out_weight, ffn_in_weight, ffn_out_weight,
        bank, joining_query, joining_key, joining_value, row(ffn_bias), row(first_gain), row(first_shift),
        row(second_gain), row(second_shift), real_mask.reshape(1, seq_len),
    )
    grad_packed = attend_back(packed, context, log_total, grad_context, seg_row, bounds)
    if joined:
        held = [value_sum] + [
            lax.ppermute(value_sum, ("wide", "narrow"), plane_order(step)) for step in range(1, PLANE)
        ]
        input_grad, held, sums = close(grad_row, grad_packed, qkv_weight, held, sums)
        value_grad, query_grad, key_grad = products(held, joining_key, joining_query)
    else:
        input_grad = (grad_row + dot_on(grad_packed, qkv_weight, 0, 1)).astype(BF)
        value_grad, joint_sum, sums = lax.psum((value_sum, joint_sum, sums), ("wide", "narrow"))
        query_grad = dot_on(joint_sum.astype(BF), joining_key, 1, 0)
        key_grad = dot_on(joint_sum.astype(BF), joining_query, 0, 0)
    return (
        out.reshape(row_count, seq_len, width),
        input_grad.reshape(row_count, seq_len, width),
        query_grad,
        key_grad,
        value_grad,
        sums[:4].reshape(4 * width),
        sums[6],
        sums[7],
        sums[4],
        sums[5],
        sums[8, 0] / sums[9, 0],
    )


def solution(mesh):
    placed = (
        P(("wide", "narrow"), None, None),
        P(("wide", "narrow"), None),
        P(("wide", "narrow"), None),
        P(),
        P(),
        P(),
        P(),
        P(),
        P(),
        P(),
        P(),
        P(),
        P(None, None, "narrow"),
        P(None, "narrow", None),
        P(),
        P(),
        P(),
        P(("wide", "narrow"), None, None),
    )
    joined = mesh.shape["wide"] == 8 and mesh.shape["narrow"] == 4
    return jax.shard_map(
        functools.partial(per_device, joined),
        mesh=mesh,
        in_specs=placed,
        out_specs=(
            P(("wide", "narrow"), None, None),
            P(("wide", "narrow"), None, None),
            P(),
            P(),
            P(),
            P(),
            P(),
            P(),
            P(),
            P(),
            P(),
        ),
        check_vma=False,
    )
```

```python
import math

import jax
import jax.numpy as jnp
import functools

from jax import lax
from jax.experimental import pallas as pl
from jax.experimental.pallas import tpu as pltpu
from jax.sharding import PartitionSpec as P

D = 768
HEADS = 12
HEAD_DIM = 64
ADAPTERS = 16
BOTTLE = 48

AUG = 16
BF = jnp.bfloat16
F32 = jnp.float32
BLOCK_Q = 256
BLOCK_K = 128
VMEM_BYTES = 64 << 20


def dot_on(left_op, right_op, left_dim, right_dim):
    return lax.dot_general(
        left_op,
        right_op,
        (((left_dim,), (right_dim,)), ((), ())),
        preferred_element_type=F32,
    )


def head_rows(part, head):
    return pl.ds(pl.multiple_of(part * D + head * HEAD_DIM, HEAD_DIM), HEAD_DIM)


def key_range(seg, i):
    seq = seg.shape[1]
    low, high = jnp.int32(0), jnp.int32(seq)
    for doc in range(1, 4):
        start = jnp.sum((seg[...] < doc).astype(jnp.int32))
        low = jnp.where(start <= i * BLOCK_Q, jnp.maximum(low, start), low)
        high = jnp.where(start >= (i + 1) * BLOCK_Q, jnp.minimum(high, start), high)
    return low // BLOCK_K, (high + BLOCK_K - 1) // BLOCK_K


def attend_kernel(
    x, w_h, seg, packed_h, ctx_h, lse, w, packed, ctx, xt, qa, kt, m_s, l_s, o_s, w_sem, packed_sem, ctx_sem
):
    seq, width = x.shape

    def w_copy(part):
        columns = pl.ds(pl.multiple_of(part * width, width), width)
        return pltpu.make_async_copy(w_h.at[:, columns], w.at[:, columns], w_sem.at[part])

    def packed_copy(part):
        rows = pl.ds(pl.multiple_of(part * width, width), width)
        return pltpu.make_async_copy(packed.at[rows, :], packed_h.at[rows, :], packed_sem.at[part])

    def ctx_copy(i):
        columns = pl.ds(pl.multiple_of(i * BLOCK_Q, BLOCK_Q), BLOCK_Q)
        return pltpu.make_async_copy(ctx.at[:, columns], ctx_h.at[:, columns], ctx_sem.at[i])

    for part in range(3):
        w_copy(part).start()
    xt[...] = x[...].T

    def project(part, unused):
        w_copy(part).wait()
        rows = pl.ds(pl.multiple_of(part * width, width), width)
        packed[rows, :] = dot_on(w[:, rows], xt[...], 0, 0).astype(BF)
        packed_copy(part).start()
        return 0

    lax.fori_loop(0, 3, project, 0)
    row = lax.broadcasted_iota(jnp.int32, (AUG, seq), 0)
    same = row == seg[...]
    aug_q = jnp.where(same, 1.0, 0.0).astype(BF)
    aug_k = jnp.where((row < 4) & (~same), -1e30, 0.0).astype(BF)

    def prepare(head, unused):
        qa[head, :HEAD_DIM, :] = packed[head_rows(0, head), :] * jnp.asarray(0.125, BF)
        qa[head, HEAD_DIM:, :] = aug_q
        kt[head] = jnp.concatenate([packed[head_rows(1, head), :], aug_k], axis=0).T
        return 0

    lax.fori_loop(0, HEADS, prepare, 0)

    def query_block(i, unused):
        qs = pl.ds(pl.multiple_of(i * BLOCK_Q, BLOCK_Q), BLOCK_Q)
        for h in range(HEADS):
            m_s[h] = jnp.full((8, BLOCK_Q), -1e30, F32)
            l_s[h] = jnp.zeros((8, BLOCK_Q), F32)
            o_s[h] = jnp.zeros((HEAD_DIM, BLOCK_Q), F32)

        def key_block(j, unused):
            ks = pl.ds(pl.multiple_of(j * BLOCK_K, BLOCK_K), BLOCK_K)
            logits = [dot_on(kt[h, ks, :], qa[h, :, qs], 1, 0) for h in range(HEADS)]
            probs = []
            for h in range(HEADS):
                tile = logits[h].reshape(BLOCK_K // 8, 8, BLOCK_Q)
                top = jnp.max(jnp.max(tile, axis=0), axis=0, keepdims=True)
                old = m_s[h]
                new = jnp.maximum(old, jnp.broadcast_to(top, (8, BLOCK_Q)))
                decay = jnp.exp(old - new)
                prob = jnp.exp(tile - new[None])
                l_s[h] = l_s[h] * decay + jnp.sum(prob, axis=0)
                m_s[h] = new
                probs.append((prob.reshape(BLOCK_K, BLOCK_Q).astype(BF), decay))
            for h in range(HEADS):
                prob, decay = probs[h]
                part = dot_on(packed[2 * D + h * HEAD_DIM : 2 * D + (h + 1) * HEAD_DIM, ks], prob, 1, 0)
                kept = o_s[h].reshape(8, 8, BLOCK_Q) * decay[None]
                o_s[h] = kept.reshape(HEAD_DIM, BLOCK_Q) + part
            return 0

        lax.fori_loop(*key_range(seg, i), key_block, 0)
        for h in range(HEADS):
            total = jnp.sum(l_s[h], axis=0, keepdims=True)
            ctx[h * HEAD_DIM : (h + 1) * HEAD_DIM, qs] = (o_s[h] * (1.0 / total)).astype(BF)
            lse[h, :, qs] = m_s[h][:1] + jnp.log(total)
        ctx_copy(i).start()
        return 0

    lax.fori_loop(0, seq // BLOCK_Q, query_block, 0)
    for part in range(3):
        packed_copy(part).wait()
    for i in range(seq // BLOCK_Q):
        ctx_copy(i).wait()


GROUP = 4


def attend_back_kernel(
    packed_h, ctx_h, lse, gctx_h, seg, out_from, w_h, grad_row_h, input_grad_h, out_to,
    packed, ctx, gctx, gp, w, grad_row, bounce, input_grad, qa, kt, da, vt, dq_s, dk_s, dv_s, in_sem, out_sem,
):
    width, seq = ctx.shape
    groups = HEADS // GROUP
    group_rows = GROUP * HEAD_DIM
    loads = []
    for group in range(groups):
        pairs = [(gctx_h, gctx, 0), (ctx_h, ctx, 0)] + [(packed_h, packed, part) for part in range(3)]
        held = []
        for number, (source, target, part) in enumerate(pairs):
            rows = pl.ds(part * width + group * group_rows, group_rows)
            held.append(pltpu.make_async_copy(source.at[rows, :], target.at[rows, :], in_sem.at[group, number]))
            held[-1].start()
        loads.append(held)
    late = [
        pltpu.make_async_copy(source, target, out_sem.at[number])
        for number, (source, target) in enumerate(((out_from, bounce), (w_h, w), (grad_row_h, grad_row)))
    ]
    back = pltpu.make_async_copy(bounce, out_to, out_sem.at[3])

    row = lax.broadcasted_iota(jnp.int32, (AUG, seq), 0)
    same = row == seg[...]
    aug_q = jnp.where(same, 1.0, 0.0)
    aug_k = jnp.where(row < 4, jnp.where(same, 0.0, -1e30), jnp.where(row < 7, 1.0, 0.0)).astype(BF)
    aug_v = jnp.where(row < 3, 1.0, 0.0).astype(BF)

    def minus_rows(value, base):
        rest = -value
        rows = jnp.zeros((AUG, seq), F32)
        for step in range(3):
            piece = rest.astype(BF).astype(F32)
            rows = jnp.where(row == base + step, jnp.broadcast_to(piece, (AUG, seq)), rows)
            rest = rest - piece
        return rows

    def prepare(head, unused):
        rows = head_rows(0, head)
        qa[head, :HEAD_DIM, :] = packed[rows, :] * jnp.asarray(0.125, BF)
        qa[head, HEAD_DIM:, :] = (aug_q + minus_rows(lse[head], 4)).astype(BF)
        kt[head] = jnp.concatenate([packed[head_rows(1, head), :], aug_k], axis=0).T
        vt[head] = jnp.concatenate([packed[head_rows(2, head), :], aug_v], axis=0).T
        grad = gctx[rows, :]
        inner = jnp.sum(grad.astype(F32) * ctx[rows, :].astype(F32), axis=0, keepdims=True)
        da[head, :HEAD_DIM, :] = grad
        da[head, HEAD_DIM:, :] = minus_rows(inner, 0).astype(BF)
        dk_s[head] = jnp.zeros((HEAD_DIM, seq), F32)
        dv_s[head] = jnp.zeros((HEAD_DIM, seq), F32)
        return 0

    for group in range(groups):
        for load in loads[group]:
            load.wait()
        lax.fori_loop(group * GROUP, (group + 1) * GROUP, prepare, 0)
    for load in late:
        load.start()

    def query_block(i, unused):
        qs = pl.ds(pl.multiple_of(i * BLOCK_Q, BLOCK_Q), BLOCK_Q)
        for h in range(HEADS):
            dq_s[h] = jnp.zeros((HEAD_DIM, BLOCK_Q), F32)

        def key_block(j, unused):
            ks = pl.ds(pl.multiple_of(j * BLOCK_K, BLOCK_K), BLOCK_K)
            first, second = {}, {}
            lag = 4
            for t in range(HEADS + 2 * lag):
                if t < HEADS:
                    first[t] = (
                        dot_on(kt[t, ks, :], qa[t, :, qs], 1, 0),
                        dot_on(vt[t, ks, :], da[t, :, qs], 1, 0),
                    )
                h = t - lag
                if 0 <= h < HEADS:
                    logits, grad = first.pop(h)
                    prob = jnp.exp(logits)
                    second[h] = (prob.astype(BF), (prob * grad).astype(BF))
                h = t - 2 * lag
                if 0 <= h < HEADS:
                    prob, grad = second.pop(h)
                    dv_s[h, :, ks] += dot_on(da[h, :HEAD_DIM, qs], prob, 1, 1)
                    dk_s[h, :, ks] += dot_on(qa[h, :HEAD_DIM, qs], grad, 1, 1)
                    dq_s[h] += dot_on(packed[D + h * HEAD_DIM : D + (h + 1) * HEAD_DIM, ks], grad, 1, 0)
            return 0

        lax.fori_loop(*key_range(seg, i), key_block, 0)
        for h in range(HEADS):
            gp[h * HEAD_DIM : (h + 1) * HEAD_DIM, qs] = (dq_s[h] * 0.125).astype(BF)
        return 0

    lax.fori_loop(0, seq // BLOCK_Q, query_block, 0)

    def finish(head, unused):
        gp[head_rows(1, head), :] = dk_s[head].astype(BF)
        gp[head_rows(2, head), :] = dv_s[head].astype(BF)
        return 0

    late[0].wait()
    back.start()
    lax.fori_loop(0, HEADS, finish, 0)
    late[1].wait()
    late[2].wait()
    outs = []

    def leave(step, part):
        rows = pl.ds(step * BLOCK_Q, BLOCK_Q)
        input_grad[rows, :] = (grad_row[rows, :] + part).astype(BF)
        outs.append(
            pltpu.make_async_copy(input_grad.at[rows, :], input_grad_h.at[rows, :], out_sem.at[4 + step])
        )
        outs[-1].start()

    staged(
        seq // BLOCK_Q,
        lambda step: dot_on(gp[:, pl.ds(step * BLOCK_Q, BLOCK_Q)], w[...], 0, 1),
        leave,
    )
    back.wait()
    for out in outs:
        out.wait()


def in_vmem():
    return pl.BlockSpec(memory_space=pltpu.VMEM)


def anywhere():
    return pl.BlockSpec(memory_space=pl.ANY)


def attend(x, w, seg):
    seq = x.shape[0]
    return pl.pallas_call(
        attend_kernel,
        in_specs=[in_vmem(), anywhere(), in_vmem()],
        out_specs=[anywhere(), anywhere(), in_vmem()],
        out_shape=(
            jax.ShapeDtypeStruct((3 * D, seq), BF),
            jax.ShapeDtypeStruct((D, seq), BF),
            jax.ShapeDtypeStruct((HEADS, 1, seq), F32),
        ),
        scratch_shapes=[
            pltpu.VMEM((D, 3 * D), BF),
            pltpu.VMEM((3 * D, seq), BF),
            pltpu.VMEM((D, seq), BF),
            pltpu.VMEM((D, seq), BF),
            pltpu.VMEM((HEADS, HEAD_DIM + AUG, seq), BF),
            pltpu.VMEM((HEADS, seq, HEAD_DIM + AUG), BF),
            pltpu.VMEM((HEADS, 8, BLOCK_Q), F32),
            pltpu.VMEM((HEADS, 8, BLOCK_Q), F32),
            pltpu.VMEM((HEADS, HEAD_DIM, BLOCK_Q), F32),
            pltpu.SemaphoreType.DMA((3,)),
            pltpu.SemaphoreType.DMA((3,)),
            pltpu.SemaphoreType.DMA((seq // BLOCK_Q,)),
        ],
        name="attend",
        compiler_params=pltpu.CompilerParams(vmem_limit_bytes=60 << 20),
    )(x, w, seg)


def attend_back(packed, ctx, lse, gctx, seg, out, w, grad_row):
    seq = packed.shape[1]
    aug = HEAD_DIM + AUG
    return pl.pallas_call(
        attend_back_kernel,
        in_specs=[anywhere(), anywhere(), in_vmem(), anywhere(), in_vmem(), anywhere(), anywhere(), anywhere()],
        out_specs=[anywhere(), anywhere()],
        out_shape=(jax.ShapeDtypeStruct((seq, D), BF), jax.ShapeDtypeStruct((seq, D), BF)),
        scratch_shapes=[
            pltpu.VMEM((3 * D, seq), BF),
            pltpu.VMEM((D, seq), BF),
            pltpu.VMEM((D, seq), BF),
            pltpu.VMEM((3 * D, seq), BF),
            pltpu.VMEM((D, 3 * D), BF),
            pltpu.VMEM((seq, D), F32),
            pltpu.VMEM((seq, D), BF),
            pltpu.VMEM((seq, D), BF),
            pltpu.VMEM((HEADS, aug, seq), BF),
            pltpu.VMEM((HEADS, seq, aug), BF),
            pltpu.VMEM((HEADS, aug, seq), BF),
            pltpu.VMEM((HEADS, seq, aug), BF),
            pltpu.VMEM((HEADS, HEAD_DIM, BLOCK_Q), F32),
            pltpu.VMEM((HEADS, HEAD_DIM, seq), F32),
            pltpu.VMEM((HEADS, HEAD_DIM, seq), F32),
            pltpu.SemaphoreType.DMA((HEADS // GROUP, 5)),
            pltpu.SemaphoreType.DMA((4 + seq // BLOCK_Q,)),
        ],
        name="attend_back",
        cost_estimate=pl.CostEstimate(flops=30_000_000_000, bytes_accessed=20_000_000, transcendentals=0),
        compiler_params=pltpu.CompilerParams(vmem_limit_bytes=62 << 20),
    )(packed, ctx, lse, gctx, seg, out, w, grad_row)


def pieces(value):
    high = value.astype(BF)
    return high, (value - high.astype(F32)).astype(BF)


def normalize(values):
    centre = values - jnp.mean(values, axis=-1, keepdims=True)
    factor = lax.rsqrt(jnp.mean(centre * centre, axis=-1, keepdims=True) + 1e-06)
    return centre * factor, factor


def norm_back(scaled, unit_vals, factor):
    return factor * (
        scaled
        - jnp.mean(scaled, axis=-1, keepdims=True)
        - unit_vals * jnp.mean(scaled * unit_vals, axis=-1, keepdims=True)
    )


def gelu_parts(values):
    rising = 0.5 * (1.0 + lax.erf(values * (1.0 / math.sqrt(2.0))))
    bell = jnp.exp(-0.5 * values * values) * (1.0 / math.sqrt(2.0 * math.pi))
    return values * rising, rising + values * bell


def fold_rows(values):
    rows, columns = values.shape
    return jnp.sum(values.reshape(rows // 8, 8, columns), axis=0)


def staged(count, product, finish):
    held = {}
    for step in range(count + 1):
        if step < count:
            held[step] = product(step)
        if step >= 1:
            finish(step - 1, held.pop(step - 1))


MESH = pl.DeviceIdType.MESH
PLANE = 4
DEPTH = 4
OWN_ROWS = 24
PLANE_ROWS = 96
CORE_ROWS = 384


def place():
    wide, narrow = lax.axis_index("wide"), lax.axis_index("narrow")
    return wide // 2, lax.rem(wide, 2), narrow // 2, lax.rem(narrow, 2)


def device(z, x, y, core):
    return (z * 2 + x, y * 2 + core)


def plane_mate(step):
    z, x, y, core = place()
    return device(z, jnp.bitwise_xor(x, step // 2), jnp.bitwise_xor(y, step % 2), core)


def depth_mate(step):
    z, x, y, core = place()
    return device(lax.rem(z + step, DEPTH), x, y, core)


def core_mate():
    z, x, y, core = place()
    return device(z, x, y, 1 - core)


def remote(source, target, sems, slot, mate):
    return pltpu.make_async_remote_copy(
        src_ref=source,
        dst_ref=target,
        send_sem=sems.at[0, slot],
        recv_sem=sems.at[1, slot],
        device_id=mate,
        device_id_type=MESH,
    )


def greet(mates):
    barrier = pltpu.get_barrier_semaphore()
    for mate in mates:
        pl.semaphore_signal(barrier, inc=1, device_id=mate, device_id_type=MESH)
    return lambda: pl.semaphore_wait(barrier, len(mates))


class Scatter:
    def __init__(self, which, square, kept, send, near, plane, small_send, small, gathered, sems):
        self.which, self.square, self.kept = which, square, kept
        self.send, self.near, self.plane = send, near, plane
        self.small_send, self.small, self.gathered, self.sems = small_send, small, gathered, sems
        z, x, y, core = place()
        self.z, self.spot, self.core = z, x * 2 + y, core
        self.copies = []

    def rows(self, start, count):
        return pl.ds(pl.multiple_of(start, 8), count)

    def finish(self):
        for copy in self.copies:
            copy.wait()
        self.copies = []

    def go(self, source, target, slot, mate):
        copy = remote(source, target, self.sems, self.which * 12 + slot, mate)
        copy.start()
        self.copies.append(copy)

    def to_core(self):
        self.go(self.send.at[self.which], self.near.at[self.which], 0, core_mate())

    def to_plane(self):
        self.finish()
        for q in range(PLANE):
            rows = pl.ds(q * PLANE_ROWS, PLANE_ROWS)
            total = self.square[rows, :] + self.near[self.which, q].astype(F32)
            self.square[rows, :] = total
            self.send[self.which, q] = total.astype(BF)
        self.kept[self.which] = self.square[self.rows(self.spot * PLANE_ROWS, PLANE_ROWS), :]
        for step in range(1, PLANE):
            spot = jnp.bitwise_xor(self.spot, step)
            self.go(self.send.at[self.which, spot], self.plane.at[self.which, step - 1], step, plane_mate(step))

    def to_depth(self):
        self.finish()
        total = self.kept[self.which]
        for step in range(1, PLANE):
            total = total + self.plane[self.which, step - 1].astype(F32)
        self.kept[self.which] = total
        for k in range(DEPTH):
            self.small_send[self.which, k] = total[k * OWN_ROWS : (k + 1) * OWN_ROWS, :].astype(BF)
        for step in range(1, DEPTH):
            spot = lax.rem(self.z + step, DEPTH)
            self.go(
                self.small_send.at[self.which, spot],
                self.small.at[self.which, step - 1],
                PLANE - 1 + step,
                depth_mate(step),
            )

    def share(self):
        self.finish()
        total = self.kept[self.which, self.rows(self.z * OWN_ROWS, OWN_ROWS), :]
        for step in range(1, DEPTH):
            total = total + self.small[self.which, step - 1].astype(F32)
        self.gathered[self.core, self.which, self.z] = total.astype(BF)
        mine = self.gathered.at[self.core, self.which, self.z]
        for step in range(1, DEPTH):
            self.go(mine, mine, PLANE + DEPTH - 2 + step, depth_mate(step))

    def pair(self):
        self.finish()
        mine = self.gathered.at[self.core, self.which]
        self.go(mine, mine, PLANE + 2 * DEPTH - 2, core_mate())


ROWS_AT_ONCE = 256
HIDDEN_AT_ONCE = 512


def middle_kernel(
    shard_units, joined, x_h, g_h, ctx_h, wo_h, win_h, wout_h, bank_h, wq_h, wk_h, wv_h,
    bias_h, gain_one_h, shift_one_h, gain_two_h, shift_two_h, mask,
    out_h, gr_h, gctx_h, v_h, gg_h, sums_out,
    x, g, ctx, wo, win, wout, bank, wq, wk, wv,
    unit_one, unit_two, bottle, guide, total, act, slope, low, factor, mix,
    v_s, gg_s, sums, sums_part, vectors, in_sem, vector_sem, out_sem, *links,
):
    seq, width = x.shape
    blocks = seq // ROWS_AT_ONCE
    mix_scale = 1.0 / math.sqrt(D)
    loads = {}
    names = ("ctx", "wo", "x", "win", "wout", "wq", "wk", "bank", "g", "wv")
    sources = (ctx_h, wo_h, x_h, win_h, wout_h, wq_h, wk_h, bank_h, g_h, wv_h)
    targets = (ctx, wo, x, win, wout, wq, wk, bank, g, wv)
    vector_loads = [
        pltpu.make_async_copy(source, vectors.at[number, pl.ds(0, width)], vector_sem.at[number])
        for number, source in enumerate((gain_one_h, shift_one_h, gain_two_h, shift_two_h))
    ] + [
        pltpu.make_async_copy(
            bias_h.at[pl.ds(number * 1024, 1024)], vectors.at[4 + number], vector_sem.at[4 + number]
        )
        for number in range(win.shape[1] // 1024)
    ]
    for load in vector_loads:
        load.start()
    gain_one, shift_one, gain_two, shift_two = (vectors.at[number : number + 1, :width] for number in range(4))
    if joined:
        (
            kept, send, near, plane, small_send, small, gathered,
            sums_near, sums_plane, sums_depth, sums_mid, link_sems, bank_sems, sums_sems,
        ) = links
        arrived = greet(
            [core_mate()]
            + [plane_mate(step) for step in range(1, PLANE)]
            + [depth_mate(step) for step in range(1, DEPTH)]
        )
        spot = lax.axis_index("narrow")
        shard = bank_h.shape[1]

        def bank_rows(index):
            return bank.at[:, pl.ds(pl.multiple_of(index * shard, 16), shard), :]

        targets = targets[:7] + (bank_rows(spot),) + targets[8:]
    for number, name in enumerate(names):
        loads[name] = pltpu.make_async_copy(sources[number], targets[number], in_sem.at[number])
    for name in (("bank",) + names[:7] + names[8:]) if joined else names:
        loads[name].start()

    def rows_of(step):
        return pl.ds(step * ROWS_AT_ONCE, ROWS_AT_ONCE)

    t_one, t_two, t_three, t_four = (pl.ds(k * width, width) for k in range(4))
    down, up = 0, 1
    column = lax.broadcasted_iota(jnp.int32, (ADAPTERS, width), 1)
    owner = lax.rem(column, ADAPTERS * shard_units) // shard_units
    chosen = jnp.where(
        owner == lax.broadcasted_iota(jnp.int32, (ADAPTERS, width), 0), 1.0, 0.0
    ).astype(BF)

    def per_adapter(values):
        high, rest = pieces(values)
        return dot_on(chosen, high, 1, 1) + dot_on(chosen, rest, 1, 1)

    def per_unit(values):
        high, rest = pieces(values)
        return dot_on(high, chosen, 0, 0) + dot_on(rest, chosen, 0, 0)

    loads["ctx"].wait()
    loads["wo"].wait()
    loads["x"].wait()
    for load in vector_loads:
        load.wait()

    def finish_first(step, part):
        rows = rows_of(step)
        unit, scale = normalize(x[rows, :].astype(F32) + part)
        unit_one[rows, :] = unit
        factor[rows, 0:1] = scale
        low[rows, :] = (unit * gain_one[...] + shift_one[...]).astype(BF)

    if joined:
        arrived()
        loads["bank"].wait()
        bank_copies = [
            remote(bank_rows(spot), bank_rows(spot), bank_sems, 0, core_mate()),
            remote(bank_rows(spot), bank_rows(spot), bank_sems, 1, plane_mate(1)),
        ]
        for copy in bank_copies:
            copy.start()
    staged(blocks, lambda step: dot_on(ctx[:, rows_of(step)], wo[...], 0, 0), finish_first)

    loads["win"].wait()

    def hidden(chunk, unused):
        columns = pl.ds(pl.multiple_of(chunk * HIDDEN_AT_ONCE, HIDDEN_AT_ONCE), HIDDEN_AT_ONCE)
        per_row = 1024 // HIDDEN_AT_ONCE
        lanes = pl.ds(pl.multiple_of(lax.rem(chunk, per_row) * HIDDEN_AT_ONCE, HIDDEN_AT_ONCE), HIDDEN_AT_ONCE)
        bias = vectors[pl.ds(4 + chunk // per_row, 1), lanes]

        def finish(step, part):
            rows = rows_of(step)
            value, rising = gelu_parts(part + bias)
            act[rows, columns] = value.astype(BF)
            slope[rows, columns] = rising.astype(BF)

        staged(blocks, lambda step: dot_on(low[rows_of(step), :], win[:, columns], 1, 0), finish)
        return 0

    lax.fori_loop(0, win.shape[1] // HIDDEN_AT_ONCE, hidden, 0)
    loads["wout"].wait()

    def second(half, unused):
        def rows_in(step):
            start = half * (seq // 2) + step * ROWS_AT_ONCE
            return pl.ds(pl.multiple_of(start, ROWS_AT_ONCE), ROWS_AT_ONCE)

        def finish(step, part):
            rows = rows_in(step)
            unit, scale = normalize(unit_one[rows, :] * gain_one[...] + shift_one[...] + part)
            unit_two[rows, :] = unit
            factor[rows, 1:2] = scale
            low[rows, :] = (unit * gain_two[...] + shift_two[...]).astype(BF)

        staged(blocks // 2, lambda step: dot_on(act[rows_in(step), :], wout[...], 1, 0), finish)
        return 0

    lax.fori_loop(0, 2, second, 0)

    def h_two(rows):
        return unit_two[rows, :] * gain_two[...] + shift_two[...]

    if joined:
        bank_copies[1].wait()
        other = jnp.bitwise_xor(spot, 2)
        bank_copies[1] = remote(bank_rows(other), bank_rows(other), bank_sems, 2, core_mate())
        bank_copies[1].start()
    loads["wq"].wait()

    def keep(place):
        def finish(step, part):
            act[rows_of(step), place] = part.astype(BF)

        return finish

    staged(blocks, lambda step: dot_on(low[rows_of(step), :], wq[...], 1, 0), keep(t_one))
    loads["wk"].wait()
    staged(blocks, lambda step: dot_on(act[rows_of(step), t_one], wk[...], 1, 1), keep(t_two))
    if joined:
        for copy in bank_copies:
            copy.wait()
    else:
        loads["bank"].wait()

    def finish_down(step, part):
        rows = rows_of(step)
        value, rising = gelu_parts(part)
        bottle[rows, :] = value
        act[rows, t_four] = rising.astype(BF)

    staged(blocks, lambda step: dot_on(low[rows_of(step), :], bank[down], 1, 1), finish_down)

    def finish_guide(step, part):
        rows = rows_of(step)
        guide[rows, :] = part
        value = bottle[rows, :]
        scores = per_adapter(value * part) * mix_scale
        shifted = scores - jnp.max(scores, axis=0, keepdims=True)
        log_weights = shifted - jnp.log(jnp.sum(jnp.exp(shifted), axis=0, keepdims=True))
        weights = jnp.exp(log_weights)
        mix[:, rows] = weights
        sums[step : step + 1, :ROWS_AT_ONCE] = -jnp.sum(weights * log_weights, axis=0, keepdims=True)
        act[rows, t_one] = (per_unit(weights) * value).astype(BF)

    staged(blocks, lambda step: dot_on(act[rows_of(step), t_two], bank[up], 1, 1), finish_guide)
    real = mask[...].astype(F32)
    ent = jnp.zeros((1, 1), F32)
    for step in range(blocks):
        part = sums[step : step + 1, :ROWS_AT_ONCE] * real[:, step * ROWS_AT_ONCE : (step + 1) * ROWS_AT_ONCE]
        ent = ent + jnp.sum(part, axis=1, keepdims=True)
    lane = lax.broadcasted_iota(jnp.int32, (1, 1024), 1)
    sums_out[7:8, :] = jnp.where(lane < 128, ent, jnp.sum(real, axis=1, keepdims=True))
    sums_out[3:7, width:] = jnp.zeros((4, 1024 - width), F32)

    def finish_update(step, part):
        rows = rows_of(step)
        x[rows, :] = (h_two(rows) + part).astype(BF)

    staged(blocks, lambda step: dot_on(act[rows_of(step), t_one], bank[up], 1, 0), finish_update)

    loads["g"].wait()
    third = width // 3

    def over_tokens(left, right, target):
        def product(step):
            return dot_on(left(pl.ds(step * third, third)), right, 0, 0)

        def finish(step, part):
            target[pl.ds(step * third, third), :] = part

        staged(3, product, finish)

    def halves(left, base, right, target, which):
        core = place()[3]

        def product(step):
            start = base + (core if step else 1 - core) * CORE_ROWS
            return dot_on(left[:, pl.ds(pl.multiple_of(start, 128), CORE_ROWS)], right, 0, 0)

        def finish(step, part):
            if step:
                target[...] = part
            else:
                for q in range(PLANE):
                    send[which, q] = part[q * PLANE_ROWS : (q + 1) * PLANE_ROWS, :].astype(BF)

        staged(2, product, finish)

    if joined:
        halves(x, 0, g[...], v_s, 0)
    else:
        over_tokens(lambda cols: x[:, cols], g[...], v_s)
    if joined:
        value_sum, joint_sum = (
            Scatter(k, v_s, kept, send, near, plane, small_send, small, gathered, link_sems) for k in range(2)
        )
        value_sum.to_core()
    else:
        v_out = pltpu.make_async_copy(v_s, v_h, out_sem.at[0])
        v_out.start()

    loads["wv"].wait()

    def finish_blend(step, part):
        rows = rows_of(step)
        total[rows, :] = g[rows, :].astype(F32) + part
        act[rows, t_one] = part.astype(BF)

    staged(blocks, lambda step: dot_on(g[rows_of(step), :], wv[...], 1, 1), finish_blend)

    if joined:
        value_sum.to_plane()

    def finish_mixed(step, part):
        rows = rows_of(step)
        value = bottle[rows, :]
        weights = mix[:, rows]
        grad_weights = per_adapter(part * value)
        grad_scores = weights * (grad_weights - jnp.sum(grad_weights * weights, axis=0, keepdims=True))
        score_term = per_unit(grad_scores * mix_scale)
        act[rows, t_one] = (score_term * value).astype(BF)
        grad_bottle = part * per_unit(weights) + score_term * guide[rows, :]
        act[rows, t_three] = (grad_bottle * act[rows, t_four].astype(F32)).astype(BF)

    staged(blocks, lambda step: dot_on(act[rows_of(step), t_one], bank[up], 1, 1), finish_mixed)
    staged(blocks, lambda step: dot_on(act[rows_of(step), t_one], bank[up], 1, 0), keep(t_two))
    if joined:
        halves(low, 0, act[:, t_two], v_s, 1)
    else:
        over_tokens(lambda cols: low[:, cols], act[:, t_two], gg_s)
    if joined:
        joint_sum.to_core()
    else:
        gg_out = pltpu.make_async_copy(gg_s, gg_h, out_sem.at[2])
        gg_out.start()
    staged(blocks, lambda step: dot_on(act[rows_of(step), t_two], wk[...], 1, 0), keep(t_one))
    partial = [jnp.zeros((8, width), F32) for unused in range(4)]

    def finish_two(step, part):
        rows = rows_of(step)
        grad = total[rows, :] + part
        unit = unit_two[rows, :]
        partial[0] = partial[0] + fold_rows(grad * unit)
        partial[1] = partial[1] + fold_rows(grad)
        back = norm_back(grad * gain_two[...], unit, factor[rows, 1:2])
        total[rows, :] = back
        low[rows, :] = back.astype(BF)

    staged(
        blocks,
        lambda step: dot_on(act[rows_of(step), t_three], bank[down], 1, 0)
        + dot_on(act[rows_of(step), t_one], wq[...], 1, 1),
        finish_two,
    )

    if joined:
        joint_sum.to_plane()
        value_sum.to_depth()

    def hidden_back(chunk, unused):
        columns = pl.ds(pl.multiple_of(chunk * HIDDEN_AT_ONCE, HIDDEN_AT_ONCE), HIDDEN_AT_ONCE)
        held = [jnp.zeros((8, HIDDEN_AT_ONCE), F32)]

        def finish(step, part):
            rows = rows_of(step)
            grad = (part * slope[rows, columns].astype(F32)).astype(BF)
            act[rows, columns] = grad
            held[0] = held[0] + fold_rows(grad.astype(F32))

        staged(blocks, lambda step: dot_on(low[rows_of(step), :], wout[columns, :], 1, 1), finish)
        sums_part[chunk] = held[0]
        return 0

    lax.fori_loop(0, win.shape[1] // HIDDEN_AT_ONCE, hidden_back, 0)
    for number in range(win.shape[1] // HIDDEN_AT_ONCE):
        at, lanes = divmod(number * HIDDEN_AT_ONCE, 1024)
        sums_out[at : at + 1, pl.ds(lanes, HIDDEN_AT_ONCE)] = jnp.sum(sums_part[number], axis=0, keepdims=True)
    sums_out[5:6, :width] = jnp.sum(partial[0], axis=0, keepdims=True)
    sums_out[6:7, :width] = jnp.sum(partial[1], axis=0, keepdims=True)
    if joined:
        value_sum.share()
        joint_sum.to_depth()

    def first_back(half, carried):
        def rows_in(step):
            start = half * (seq // 2) + step * ROWS_AT_ONCE
            return pl.ds(pl.multiple_of(start, ROWS_AT_ONCE), ROWS_AT_ONCE)

        held = list(carried)

        def finish(step, part):
            rows = rows_in(step)
            grad = total[rows, :] + part
            unit = unit_one[rows, :]
            held[0] = held[0] + fold_rows(grad * unit)
            held[1] = held[1] + fold_rows(grad)
            back = norm_back(grad * gain_one[...], unit, factor[rows, 0:1])
            total[rows, :] = back
            low[rows, :] = back.astype(BF)

        staged(blocks // 2, lambda step: dot_on(act[rows_in(step), :], win[...], 1, 1), finish)
        return tuple(held)

    zero = jnp.zeros((8, width), F32)
    gain_sum, shift_sum = lax.fori_loop(0, 2, first_back, (zero, zero))
    sums_out[3:4, :width] = jnp.sum(gain_sum, axis=0, keepdims=True)
    sums_out[4:5, :width] = jnp.sum(shift_sum, axis=0, keepdims=True)
    if joined:
        near_copy = remote(sums_out, sums_near, sums_sems, 0, core_mate())
        near_copy.start()
        value_sum.pair()
        joint_sum.share()
    gr_copy = pltpu.make_async_copy(total, gr_h, out_sem.at[3])
    gr_copy.start()

    def finish_ctx(step, part):
        ctx[pl.ds(step * third, third), :] = part.astype(BF)

    staged(3, lambda step: dot_on(wo[pl.ds(step * third, third), :], low[...], 1, 1), finish_ctx)
    gctx_copy = pltpu.make_async_copy(ctx, gctx_h, out_sem.at[4])
    gctx_copy.start()
    if joined:
        near_copy.wait()
        sums_mid[0] = sums_out[...] + sums_near[...]
        plane_copies = [
            remote(sums_mid.at[0], sums_plane.at[step - 1], sums_sems, step, plane_mate(step))
            for step in range(1, PLANE)
        ]
        for copy in plane_copies:
            copy.start()
        value_sum.finish()

    def finish_out(step, part):
        rows = rows_of(step)
        x[rows, :] = (h_two(rows) + part).astype(BF)

    staged(blocks, lambda step: dot_on(x[rows_of(step), :], wv[...], 1, 0), finish_out)
    out_copy = pltpu.make_async_copy(x, out_h, out_sem.at[1])
    out_copy.start()
    if joined:
        for copy in plane_copies:
            copy.wait()
        sums_mid[1] = sums_mid[0] + sums_plane[0] + sums_plane[1] + sums_plane[2]
        depth_copies = [
            remote(sums_mid.at[1], sums_depth.at[step - 1], sums_sems, PLANE - 1 + step, depth_mate(step))
            for step in range(1, DEPTH)
        ]
        for copy in depth_copies:
            copy.start()
        joint_sum.pair()
        joint_sum.finish()
        v_out = pltpu.make_async_copy(gathered, v_h, out_sem.at[0])
        v_out.start()
        for copy in depth_copies:
            copy.wait()
        sums_out[...] = sums_mid[1] + sums_depth[0] + sums_depth[1] + sums_depth[2]
    else:
        gg_out.wait()
    v_out.wait()
    out_copy.wait()
    gr_copy.wait()
    gctx_copy.wait()


def middle(joined, units, x, g, ctx, wo, win, wout, bank, wq, wk, wv, bias, gain_one, shift_one, gain_two, shift_two, mask):
    seq, width = x.shape
    hidden = win.shape[1]
    token_low = pltpu.VMEM((seq, width), BF)
    token_wide = pltpu.VMEM((seq, width), F32)
    square = pltpu.VMEM((width, width), BF)
    sum_square = pltpu.VMEM((CORE_ROWS if joined else width, width), F32)
    links = [
        pltpu.VMEM((2, PLANE_ROWS, width), F32),
        pltpu.VMEM((2, PLANE, PLANE_ROWS, width), BF),
        pltpu.VMEM((2, PLANE, PLANE_ROWS, width), BF),
        pltpu.VMEM((2, PLANE - 1, PLANE_ROWS, width), BF),
        pltpu.VMEM((2, DEPTH, OWN_ROWS, width), BF),
        pltpu.VMEM((2, DEPTH - 1, OWN_ROWS, width), BF),
        pltpu.VMEM((2, 2, DEPTH, OWN_ROWS, width), BF),
        pltpu.VMEM((8, 1024), F32),
        pltpu.VMEM((PLANE - 1, 8, 1024), F32),
        pltpu.VMEM((DEPTH - 1, 8, 1024), F32),
        pltpu.VMEM((2, 8, 1024), F32),
        pltpu.SemaphoreType.DMA((2, 24)),
        pltpu.SemaphoreType.DMA((2, 3)),
        pltpu.SemaphoreType.DMA((2, PLANE + DEPTH - 1)),
    ]
    return pl.pallas_call(
        functools.partial(middle_kernel, units, joined),
        in_specs=[anywhere() for unused in range(15)] + [in_vmem()],
        out_specs=[anywhere() for unused in range(5)] + [in_vmem()],
        out_shape=(
            jax.ShapeDtypeStruct((seq, width), BF),
            jax.ShapeDtypeStruct((seq, width), F32),
            jax.ShapeDtypeStruct((width, seq), BF),
            jax.ShapeDtypeStruct((2, 2, DEPTH, OWN_ROWS, width), BF)
            if joined
            else jax.ShapeDtypeStruct((width, width), F32),
            jax.ShapeDtypeStruct((8, 128) if joined else (width, width), F32),
            jax.ShapeDtypeStruct((8, 1024), F32),
        ),
        scratch_shapes=[
            token_low, token_low, pltpu.VMEM((width, seq), BF),
            square, pltpu.VMEM((width, hidden), BF), pltpu.VMEM((hidden, width), BF),
            pltpu.VMEM((2, width, width), BF), square, square, square,
            token_wide, token_wide, token_wide, token_wide, token_wide,
            pltpu.VMEM((seq, hidden), BF), pltpu.VMEM((seq, hidden), BF), token_low,
            pltpu.VMEM((seq, 2), F32), pltpu.VMEM((ADAPTERS, seq), F32),
            sum_square, pltpu.VMEM((8, 128) if joined else (width, width), F32),
            pltpu.VMEM((8, ROWS_AT_ONCE), F32), pltpu.VMEM((hidden // HIDDEN_AT_ONCE, 8, HIDDEN_AT_ONCE), F32),
            pltpu.VMEM((8, 1024), F32),
            pltpu.SemaphoreType.DMA((10,)), pltpu.SemaphoreType.DMA((7,)), pltpu.SemaphoreType.DMA((5,)),
        ]
        + (links if joined else []),
        name="middle",
        compiler_params=pltpu.CompilerParams(
            vmem_limit_bytes=VMEM_BYTES, **(dict(collective_id=0, has_side_effects=True) if joined else {})
        ),
    )(x, g, ctx, wo, win, wout, bank, wq, wk, wv, bias, gain_one, shift_one, gain_two, shift_two, mask)

def products_kernel(
    mine_h, first_h, second_h, third_h, wk_h, wq_h, sums,
    value_h, query_h, key_h, bias_h, gain_one_h, shift_one_h, gain_two_h, shift_two_h, entropy,
    held, wk, wq, square, joint, low, in_sem, out_sem,
):
    width = wk.shape[0]
    z, x, y, core = place()
    loads = [
        pltpu.make_async_copy(source, target, in_sem.at[number])
        for number, (source, target) in enumerate(
            [(source, held.at[step]) for step, source in enumerate((mine_h, first_h, second_h, third_h))]
            + [(wk_h, wk), (wq_h, wq)]
        )
    ]
    for load in loads:
        load.start()
    outs = []

    def leave(source, target):
        outs.append(pltpu.make_async_copy(source, target, out_sem.at[len(outs)]))
        outs[-1].start()

    for number in range(bias_h.shape[0] // 1024):
        leave(sums.at[number], bias_h.at[pl.ds(number * 1024, 1024)])
    for number, target in enumerate((gain_one_h, shift_one_h, gain_two_h, shift_two_h)):
        leave(sums.at[3 + number, pl.ds(0, width)], target)
    entropy[...] = sums[7:8, 0:1] / sums[7:8, 128:129]
    for load in loads[:PLANE]:
        load.wait()

    def unpack(which, target):
        for step in range(PLANE):
            base = jnp.bitwise_xor(x * 2 + y, step) * PLANE_ROWS
            for side in range(2):
                for depth in range(DEPTH):
                    start = pl.multiple_of(base + side * CORE_ROWS + depth * OWN_ROWS, 8)
                    target[pl.ds(start, OWN_ROWS), :] = held[step, side, which, depth].astype(F32)

    unpack(1, joint)
    low[...] = joint[...].astype(BF)
    loads[PLANE].wait()
    square[1] = dot_on(low[...], wk[...], 1, 0)
    leave(square.at[1], query_h)
    unpack(0, square.at[0])
    leave(square.at[0], value_h)
    loads[PLANE + 1].wait()
    joint[...] = dot_on(low[...], wq[...], 0, 0)
    leave(joint, key_h)
    for out in outs:
        out.wait()


def products(held, wk, wq, sums, hidden):
    width = wk.shape[0]
    square = jax.ShapeDtypeStruct((width, width), F32)
    vector = jax.ShapeDtypeStruct((width,), F32)
    return pl.pallas_call(
        products_kernel,
        in_specs=[anywhere() for unused in range(6)] + [in_vmem()],
        out_specs=[anywhere() for unused in range(8)] + [in_vmem()],
        out_shape=(
            square, square, square, jax.ShapeDtypeStruct((hidden,), F32), vector, vector, vector, vector,
            jax.ShapeDtypeStruct((1, 1), F32),
        ),
        scratch_shapes=[
            pltpu.VMEM((PLANE,) + held[0].shape, BF),
            pltpu.VMEM((width, width), BF),
            pltpu.VMEM((width, width), BF),
            pltpu.VMEM((2, width, width), F32),
            pltpu.VMEM((width, width), F32),
            pltpu.VMEM((width, width), BF),
            pltpu.SemaphoreType.DMA((PLANE + 2,)),
            pltpu.SemaphoreType.DMA((10,)),
        ],
        name="products",
        compiler_params=pltpu.CompilerParams(vmem_limit_bytes=VMEM_BYTES),
    )(*held, wk, wq, sums)


def plane_order(step):
    order = []
    for index in range(32):
        wide, narrow = index // 4, index % 4
        wide, narrow = wide ^ (step // 2), narrow ^ (2 * (step % 2))
        order.append((index, wide * 4 + narrow))
    return order

def per_device(
    joined,
    block_input, segments, real_mask, qkv_weight, attn_out_weight, ffn_in_weight, ffn_bias, ffn_out_weight,
    first_gain, first_shift, second_gain, second_shift, adapter_down, adapter_up,
    joining_query, joining_key, joining_value, cotangent,
):
    row_count, seq_len, width = block_input.shape
    tokens = block_input.reshape(seq_len, width)
    units = adapter_down.shape[2]
    bank = jnp.stack(
        [
            jnp.transpose(adapter_down, (1, 2, 0)).reshape(ADAPTERS * units, width),
            adapter_up.reshape(ADAPTERS * units, width),
        ]
    )
    if not joined:
        bank = lax.all_gather(bank, "narrow", axis=1, tiled=True)
    seg_row = segments.reshape(1, seq_len)
    packed, context, log_total = attend(tokens, qkv_weight, seg_row)
    out, grad_row, grad_context, value_sum, joint_sum, sums = middle(
        joined, units,
        tokens, cotangent.reshape(seq_len, width), context, attn_out_weight, ffn_in_weight, ffn_out_weight,
        bank, joining_query, joining_key, joining_value, ffn_bias, first_gain, first_shift,
        second_gain, second_shift, real_mask.reshape(1, seq_len),
    )
    input_grad, out = attend_back(
        packed, context, log_total, grad_context, seg_row, out, qkv_weight, grad_row
    )
    if joined:
        held = [value_sum] + [
            lax.ppermute(value_sum, ("wide", "narrow"), plane_order(step)) for step in range(1, PLANE)
        ]
        value_grad, query_grad, key_grad, bias_grad, gain_one, shift_one, gain_two, shift_two, entropy = products(
            held, joining_key, joining_query, sums, ffn_bias.shape[0]
        )
    else:
        value_grad, joint_sum, sums = lax.psum((value_sum, joint_sum, sums), ("wide", "narrow"))
        query_grad = dot_on(joint_sum.astype(BF), joining_key, 1, 0)
        key_grad = dot_on(joint_sum.astype(BF), joining_query, 0, 0)
        bias_grad = sums[:3].reshape(ffn_bias.shape[0])
        gain_one, shift_one, gain_two, shift_two = (sums[number, :width] for number in range(3, 7))
        entropy = sums[7, 0] / sums[7, 128]
    return (
        out.reshape(row_count, seq_len, width),
        input_grad.reshape(row_count, seq_len, width),
        query_grad,
        key_grad,
        value_grad,
        bias_grad,
        gain_one,
        shift_one,
        gain_two,
        shift_two,
        entropy.reshape(()),
    )


def solution(mesh):
    placed = (
        P(("wide", "narrow"), None, None),
        P(("wide", "narrow"), None),
        P(("wide", "narrow"), None),
        P(),
        P(),
        P(),
        P(),
        P(),
        P(),
        P(),
        P(),
        P(),
        P(None, None, "narrow"),
        P(None, "narrow", None),
        P(),
        P(),
        P(),
        P(("wide", "narrow"), None, None),
    )
    joined = mesh.shape["wide"] == 8 and mesh.shape["narrow"] == 4
    return jax.shard_map(
        functools.partial(per_device, joined),
        mesh=mesh,
        in_specs=placed,
        out_specs=(
            P(("wide", "narrow"), None, None),
            P(("wide", "narrow"), None, None),
            P(),
            P(),
            P(),
            P(),
            P(),
            P(),
            P(),
            P(),
            P(),
        ),
        check_vma=False,
    )
```

```python
import math

import jax
import jax.numpy as jnp
import functools

from jax import lax
from jax.experimental import pallas as pl
from jax.experimental.pallas import tpu as pltpu
from jax.sharding import PartitionSpec as P

D = 768
HEADS = 12
HEAD_DIM = 64
ADAPTERS = 16
BOTTLE = 48

AUG = 16
BF = jnp.bfloat16
F32 = jnp.float32
BLOCK_Q = 256
BLOCK_K = 128
VMEM_BYTES = 64 << 20


def dot_on(left_op, right_op, left_dim, right_dim):
    return lax.dot_general(
        left_op,
        right_op,
        (((left_dim,), (right_dim,)), ((), ())),
        preferred_element_type=F32,
    )


def head_rows(part, head):
    return pl.ds(pl.multiple_of(part * D + head * HEAD_DIM, HEAD_DIM), HEAD_DIM)


def key_range(seg, i):
    seq = seg.shape[1]
    low, high = jnp.int32(0), jnp.int32(seq)
    for doc in range(1, 4):
        start = jnp.sum((seg[...] < doc).astype(jnp.int32))
        low = jnp.where(start <= i * BLOCK_Q, jnp.maximum(low, start), low)
        high = jnp.where(start >= (i + 1) * BLOCK_Q, jnp.minimum(high, start), high)
    return low // BLOCK_K, (high + BLOCK_K - 1) // BLOCK_K


def attend_kernel(
    x, w_h, seg, packed_h, ctx_h, lse, w, packed, ctx, xt, qa, kt, va, m_s, o_s, w_sem, packed_sem, ctx_sem
):
    seq, width = x.shape

    def w_copy(part):
        columns = pl.ds(pl.multiple_of(part * width, width), width)
        return pltpu.make_async_copy(w_h.at[:, columns], w.at[:, columns], w_sem.at[part])

    def packed_copy(part):
        rows = pl.ds(pl.multiple_of(part * width, width), width)
        return pltpu.make_async_copy(packed.at[rows, :], packed_h.at[rows, :], packed_sem.at[part])

    def ctx_copy(i):
        columns = pl.ds(pl.multiple_of(i * BLOCK_Q, BLOCK_Q), BLOCK_Q)
        return pltpu.make_async_copy(ctx.at[:, columns], ctx_h.at[:, columns], ctx_sem.at[i])

    for part in range(3):
        w_copy(part).start()
    xt[...] = x[...].T

    def project(part, unused):
        w_copy(part).wait()
        rows = pl.ds(pl.multiple_of(part * width, width), width)
        packed[rows, :] = dot_on(w[:, rows], xt[...], 0, 0).astype(BF)
        packed_copy(part).start()
        return 0

    lax.fori_loop(0, 3, project, 0)
    row = lax.broadcasted_iota(jnp.int32, (AUG, seq), 0)
    same = row == seg[...]
    aug_q = jnp.where(same, 1.0, 0.0).astype(BF)
    aug_k = jnp.where((row < 4) & (~same), -1e30, 0.0).astype(BF)

    def prepare(head, unused):
        qa[head, :HEAD_DIM, :] = packed[head_rows(0, head), :] * jnp.asarray(0.125, BF)
        qa[head, HEAD_DIM:, :] = aug_q
        kt[head] = jnp.concatenate([packed[head_rows(1, head), :], aug_k], axis=0).T
        va[head, :HEAD_DIM, :] = packed[head_rows(2, head), :]
        va[head, HEAD_DIM:, :] = jnp.ones((AUG, seq), BF)
        return 0

    lax.fori_loop(0, HEADS, prepare, 0)

    def query_block(i, unused):
        qs = pl.ds(pl.multiple_of(i * BLOCK_Q, BLOCK_Q), BLOCK_Q)
        for h in range(HEADS):
            m_s[h] = jnp.full((8, BLOCK_Q), -1e30, F32)
            o_s[h] = jnp.zeros((HEAD_DIM + AUG, BLOCK_Q), F32)

        def key_block(j, unused):
            ks = pl.ds(pl.multiple_of(j * BLOCK_K, BLOCK_K), BLOCK_K)
            first, second = {}, {}
            lag = 4
            for t in range(HEADS + 2 * lag):
                if t < HEADS:
                    first[t] = dot_on(kt[t, ks, :], qa[t, :, qs], 1, 0)
                h = t - lag
                if 0 <= h < HEADS:
                    tile = first.pop(h).reshape(BLOCK_K // 8, 8, BLOCK_Q)
                    top = jnp.max(jnp.max(tile, axis=0), axis=0, keepdims=True)
                    old = m_s[h]
                    new = jnp.maximum(old, jnp.broadcast_to(top, (8, BLOCK_Q)))
                    m_s[h] = new
                    prob = jnp.exp(tile - new[None]).reshape(BLOCK_K, BLOCK_Q).astype(BF)
                    second[h] = (prob, jnp.exp(old - new))
                h = t - 2 * lag
                if 0 <= h < HEADS:
                    prob, decay = second.pop(h)
                    rows = HEAD_DIM + AUG
                    kept = (o_s[h].reshape(rows // 8, 8, BLOCK_Q) * decay[None]).reshape(rows, BLOCK_Q)
                    o_s[h] = kept + dot_on(va[h, :, ks], prob, 1, 0)
            return 0

        lax.fori_loop(*key_range(seg, i), key_block, 0)
        for h in range(HEADS):
            total = o_s[h, HEAD_DIM : HEAD_DIM + 1, :]
            ctx[h * HEAD_DIM : (h + 1) * HEAD_DIM, qs] = (o_s[h, :HEAD_DIM, :] * (1.0 / total)).astype(BF)
            lse[h, :, qs] = m_s[h][:1] + jnp.log(total)
        ctx_copy(i).start()
        return 0

    lax.fori_loop(0, seq // BLOCK_Q, query_block, 0)
    for part in range(3):
        packed_copy(part).wait()
    for i in range(seq // BLOCK_Q):
        ctx_copy(i).wait()


GROUP = 4


def attend_back_kernel(
    packed_h, ctx_h, lse, gctx_h, seg, out_from, w_h, grad_row_h, input_grad_h, out_to,
    packed, ctx, gctx, gp, w, grad_row, bounce, input_grad, qs_s, qt, dt, ka, va, dq_s, dk_s, dv_s, in_sem, out_sem,
):
    width, seq = ctx.shape
    groups = HEADS // GROUP
    group_rows = GROUP * HEAD_DIM
    loads = []
    for group in range(groups):
        pairs = [(gctx_h, gctx, 0), (ctx_h, ctx, 0)] + [(packed_h, packed, part) for part in range(3)]
        held = []
        for number, (source, target, part) in enumerate(pairs):
            rows = pl.ds(part * width + group * group_rows, group_rows)
            held.append(pltpu.make_async_copy(source.at[rows, :], target.at[rows, :], in_sem.at[group, number]))
            held[-1].start()
        loads.append(held)
    late = [
        pltpu.make_async_copy(source, target, out_sem.at[number])
        for number, (source, target) in enumerate(((out_from, bounce), (w_h, w), (grad_row_h, grad_row)))
    ]
    back = pltpu.make_async_copy(bounce, out_to, out_sem.at[3])

    row = lax.broadcasted_iota(jnp.int32, (AUG, seq), 0)
    same = row == seg[...]
    aug_q = jnp.where(same, 1.0, 0.0)
    aug_k = jnp.where(row < 4, jnp.where(same, 0.0, -1e30), jnp.where(row < 7, 1.0, 0.0)).astype(BF)
    aug_v = jnp.where(row < 3, 1.0, 0.0).astype(BF)

    def minus_rows(value, base):
        rest = -value
        rows = jnp.zeros((AUG, seq), F32)
        for step in range(3):
            piece = rest.astype(BF).astype(F32)
            rows = jnp.where(row == base + step, jnp.broadcast_to(piece, (AUG, seq)), rows)
            rest = rest - piece
        return rows

    def prepare(head, unused):
        rows = head_rows(0, head)
        scaled = packed[rows, :] * jnp.asarray(0.125, BF)
        qs_s[head] = scaled
        qt[head] = jnp.concatenate([scaled, (aug_q + minus_rows(lse[head], 4)).astype(BF)], axis=0).T
        ka[head, :HEAD_DIM, :] = packed[head_rows(1, head), :]
        ka[head, HEAD_DIM:, :] = aug_k
        va[head, :HEAD_DIM, :] = packed[head_rows(2, head), :]
        va[head, HEAD_DIM:, :] = aug_v
        grad = gctx[rows, :]
        inner = jnp.sum(grad.astype(F32) * ctx[rows, :].astype(F32), axis=0, keepdims=True)
        dt[head] = jnp.concatenate([grad, minus_rows(inner, 0).astype(BF)], axis=0).T
        dq_s[head] = jnp.zeros((HEAD_DIM, seq), F32)
        return 0

    for group in range(groups):
        for load in loads[group]:
            load.wait()
        lax.fori_loop(group * GROUP, (group + 1) * GROUP, prepare, 0)
    for load in late:
        load.start()

    def outer(i, unused):
        ks = pl.ds(pl.multiple_of(i * BLOCK_Q, BLOCK_Q), BLOCK_Q)
        for h in range(HEADS):
            dk_s[h] = jnp.zeros((HEAD_DIM, BLOCK_Q), F32)
            dv_s[h] = jnp.zeros((HEAD_DIM, BLOCK_Q), F32)

        def inner_block(j, unused):
            qs = pl.ds(pl.multiple_of(j * BLOCK_K, BLOCK_K), BLOCK_K)
            first, second = {}, {}
            lag = 4
            for t in range(HEADS + 2 * lag):
                if t < HEADS:
                    first[t] = (
                        dot_on(qt[t, qs, :], ka[t, :, ks], 1, 0),
                        dot_on(dt[t, qs, :], va[t, :, ks], 1, 0),
                    )
                h = t - lag
                if 0 <= h < HEADS:
                    logits, grad = first.pop(h)
                    prob = jnp.exp(logits)
                    second[h] = (prob.astype(BF), (prob * grad).astype(BF))
                h = t - 2 * lag
                if 0 <= h < HEADS:
                    prob, grad = second.pop(h)
                    dv_s[h] += dot_on(gctx[h * HEAD_DIM : (h + 1) * HEAD_DIM, qs], prob, 1, 0)
                    dk_s[h] += dot_on(qs_s[h, :, qs], grad, 1, 0)
                    dq_s[h, :, qs] += dot_on(packed[D + h * HEAD_DIM : D + (h + 1) * HEAD_DIM, ks], grad, 1, 1)
            return 0

        lax.fori_loop(*key_range(seg, i), inner_block, 0)
        for h in range(HEADS):
            gp[D + h * HEAD_DIM : D + (h + 1) * HEAD_DIM, ks] = dk_s[h].astype(BF)
            gp[2 * D + h * HEAD_DIM : 2 * D + (h + 1) * HEAD_DIM, ks] = dv_s[h].astype(BF)
        return 0

    lax.fori_loop(0, seq // BLOCK_Q, outer, 0)

    def finish(head, unused):
        gp[head_rows(0, head), :] = (dq_s[head] * 0.125).astype(BF)
        return 0

    late[0].wait()
    back.start()
    lax.fori_loop(0, HEADS, finish, 0)
    late[1].wait()
    late[2].wait()
    outs = []

    def leave(step, part):
        rows = pl.ds(step * BLOCK_Q, BLOCK_Q)
        input_grad[rows, :] = (grad_row[rows, :] + part).astype(BF)
        outs.append(
            pltpu.make_async_copy(input_grad.at[rows, :], input_grad_h.at[rows, :], out_sem.at[4 + step])
        )
        outs[-1].start()

    staged(
        seq // BLOCK_Q,
        lambda step: dot_on(gp[:, pl.ds(step * BLOCK_Q, BLOCK_Q)], w[...], 0, 1),
        leave,
    )
    back.wait()
    for out in outs:
        out.wait()


def in_vmem():
    return pl.BlockSpec(memory_space=pltpu.VMEM)


def anywhere():
    return pl.BlockSpec(memory_space=pl.ANY)


def attend(x, w, seg):
    seq = x.shape[0]
    return pl.pallas_call(
        attend_kernel,
        in_specs=[in_vmem(), anywhere(), in_vmem()],
        out_specs=[anywhere(), anywhere(), in_vmem()],
        out_shape=(
            jax.ShapeDtypeStruct((3 * D, seq), BF),
            jax.ShapeDtypeStruct((D, seq), BF),
            jax.ShapeDtypeStruct((HEADS, 1, seq), F32),
        ),
        scratch_shapes=[
            pltpu.VMEM((D, 3 * D), BF),
            pltpu.VMEM((3 * D, seq), BF),
            pltpu.VMEM((D, seq), BF),
            pltpu.VMEM((D, seq), BF),
            pltpu.VMEM((HEADS, HEAD_DIM + AUG, seq), BF),
            pltpu.VMEM((HEADS, seq, HEAD_DIM + AUG), BF),
            pltpu.VMEM((HEADS, HEAD_DIM + AUG, seq), BF),
            pltpu.VMEM((HEADS, 8, BLOCK_Q), F32),
            pltpu.VMEM((HEADS, HEAD_DIM + AUG, BLOCK_Q), F32),
            pltpu.SemaphoreType.DMA((3,)),
            pltpu.SemaphoreType.DMA((3,)),
            pltpu.SemaphoreType.DMA((seq // BLOCK_Q,)),
        ],
        name="attend",
        compiler_params=pltpu.CompilerParams(vmem_limit_bytes=60 << 20),
    )(x, w, seg)


def attend_back(packed, ctx, lse, gctx, seg, out, w, grad_row):
    seq = packed.shape[1]
    aug = HEAD_DIM + AUG
    return pl.pallas_call(
        attend_back_kernel,
        in_specs=[anywhere(), anywhere(), in_vmem(), anywhere(), in_vmem(), anywhere(), anywhere(), anywhere()],
        out_specs=[anywhere(), anywhere()],
        out_shape=(jax.ShapeDtypeStruct((seq, D), BF), jax.ShapeDtypeStruct((seq, D), BF)),
        scratch_shapes=[
            pltpu.VMEM((3 * D, seq), BF),
            pltpu.VMEM((D, seq), BF),
            pltpu.VMEM((D, seq), BF),
            pltpu.VMEM((3 * D, seq), BF),
            pltpu.VMEM((D, 3 * D), BF),
            pltpu.VMEM((seq, D), F32),
            pltpu.VMEM((seq, D), BF),
            pltpu.VMEM((seq, D), BF),
            pltpu.VMEM((HEADS, HEAD_DIM, seq), BF),
            pltpu.VMEM((HEADS, seq, aug), BF),
            pltpu.VMEM((HEADS, seq, aug), BF),
            pltpu.VMEM((HEADS, aug, seq), BF),
            pltpu.VMEM((HEADS, aug, seq), BF),
            pltpu.VMEM((HEADS, HEAD_DIM, seq), F32),
            pltpu.VMEM((HEADS, HEAD_DIM, BLOCK_Q), F32),
            pltpu.VMEM((HEADS, HEAD_DIM, BLOCK_Q), F32),
            pltpu.SemaphoreType.DMA((HEADS // GROUP, 5)),
            pltpu.SemaphoreType.DMA((4 + seq // BLOCK_Q,)),
        ],
        name="attend_back",
        cost_estimate=pl.CostEstimate(flops=30_000_000_000, bytes_accessed=20_000_000, transcendentals=0),
        compiler_params=pltpu.CompilerParams(vmem_limit_bytes=62 << 20),
    )(packed, ctx, lse, gctx, seg, out, w, grad_row)


def pieces(value):
    high = value.astype(BF)
    return high, (value - high.astype(F32)).astype(BF)


def normalize(values):
    centre = values - jnp.mean(values, axis=-1, keepdims=True)
    factor = lax.rsqrt(jnp.mean(centre * centre, axis=-1, keepdims=True) + 1e-06)
    return centre * factor, factor


def norm_back(scaled, unit_vals, factor):
    return factor * (
        scaled
        - jnp.mean(scaled, axis=-1, keepdims=True)
        - unit_vals * jnp.mean(scaled * unit_vals, axis=-1, keepdims=True)
    )


def gelu_parts(values):
    rising = 0.5 * lax.erf(values * math.sqrt(0.5)) + 0.5
    low = values.astype(BF)
    bell = jnp.exp2(low * low * jnp.asarray(-0.5 * math.log2(math.e), BF))
    steep = low * jnp.asarray(1.0 / math.sqrt(2.0 * math.pi), BF)
    return (values * rising).astype(BF), rising.astype(BF) + steep * bell


def fold_rows(values):
    rows, columns = values.shape
    return jnp.sum(values.reshape(rows // 8, 8, columns), axis=0)


def staged(count, product, finish, between=None):
    held = {}
    for step in range(count + 1):
        if between is not None and step == count // 2:
            between()
        if step < count:
            held[step] = product(step)
        if step >= 1:
            finish(step - 1, held.pop(step - 1))


MESH = pl.DeviceIdType.MESH
PLANE = 4
DEPTH = 4
OWN_ROWS = 24
PLANE_ROWS = 96
CORE_ROWS = 384


def place():
    wide, narrow = lax.axis_index("wide"), lax.axis_index("narrow")
    return wide // 2, lax.rem(wide, 2), narrow // 2, lax.rem(narrow, 2)


def device(z, x, y, core):
    return (z * 2 + x, y * 2 + core)


def plane_mate(step):
    z, x, y, core = place()
    return device(z, jnp.bitwise_xor(x, step // 2), jnp.bitwise_xor(y, step % 2), core)


def depth_mate(step):
    z, x, y, core = place()
    return device(lax.rem(z + step, DEPTH), x, y, core)


def core_mate():
    z, x, y, core = place()
    return device(z, x, y, 1 - core)


def remote(source, target, sems, slot, mate):
    return pltpu.make_async_remote_copy(
        src_ref=source,
        dst_ref=target,
        send_sem=sems.at[0, slot],
        recv_sem=sems.at[1, slot],
        device_id=mate,
        device_id_type=MESH,
    )


def greet(mates):
    barrier = pltpu.get_barrier_semaphore()
    for mate in mates:
        pl.semaphore_signal(barrier, inc=1, device_id=mate, device_id_type=MESH)
    return lambda: pl.semaphore_wait(barrier, len(mates))


class Scatter:
    def __init__(self, which, square, kept, send, near, plane, small_send, small, gathered, sems):
        self.which, self.square, self.kept = which, square, kept
        self.send, self.near, self.plane = send, near, plane
        self.small_send, self.small, self.gathered, self.sems = small_send, small, gathered, sems
        z, x, y, core = place()
        self.z, self.spot, self.core = z, x * 2 + y, core
        self.copies = []

    def rows(self, start, count):
        return pl.ds(pl.multiple_of(start, 8), count)

    def finish(self):
        for copy in self.copies:
            copy.wait()
        self.copies = []

    def go(self, source, target, slot, mate):
        copy = remote(source, target, self.sems, self.which * 16 + slot, mate)
        copy.start()
        self.copies.append(copy)

    def to_core(self):
        self.go(self.send.at[self.which], self.near.at[self.which], 0, core_mate())

    def to_plane(self):
        self.finish()
        for q in range(PLANE):
            rows = pl.ds(q * PLANE_ROWS, PLANE_ROWS)
            total = self.square[rows, :] + self.near[self.which, q].astype(F32)
            self.square[rows, :] = total
            self.send[self.which, q] = total.astype(BF)
        self.kept[self.which] = self.square[self.rows(self.spot * PLANE_ROWS, PLANE_ROWS), :]
        for step in range(1, PLANE):
            spot = jnp.bitwise_xor(self.spot, step)
            self.go(self.send.at[self.which, spot], self.plane.at[self.which, step - 1], step, plane_mate(step))

    def to_depth(self):
        self.finish()
        total = self.kept[self.which]
        for step in range(1, PLANE):
            total = total + self.plane[self.which, step - 1].astype(F32)
        self.kept[self.which] = total
        for k in range(DEPTH):
            self.small_send[self.which, k] = total[k * OWN_ROWS : (k + 1) * OWN_ROWS, :].astype(BF)
        for step in range(1, DEPTH):
            spot = lax.rem(self.z + step, DEPTH)
            self.go(
                self.small_send.at[self.which, spot],
                self.small.at[self.which, step - 1],
                PLANE - 1 + step,
                depth_mate(step),
            )

    def share(self):
        self.finish()
        total = self.kept[self.which, self.rows(self.z * OWN_ROWS, OWN_ROWS), :]
        for step in range(1, DEPTH):
            total = total + self.small[self.which, step - 1].astype(F32)
        self.gathered[self.core, self.which, self.z] = total.astype(BF)
        mine = self.gathered.at[self.core, self.which, self.z]
        for step in range(1, DEPTH):
            self.go(mine, mine, PLANE + DEPTH - 2 + step, depth_mate(step))

    def pair(self):
        arriving, self.copies = self.copies, []
        for step in range(DEPTH):
            if step:
                arriving[step - 1].wait()
            spot = lax.rem(self.z - step + DEPTH, DEPTH)
            chunk = self.gathered.at[self.core, self.which, spot]
            self.go(chunk, chunk, PLANE + 2 * DEPTH - 2 + step, core_mate())


ROWS_AT_ONCE = 256
HIDDEN_AT_ONCE = 512
HIDDEN_ROWS = 512


def middle_kernel(
    joined, x_h, g_h, ctx_h, wo_h, win_h, wout_h, down_h, up_h, wq_h, wk_h, wv_h,
    bias_h, gain_one_h, shift_one_h, gain_two_h, shift_two_h, mask,
    out_h, gr_h, gctx_h, v_h, gg_h, sums_out,
    x, g, ctx, wo, win, wout, bank, wq, wk, wv,
    unit_one, unit_two, bottle, guide, total, act, slope, low, factor, mix, score_grads,
    v_s, gg_s, sums_part, vectors, in_sem, vector_sem, out_sem, *links,
):
    seq, width = x.shape
    blocks = seq // ROWS_AT_ONCE
    mix_scale = 1.0 / math.sqrt(D)
    loads = {}
    names = ("down", "up", "ctx", "wo", "x", "win", "wout", "wq", "wk", "g", "wv")
    sources = (down_h, up_h, ctx_h, wo_h, x_h, win_h, wout_h, wq_h, wk_h, g_h, wv_h)
    targets = (bank.at[0], bank.at[1], ctx, wo, x, win, wout, wq, wk, g, wv)
    vector_loads = [
        pltpu.make_async_copy(source, vectors.at[number, pl.ds(0, width)], vector_sem.at[number])
        for number, source in enumerate((gain_one_h, shift_one_h, gain_two_h, shift_two_h))
    ] + [
        pltpu.make_async_copy(
            bias_h.at[pl.ds(number * 1024, 1024)], vectors.at[4 + number], vector_sem.at[4 + number]
        )
        for number in range(win.shape[1] // 1024)
    ]
    for load in vector_loads:
        load.start()
    gain_one, shift_one, gain_two, shift_two = (vectors.at[number : number + 1, :width] for number in range(4))
    if joined:
        (
            kept, send, near, plane, small_send, small, gathered,
            sums_near, sums_plane, sums_depth, sums_mid, link_sems, bank_sems, sums_sems,
        ) = links
        arrived = greet(
            [core_mate()]
            + [plane_mate(step) for step in range(1, PLANE)]
            + [depth_mate(step) for step in range(1, DEPTH)]
        )
        spot = lax.axis_index("narrow")
        shard = down_h.shape[0]

        def bank_rows(index):
            return bank.at[:, pl.ds(pl.multiple_of(index * shard, 16), shard), :]

        own_rows = pl.ds(pl.multiple_of(spot * shard, 16), shard)
        targets = (bank.at[0, own_rows, :], bank.at[1, own_rows, :]) + targets[2:]
    for number, name in enumerate(names):
        loads[name] = pltpu.make_async_copy(sources[number], targets[number], in_sem.at[number])
    for name in names:
        loads[name].start()

    def rows_of(step):
        return pl.ds(step * ROWS_AT_ONCE, ROWS_AT_ONCE)

    t_one, t_two, t_three, t_four = (pl.ds(k * width, width) for k in range(4))
    down, up = 0, 1
    column = lax.broadcasted_iota(jnp.int32, (ADAPTERS, width), 1)
    owner = lax.rem(column, ADAPTERS)
    chosen = jnp.where(
        owner == lax.broadcasted_iota(jnp.int32, (ADAPTERS, width), 0), 1.0, 0.0
    ).astype(BF)

    chosen_twice = jnp.concatenate([chosen, chosen], axis=0)

    def per_adapter(values):
        high, rest = pieces(values)
        return dot_on(chosen, high, 1, 1) + dot_on(chosen, rest, 1, 1)

    def per_unit(values):
        return dot_on(jnp.concatenate(pieces(values), axis=0), chosen_twice, 0, 0)

    loads["ctx"].wait()
    loads["wo"].wait()
    loads["x"].wait()
    for load in vector_loads:
        load.wait()

    def finish_first(step, part):
        rows = rows_of(step)
        unit, scale = normalize(x[rows, :].astype(F32) + part)
        unit_one[rows, :] = unit
        factor[rows, 0:1] = scale
        low[rows, :] = (unit * gain_one[...] + shift_one[...]).astype(BF)

    if joined:
        arrived()
        loads["down"].wait()
        loads["up"].wait()
        bank_copies = [
            remote(bank_rows(spot), bank_rows(spot), bank_sems, 0, core_mate()),
            remote(bank_rows(spot), bank_rows(spot), bank_sems, 1, plane_mate(1)),
        ]
        for copy in bank_copies:
            copy.start()
    staged(blocks, lambda step: dot_on(ctx[:, rows_of(step)], wo[...], 0, 0), finish_first)

    loads["win"].wait()

    def hidden(chunk, unused):
        columns = pl.ds(pl.multiple_of(chunk * HIDDEN_AT_ONCE, HIDDEN_AT_ONCE), HIDDEN_AT_ONCE)
        per_row = 1024 // HIDDEN_AT_ONCE
        lanes = pl.ds(pl.multiple_of(lax.rem(chunk, per_row) * HIDDEN_AT_ONCE, HIDDEN_AT_ONCE), HIDDEN_AT_ONCE)
        bias = vectors[pl.ds(4 + chunk // per_row, 1), lanes]

        def rows_in(step):
            return pl.ds(step * HIDDEN_ROWS, HIDDEN_ROWS)

        def finish(step, part):
            rows = rows_in(step)
            value, rising = gelu_parts(part + bias)
            act[rows, columns] = value
            slope[rows, columns] = rising

        staged(seq // HIDDEN_ROWS, lambda step: dot_on(low[rows_in(step), :], win[:, columns], 1, 0), finish)
        return 0

    lax.fori_loop(0, win.shape[1] // HIDDEN_AT_ONCE, hidden, 0)
    loads["wout"].wait()

    def second(half, unused):
        def rows_in(step):
            start = half * (seq // 2) + step * ROWS_AT_ONCE
            return pl.ds(pl.multiple_of(start, ROWS_AT_ONCE), ROWS_AT_ONCE)

        def finish(step, part):
            rows = rows_in(step)
            unit, scale = normalize(unit_one[rows, :] * gain_one[...] + shift_one[...] + part)
            unit_two[rows, :] = unit
            factor[rows, 1:2] = scale
            low[rows, :] = (unit * gain_two[...] + shift_two[...]).astype(BF)

        staged(blocks // 2, lambda step: dot_on(act[rows_in(step), :], wout[...], 1, 0), finish)
        return 0

    lax.fori_loop(0, 2, second, 0)

    def h_two(rows):
        return unit_two[rows, :] * gain_two[...] + shift_two[...]

    if joined:
        bank_copies[1].wait()
        other = jnp.bitwise_xor(spot, 2)
        bank_copies[1] = remote(bank_rows(other), bank_rows(other), bank_sems, 2, core_mate())
        bank_copies[1].start()
    loads["wq"].wait()

    def keep(place):
        def finish(step, part):
            act[rows_of(step), place] = part.astype(BF)

        return finish

    staged(blocks, lambda step: dot_on(low[rows_of(step), :], wq[...], 1, 0), keep(t_one))
    loads["wk"].wait()
    staged(blocks, lambda step: dot_on(act[rows_of(step), t_one], wk[...], 1, 1), keep(t_two))
    if joined:
        for copy in bank_copies:
            copy.wait()
    else:
        loads["down"].wait()
        loads["up"].wait()

    def finish_down(step, part):
        rows = rows_of(step)
        bottle[rows, :] = part * (0.5 * lax.erf(part * math.sqrt(0.5)) + 0.5)
        act[rows, t_four] = gelu_parts(part)[1]

    staged(blocks, lambda step: dot_on(low[rows_of(step), :], bank[down], 1, 1), finish_down)

    def finish_guide(step, part):
        rows = rows_of(step)
        guide[rows, :] = part
        mix[:, rows] = per_adapter(bottle[rows, :] * part)

    staged(blocks, lambda step: dot_on(act[rows_of(step), t_two], bank[up], 1, 1), finish_guide)
    scores = mix[...] * mix_scale
    shifted = scores - jnp.max(scores, axis=0, keepdims=True)
    exponents = jnp.exp(shifted)
    total_exponent = jnp.sum(exponents, axis=0, keepdims=True)
    weights = exponents / total_exponent
    entropies = -jnp.sum(weights * (shifted - jnp.log(total_exponent)), axis=0, keepdims=True)
    mix[...] = weights

    def finish_mix(step, part):
        rows = rows_of(step)
        act[rows, t_one] = (part * bottle[rows, :]).astype(BF)

    staged(blocks, lambda step: per_unit(mix[:, rows_of(step)]), finish_mix)
    real = mask[...].astype(F32)
    ent = jnp.sum(entropies * real, axis=1, keepdims=True)
    lane = lax.broadcasted_iota(jnp.int32, (1, 1024), 1)
    sums_out[7:8, :] = jnp.where(lane < 128, ent, jnp.sum(real, axis=1, keepdims=True))
    sums_out[3:7, width:] = jnp.zeros((4, 1024 - width), F32)

    def finish_update(step, part):
        rows = rows_of(step)
        x[rows, :] = (h_two(rows) + part).astype(BF)

    staged(blocks, lambda step: dot_on(act[rows_of(step), t_one], bank[up], 1, 0), finish_update)

    loads["g"].wait()
    third = width // 3

    def over_tokens(left, right, target):
        def product(step):
            return dot_on(left(pl.ds(step * third, third)), right, 0, 0)

        def finish(step, part):
            target[pl.ds(step * third, third), :] = part

        staged(3, product, finish)

    def halves(left, base, right, target, which):
        core = place()[3]

        def product(step):
            start = base + (core if step else 1 - core) * CORE_ROWS
            return dot_on(left[:, pl.ds(pl.multiple_of(start, 128), CORE_ROWS)], right, 0, 0)

        def finish(step, part):
            if step:
                target[...] = part
            else:
                for q in range(PLANE):
                    send[which, q] = part[q * PLANE_ROWS : (q + 1) * PLANE_ROWS, :].astype(BF)

        staged(2, product, finish)

    if joined:
        halves(x, 0, g[...], v_s, 0)
    else:
        over_tokens(lambda cols: x[:, cols], g[...], v_s)
    if joined:
        value_sum, joint_sum = (
            Scatter(k, v_s, kept, send, near, plane, small_send, small, gathered, link_sems) for k in range(2)
        )
        value_sum.to_core()
    else:
        v_out = pltpu.make_async_copy(v_s, v_h, out_sem.at[0])
        v_out.start()

    loads["wv"].wait()

    def finish_blend(step, part):
        rows = rows_of(step)
        total[rows, :] = g[rows, :].astype(F32) + part
        act[rows, t_one] = part.astype(BF)

    staged(blocks, lambda step: dot_on(g[rows_of(step), :], wv[...], 1, 1), finish_blend)

    def finish_mixed(step, part):
        rows = rows_of(step)
        act[rows, t_one] = part.astype(BF)
        score_grads[:, rows] = per_adapter(part * bottle[rows, :])

    staged(blocks, lambda step: dot_on(act[rows_of(step), t_one], bank[up], 1, 1), finish_mixed, value_sum.to_plane if joined else None)
    weights = mix[...]
    grad_weights = score_grads[...]
    inner = jnp.sum(grad_weights * weights, axis=0, keepdims=True)
    score_grads[...] = weights * (grad_weights - inner) * mix_scale

    def finish_units(step, part):
        rows = rows_of(step)
        mixed, score_term = part
        grad_bottle = act[rows, t_one].astype(F32) * mixed + score_term * guide[rows, :]
        act[rows, t_three] = (grad_bottle * act[rows, t_four].astype(F32)).astype(BF)
        act[rows, t_one] = (score_term * bottle[rows, :]).astype(BF)

    staged(
        blocks,
        lambda step: (per_unit(mix[:, rows_of(step)]), per_unit(score_grads[:, rows_of(step)])),
        finish_units,
    )
    staged(blocks, lambda step: dot_on(act[rows_of(step), t_one], bank[up], 1, 0), keep(t_two))
    if joined:
        halves(low, 0, act[:, t_two], v_s, 1)
    else:
        over_tokens(lambda cols: low[:, cols], act[:, t_two], gg_s)
    if joined:
        joint_sum.to_core()
    else:
        gg_out = pltpu.make_async_copy(gg_s, gg_h, out_sem.at[2])
        gg_out.start()
    staged(blocks, lambda step: dot_on(act[rows_of(step), t_two], wk[...], 1, 0), keep(t_one))
    partial = [jnp.zeros((8, width), F32) for unused in range(4)]

    def finish_two(step, part):
        rows = rows_of(step)
        grad = total[rows, :] + part
        unit = unit_two[rows, :]
        partial[0] = partial[0] + fold_rows(grad * unit)
        partial[1] = partial[1] + fold_rows(grad)
        back = norm_back(grad * gain_two[...], unit, factor[rows, 1:2])
        total[rows, :] = back
        low[rows, :] = back.astype(BF)

    staged(
        blocks,
        lambda step: dot_on(act[rows_of(step), t_three], bank[down], 1, 0)
        + dot_on(act[rows_of(step), t_one], wq[...], 1, 1),
        finish_two,
        joint_sum.to_plane if joined else None,
    )

    if joined:
        value_sum.to_depth()

    def hidden_back(chunk, unused):
        columns = pl.ds(pl.multiple_of(chunk * HIDDEN_AT_ONCE, HIDDEN_AT_ONCE), HIDDEN_AT_ONCE)
        held = [jnp.zeros((8, HIDDEN_AT_ONCE), F32)]

        def rows_in(step):
            return pl.ds(step * HIDDEN_ROWS, HIDDEN_ROWS)

        def finish(step, part):
            rows = rows_in(step)
            grad = (part * slope[rows, columns].astype(F32)).astype(BF)
            act[rows, columns] = grad
            held[0] = held[0] + fold_rows(grad.astype(F32))

        staged(seq // HIDDEN_ROWS, lambda step: dot_on(low[rows_in(step), :], wout[columns, :], 1, 1), finish)
        sums_part[chunk] = held[0]
        return 0

    lax.fori_loop(0, win.shape[1] // HIDDEN_AT_ONCE, hidden_back, 0)
    for number in range(win.shape[1] // HIDDEN_AT_ONCE):
        at, lanes = divmod(number * HIDDEN_AT_ONCE, 1024)
        sums_out[at : at + 1, pl.ds(lanes, HIDDEN_AT_ONCE)] = jnp.sum(sums_part[number], axis=0, keepdims=True)
    sums_out[5:6, :width] = jnp.sum(partial[0], axis=0, keepdims=True)
    sums_out[6:7, :width] = jnp.sum(partial[1], axis=0, keepdims=True)
    if joined:
        value_sum.share()
        joint_sum.to_depth()

    def first_back(half, carried):
        def rows_in(step):
            start = half * (seq // 2) + step * ROWS_AT_ONCE
            return pl.ds(pl.multiple_of(start, ROWS_AT_ONCE), ROWS_AT_ONCE)

        held = list(carried)

        def finish(step, part):
            rows = rows_in(step)
            grad = total[rows, :] + part
            unit = unit_one[rows, :]
            held[0] = held[0] + fold_rows(grad * unit)
            held[1] = held[1] + fold_rows(grad)
            back = norm_back(grad * gain_one[...], unit, factor[rows, 0:1])
            total[rows, :] = back
            low[rows, :] = back.astype(BF)

        staged(blocks // 2, lambda step: dot_on(act[rows_in(step), :], win[...], 1, 1), finish)
        return tuple(held)

    zero = jnp.zeros((8, width), F32)
    gain_sum, shift_sum = lax.fori_loop(0, 2, first_back, (zero, zero))
    sums_out[3:4, :width] = jnp.sum(gain_sum, axis=0, keepdims=True)
    sums_out[4:5, :width] = jnp.sum(shift_sum, axis=0, keepdims=True)
    if joined:
        near_copy = remote(sums_out, sums_near, sums_sems, 0, core_mate())
        near_copy.start()
        value_sum.pair()
        joint_sum.share()
    gr_copy = pltpu.make_async_copy(total, gr_h, out_sem.at[3])
    gr_copy.start()

    def finish_ctx(step, part):
        ctx[pl.ds(step * third, third), :] = part.astype(BF)

    staged(3, lambda step: dot_on(wo[pl.ds(step * third, third), :], low[...], 1, 1), finish_ctx)
    gctx_copy = pltpu.make_async_copy(ctx, gctx_h, out_sem.at[4])
    gctx_copy.start()
    if joined:
        near_copy.wait()
        sums_mid[0] = sums_out[...] + sums_near[...]
        plane_copies = [
            remote(sums_mid.at[0], sums_plane.at[step - 1], sums_sems, step, plane_mate(step))
            for step in range(1, PLANE)
        ]
        for copy in plane_copies:
            copy.start()
        value_sum.finish()

    def finish_out(step, part):
        rows = rows_of(step)
        x[rows, :] = (h_two(rows) + part).astype(BF)

    staged(blocks, lambda step: dot_on(x[rows_of(step), :], wv[...], 1, 0), finish_out)
    out_copy = pltpu.make_async_copy(x, out_h, out_sem.at[1])
    out_copy.start()
    if joined:
        for copy in plane_copies:
            copy.wait()
        sums_mid[1] = sums_mid[0] + sums_plane[0] + sums_plane[1] + sums_plane[2]
        depth_copies = [
            remote(sums_mid.at[1], sums_depth.at[step - 1], sums_sems, PLANE - 1 + step, depth_mate(step))
            for step in range(1, DEPTH)
        ]
        for copy in depth_copies:
            copy.start()
        joint_sum.pair()
        joint_sum.finish()
        v_out = pltpu.make_async_copy(gathered, v_h, out_sem.at[0])
        v_out.start()
        for copy in depth_copies:
            copy.wait()
        sums_out[...] = sums_mid[1] + sums_depth[0] + sums_depth[1] + sums_depth[2]
    else:
        gg_out.wait()
    v_out.wait()
    out_copy.wait()
    gr_copy.wait()
    gctx_copy.wait()


def middle(joined, x, g, ctx, wo, win, wout, down, up, wq, wk, wv, bias, gain_one, shift_one, gain_two, shift_two, mask):
    seq, width = x.shape
    hidden = win.shape[1]
    token_low = pltpu.VMEM((seq, width), BF)
    token_wide = pltpu.VMEM((seq, width), F32)
    square = pltpu.VMEM((width, width), BF)
    sum_square = pltpu.VMEM((CORE_ROWS if joined else width, width), F32)
    links = [
        pltpu.VMEM((2, PLANE_ROWS, width), F32),
        pltpu.VMEM((2, PLANE, PLANE_ROWS, width), BF),
        pltpu.VMEM((2, PLANE, PLANE_ROWS, width), BF),
        pltpu.VMEM((2, PLANE - 1, PLANE_ROWS, width), BF),
        pltpu.VMEM((2, DEPTH, OWN_ROWS, width), BF),
        pltpu.VMEM((2, DEPTH - 1, OWN_ROWS, width), BF),
        pltpu.VMEM((2, 2, DEPTH, OWN_ROWS, width), BF),
        pltpu.VMEM((8, 1024), F32),
        pltpu.VMEM((PLANE - 1, 8, 1024), F32),
        pltpu.VMEM((DEPTH - 1, 8, 1024), F32),
        pltpu.VMEM((2, 8, 1024), F32),
        pltpu.SemaphoreType.DMA((2, 32)),
        pltpu.SemaphoreType.DMA((2, 3)),
        pltpu.SemaphoreType.DMA((2, PLANE + DEPTH - 1)),
    ]
    return pl.pallas_call(
        functools.partial(middle_kernel, joined),
        in_specs=[anywhere() for unused in range(16)] + [in_vmem()],
        out_specs=[anywhere() for unused in range(5)] + [in_vmem()],
        out_shape=(
            jax.ShapeDtypeStruct((seq, width), BF),
            jax.ShapeDtypeStruct((seq, width), F32),
            jax.ShapeDtypeStruct((width, seq), BF),
            jax.ShapeDtypeStruct((2, 2, DEPTH, OWN_ROWS, width), BF)
            if joined
            else jax.ShapeDtypeStruct((width, width), F32),
            jax.ShapeDtypeStruct((8, 128) if joined else (width, width), F32),
            jax.ShapeDtypeStruct((8, 1024), F32),
        ),
        scratch_shapes=[
            token_low, token_low, pltpu.VMEM((width, seq), BF),
            square, pltpu.VMEM((width, hidden), BF), pltpu.VMEM((hidden, width), BF),
            pltpu.VMEM((2, width, width), BF), square, square, square,
            token_wide, token_wide, token_wide, token_wide, token_wide,
            pltpu.VMEM((seq, hidden), BF), pltpu.VMEM((seq, hidden), BF), token_low,
            pltpu.VMEM((seq, 2), F32), pltpu.VMEM((ADAPTERS, seq), F32), pltpu.VMEM((ADAPTERS, seq), F32),
            sum_square, pltpu.VMEM((8, 128) if joined else (width, width), F32),
            pltpu.VMEM((hidden // HIDDEN_AT_ONCE, 8, HIDDEN_AT_ONCE), F32),
            pltpu.VMEM((8, 1024), F32),
            pltpu.SemaphoreType.DMA((11,)), pltpu.SemaphoreType.DMA((7,)), pltpu.SemaphoreType.DMA((5,)),
        ]
        + (links if joined else []),
        name="middle",
        compiler_params=pltpu.CompilerParams(
            vmem_limit_bytes=VMEM_BYTES, **(dict(collective_id=0, has_side_effects=True) if joined else {})
        ),
    )(x, g, ctx, wo, win, wout, down, up, wq, wk, wv, bias, gain_one, shift_one, gain_two, shift_two, mask)

def products_kernel(
    mine_h, first_h, second_h, third_h, wk_h, wq_h, sums,
    value_h, query_h, key_h, bias_h, gain_one_h, shift_one_h, gain_two_h, shift_two_h, entropy,
    held, wk, wq, square, joint, low, in_sem, out_sem,
):
    width = wk.shape[0]
    z, x, y, core = place()
    loads = [
        pltpu.make_async_copy(source, target, in_sem.at[number])
        for number, (source, target) in enumerate(
            [(source, held.at[step]) for step, source in enumerate((mine_h, first_h, second_h, third_h))]
            + [(wk_h, wk), (wq_h, wq)]
        )
    ]
    for load in loads:
        load.start()
    outs = []

    def leave(source, target):
        outs.append(pltpu.make_async_copy(source, target, out_sem.at[len(outs)]))
        outs[-1].start()

    for number in range(bias_h.shape[0] // 1024):
        leave(sums.at[number], bias_h.at[pl.ds(number * 1024, 1024)])
    for number, target in enumerate((gain_one_h, shift_one_h, gain_two_h, shift_two_h)):
        leave(sums.at[3 + number, pl.ds(0, width)], target)
    entropy[...] = sums[7:8, 0:1] / sums[7:8, 128:129]
    for load in loads[:PLANE]:
        load.wait()

    def unpack(which, target):
        for step in range(PLANE):
            base = jnp.bitwise_xor(x * 2 + y, step) * PLANE_ROWS
            for side in range(2):
                for depth in range(DEPTH):
                    start = pl.multiple_of(base + side * CORE_ROWS + depth * OWN_ROWS, 8)
                    target[pl.ds(start, OWN_ROWS), :] = held[step, side, which, depth].astype(F32)

    unpack(0, square.at[0])
    leave(square.at[0], value_h)
    unpack(1, joint)
    low[...] = joint[...].astype(BF)
    loads[PLANE].wait()
    half = width // 2
    for step in range(2):
        rows = pl.ds(step * half, half)
        square[1, rows, :] = dot_on(low[rows, :], wk[...], 1, 0)
        leave(square.at[1, rows, :], query_h.at[rows, :])
    loads[PLANE + 1].wait()
    for step in range(2):
        rows = pl.ds(step * half, half)
        joint[rows, :] = dot_on(low[:, rows], wq[...], 0, 0)
        leave(joint.at[rows, :], key_h.at[rows, :])
    for out in outs:
        out.wait()


def products(held, wk, wq, sums, hidden):
    width = wk.shape[0]
    square = jax.ShapeDtypeStruct((width, width), F32)
    vector = jax.ShapeDtypeStruct((width,), F32)
    return pl.pallas_call(
        products_kernel,
        in_specs=[anywhere() for unused in range(6)] + [in_vmem()],
        out_specs=[anywhere() for unused in range(8)] + [in_vmem()],
        out_shape=(
            square, square, square, jax.ShapeDtypeStruct((hidden,), F32), vector, vector, vector, vector,
            jax.ShapeDtypeStruct((1, 1), F32),
        ),
        scratch_shapes=[
            pltpu.VMEM((PLANE,) + held[0].shape, BF),
            pltpu.VMEM((width, width), BF),
            pltpu.VMEM((width, width), BF),
            pltpu.VMEM((2, width, width), F32),
            pltpu.VMEM((width, width), F32),
            pltpu.VMEM((width, width), BF),
            pltpu.SemaphoreType.DMA((PLANE + 2,)),
            pltpu.SemaphoreType.DMA((12,)),
        ],
        name="products",
        compiler_params=pltpu.CompilerParams(vmem_limit_bytes=VMEM_BYTES),
    )(*held, wk, wq, sums)


def plane_order(step):
    order = []
    for index in range(32):
        wide, narrow = index // 4, index % 4
        wide, narrow = wide ^ (step // 2), narrow ^ (2 * (step % 2))
        order.append((index, wide * 4 + narrow))
    return order

def per_device(
    joined,
    block_input, segments, real_mask, qkv_weight, attn_out_weight, ffn_in_weight, ffn_bias, ffn_out_weight,
    first_gain, first_shift, second_gain, second_shift, adapter_down, adapter_up,
    joining_query, joining_key, joining_value, cotangent,
):
    row_count, seq_len, width = block_input.shape
    tokens = block_input.reshape(seq_len, width)
    units = adapter_down.shape[2]
    down = jnp.transpose(adapter_down, (2, 1, 0)).reshape(ADAPTERS * units, width)
    up = jnp.transpose(adapter_up, (1, 0, 2)).reshape(ADAPTERS * units, width)
    if not joined:
        down, up = (lax.all_gather(part, "narrow", axis=0, tiled=True) for part in (down, up))
    seg_row = segments.reshape(1, seq_len)
    packed, context, log_total = attend(tokens, qkv_weight, seg_row)
    out, grad_row, grad_context, value_sum, joint_sum, sums = middle(
        joined,
        tokens, cotangent.reshape(seq_len, width), context, attn_out_weight, ffn_in_weight, ffn_out_weight,
        down, up, joining_query, joining_key, joining_value, ffn_bias, first_gain, first_shift,
        second_gain, second_shift, real_mask.reshape(1, seq_len),
    )
    input_grad, out = attend_back(
        packed, context, log_total, grad_context, seg_row, out, qkv_weight, grad_row
    )
    if joined:
        held = [value_sum] + [
            lax.ppermute(value_sum, ("wide", "narrow"), plane_order(step)) for step in range(1, PLANE)
        ]
        value_grad, query_grad, key_grad, bias_grad, gain_one, shift_one, gain_two, shift_two, entropy = products(
            held, joining_key, joining_query, sums, ffn_bias.shape[0]
        )
    else:
        value_grad, joint_sum, sums = lax.psum((value_sum, joint_sum, sums), ("wide", "narrow"))
        query_grad = dot_on(joint_sum.astype(BF), joining_key, 1, 0)
        key_grad = dot_on(joint_sum.astype(BF), joining_query, 0, 0)
        bias_grad = sums[:3].reshape(ffn_bias.shape[0])
        gain_one, shift_one, gain_two, shift_two = (sums[number, :width] for number in range(3, 7))
        entropy = sums[7, 0] / sums[7, 128]
    return (
        out.reshape(row_count, seq_len, width),
        input_grad.reshape(row_count, seq_len, width),
        query_grad,
        key_grad,
        value_grad,
        bias_grad,
        gain_one,
        shift_one,
        gain_two,
        shift_two,
        entropy.reshape(()),
    )


def solution(mesh):
    placed = (
        P(("wide", "narrow"), None, None),
        P(("wide", "narrow"), None),
        P(("wide", "narrow"), None),
        P(),
        P(),
        P(),
        P(),
        P(),
        P(),
        P(),
        P(),
        P(),
        P(None, None, "narrow"),
        P(None, "narrow", None),
        P(),
        P(),
        P(),
        P(("wide", "narrow"), None, None),
    )
    joined = mesh.shape["wide"] == 8 and mesh.shape["narrow"] == 4
    return jax.shard_map(
        functools.partial(per_device, joined),
        mesh=mesh,
        in_specs=placed,
        out_specs=(
            P(("wide", "narrow"), None, None),
            P(("wide", "narrow"), None, None),
            P(),
            P(),
            P(),
            P(),
            P(),
            P(),
            P(),
            P(),
            P(),
        ),
        check_vma=False,
    )
```

```python
import math

import jax
import jax.numpy as jnp
import functools

from jax import lax
from jax.experimental import pallas as pl
from jax.experimental.pallas import tpu as pltpu
from jax.sharding import PartitionSpec as P

D = 768
HEADS = 12
HEAD_DIM = 64
ADAPTERS = 16
BOTTLE = 48

AUG = 16
BF = jnp.bfloat16
F32 = jnp.float32
BLOCK_Q = 256
BLOCK_K = 128
UNROLL = 4
VMEM_BYTES = 64 << 20


def dot_on(left_op, right_op, left_dim, right_dim):
    return lax.dot_general(
        left_op,
        right_op,
        (((left_dim,), (right_dim,)), ((), ())),
        preferred_element_type=F32,
    )


def head_rows(part, head):
    return pl.ds(pl.multiple_of(part * D + head * HEAD_DIM, HEAD_DIM), HEAD_DIM)


def doc_starts(seg):
    return [jnp.sum((seg[...] < doc).astype(jnp.int32)) for doc in range(1, 4)]


def key_range(starts, seq, i):
    low, high = jnp.int32(0), jnp.int32(seq)
    for start in starts:
        low = jnp.where(start <= i * BLOCK_Q, jnp.maximum(low, start), low)
        high = jnp.where(start >= (i + 1) * BLOCK_Q, jnp.minimum(high, start), high)
    return low // BLOCK_K, (high + BLOCK_K - 1) // BLOCK_K


def attend_kernel(
    x_h, w_h, seg_h, packed_h, ctx_h, lse_h,
    x, w, seg, packed, ctx, lse, xt, qa, kt, va, m_s, o_s, in_sem, w_sem, packed_sem, ctx_sem,
):
    seq, width = x.shape

    def w_copy(part):
        columns = pl.ds(pl.multiple_of(part * width, width), width)
        return pltpu.make_async_copy(w_h.at[:, columns], w.at[:, columns], w_sem.at[part])

    def packed_copy(part):
        rows = pl.ds(pl.multiple_of(part * width, width), width)
        return pltpu.make_async_copy(packed.at[rows, :], packed_h.at[rows, :], packed_sem.at[part])

    def ctx_copies(i):
        columns = pl.ds(pl.multiple_of(i * BLOCK_Q, BLOCK_Q), BLOCK_Q)
        return (
            pltpu.make_async_copy(ctx.at[:, columns], ctx_h.at[:, columns], ctx_sem.at[0, i]),
            pltpu.make_async_copy(lse.at[:, :, columns], lse_h.at[:, :, columns], ctx_sem.at[1, i]),
        )

    seg_copy = pltpu.make_async_copy(seg_h, seg, in_sem.at[0])
    x_copy = pltpu.make_async_copy(x_h, x, in_sem.at[1])
    seg_copy.start()
    x_copy.start()
    for part in range(3):
        w_copy(part).start()
    seg_copy.wait()
    starts = doc_starts(seg)
    x_copy.wait()
    xt[...] = x[...].T

    def project(part, unused):
        w_copy(part).wait()
        rows = pl.ds(pl.multiple_of(part * width, width), width)
        packed[rows, :] = dot_on(w[:, rows], xt[...], 0, 0).astype(BF)
        packed_copy(part).start()
        return 0

    lax.fori_loop(0, 3, project, 0)
    row = lax.broadcasted_iota(jnp.int32, (AUG, seq), 0)
    same = row == seg[...]
    aug_q = jnp.where(same, 1.0, 0.0).astype(BF)
    aug_k = jnp.where((row < 4) & (~same), -1e30, 0.0).astype(BF)

    def prepare(head, unused):
        qa[head, :HEAD_DIM, :] = packed[head_rows(0, head), :] * jnp.asarray(0.125, BF)
        qa[head, HEAD_DIM:, :] = aug_q
        kt[head] = jnp.concatenate([packed[head_rows(1, head), :], aug_k], axis=0).T
        va[head, :HEAD_DIM, :] = packed[head_rows(2, head), :]
        va[head, HEAD_DIM:, :] = jnp.ones((AUG, seq), BF)
        return 0

    lax.fori_loop(0, HEADS, prepare, 0, unroll=UNROLL)

    def query_block(i, unused):
        qs = pl.ds(pl.multiple_of(i * BLOCK_Q, BLOCK_Q), BLOCK_Q)
        for h in range(HEADS):
            m_s[h] = jnp.full((8, BLOCK_Q), -1e30, F32)
            o_s[h] = jnp.zeros((HEAD_DIM + AUG, BLOCK_Q), F32)

        def key_block(j, unused):
            ks = pl.ds(pl.multiple_of(j * BLOCK_K, BLOCK_K), BLOCK_K)
            first, second = {}, {}
            lag = 4
            for t in range(HEADS + 2 * lag):
                if t < HEADS:
                    first[t] = dot_on(kt[t, ks, :], qa[t, :, qs], 1, 0)
                h = t - lag
                if 0 <= h < HEADS:
                    tile = first.pop(h).reshape(BLOCK_K // 8, 8, BLOCK_Q)
                    top = jnp.max(jnp.max(tile, axis=0), axis=0, keepdims=True)
                    old = m_s[h]
                    new = jnp.maximum(old, jnp.broadcast_to(top, (8, BLOCK_Q)))
                    m_s[h] = new
                    prob = jnp.exp(tile - new[None]).reshape(BLOCK_K, BLOCK_Q).astype(BF)
                    second[h] = (prob, jnp.exp(old - new))
                h = t - 2 * lag
                if 0 <= h < HEADS:
                    prob, decay = second.pop(h)
                    rows = HEAD_DIM + AUG
                    kept = (o_s[h].reshape(rows // 8, 8, BLOCK_Q) * decay[None]).reshape(rows, BLOCK_Q)
                    o_s[h] = kept + dot_on(va[h, :, ks], prob, 1, 0)
            return 0

        lax.fori_loop(*key_range(starts, seq, i), key_block, 0)
        for h in range(HEADS):
            total = o_s[h, HEAD_DIM : HEAD_DIM + 1, :]
            ctx[h * HEAD_DIM : (h + 1) * HEAD_DIM, qs] = (o_s[h, :HEAD_DIM, :] * (1.0 / total)).astype(BF)
            lse[h, :, qs] = m_s[h][:1] + jnp.log(total)
        for copy in ctx_copies(i):
            copy.start()
        return 0

    lax.fori_loop(0, seq // BLOCK_Q, query_block, 0)
    for part in range(3):
        packed_copy(part).wait()
    for i in range(seq // BLOCK_Q):
        for copy in ctx_copies(i):
            copy.wait()


GROUP = 4


def attend_back_kernel(
    packed_h, ctx_h, lse_h, gctx_h, seg_h, out_from, w_h, grad_row_h, input_grad_h, out_to,
    lse, seg, packed, ctx, gctx, gp, w, grad_row, bounce, input_grad, qs_s, qt, dt, ka, va, dq_s, dk_s, dv_s, in_sem, out_sem,
):
    width, seq = ctx.shape
    groups = HEADS // GROUP
    group_rows = GROUP * HEAD_DIM
    loads = [
        [
            pltpu.make_async_copy(lse_h, lse, in_sem.at[groups, 0]),
            pltpu.make_async_copy(seg_h, seg, in_sem.at[groups, 1]),
        ]
    ]
    for load in loads[0]:
        load.start()
    for group in range(groups):
        pairs = [(gctx_h, gctx, 0), (ctx_h, ctx, 0)] + [(packed_h, packed, part) for part in range(3)]
        held = []
        for number, (source, target, part) in enumerate(pairs):
            rows = pl.ds(part * width + group * group_rows, group_rows)
            held.append(pltpu.make_async_copy(source.at[rows, :], target.at[rows, :], in_sem.at[group, number]))
            held[-1].start()
        loads.append(held)
    late = [
        pltpu.make_async_copy(source, target, out_sem.at[number])
        for number, (source, target) in enumerate(((out_from, bounce), (w_h, w), (grad_row_h, grad_row)))
    ]
    back = pltpu.make_async_copy(bounce, out_to, out_sem.at[3])

    for load in loads.pop(0):
        load.wait()
    starts = doc_starts(seg)
    row = lax.broadcasted_iota(jnp.int32, (AUG, seq), 0)
    same = row == seg[...]
    aug_q = jnp.where(same, 1.0, 0.0)
    aug_k = jnp.where(row < 4, jnp.where(same, 0.0, -1e30), jnp.where(row < 7, 1.0, 0.0)).astype(BF)
    aug_v = jnp.where(row < 3, 1.0, 0.0).astype(BF)

    def minus_rows(value, base):
        rest = -value
        rows = jnp.zeros((AUG, seq), F32)
        for step in range(3):
            piece = rest.astype(BF).astype(F32)
            rows = jnp.where(row == base + step, jnp.broadcast_to(piece, (AUG, seq)), rows)
            rest = rest - piece
        return rows

    def prepare(head, unused):
        rows = head_rows(0, head)
        scaled = packed[rows, :] * jnp.asarray(0.125, BF)
        qs_s[head] = scaled
        qt[head] = jnp.concatenate([scaled, (aug_q + minus_rows(lse[head], 4)).astype(BF)], axis=0).T
        ka[head, :HEAD_DIM, :] = packed[head_rows(1, head), :]
        ka[head, HEAD_DIM:, :] = aug_k
        va[head, :HEAD_DIM, :] = packed[head_rows(2, head), :]
        va[head, HEAD_DIM:, :] = aug_v
        grad = gctx[rows, :]
        inner = jnp.sum(grad.astype(F32) * ctx[rows, :].astype(F32), axis=0, keepdims=True)
        dt[head] = jnp.concatenate([grad, minus_rows(inner, 0).astype(BF)], axis=0).T
        dq_s[head] = jnp.zeros((HEAD_DIM, seq), F32)
        return 0

    for group in range(groups):
        for load in loads[group]:
            load.wait()
        lax.fori_loop(group * GROUP, (group + 1) * GROUP, prepare, 0, unroll=UNROLL)
    for load in late:
        load.start()

    def outer(i, unused):
        ks = pl.ds(pl.multiple_of(i * BLOCK_Q, BLOCK_Q), BLOCK_Q)
        for h in range(HEADS):
            dk_s[h] = jnp.zeros((HEAD_DIM, BLOCK_Q), F32)
            dv_s[h] = jnp.zeros((HEAD_DIM, BLOCK_Q), F32)

        def inner_block(j, unused):
            qs = pl.ds(pl.multiple_of(j * BLOCK_K, BLOCK_K), BLOCK_K)
            first, second = {}, {}
            lag = 4
            for t in range(HEADS + 2 * lag):
                if t < HEADS:
                    first[t] = (
                        dot_on(qt[t, qs, :], ka[t, :, ks], 1, 0),
                        dot_on(dt[t, qs, :], va[t, :, ks], 1, 0),
                    )
                h = t - lag
                if 0 <= h < HEADS:
                    logits, grad = first.pop(h)
                    prob = jnp.exp(logits)
                    second[h] = (prob.astype(BF), (prob * grad).astype(BF))
                h = t - 2 * lag
                if 0 <= h < HEADS:
                    prob, grad = second.pop(h)
                    dv_s[h] += dot_on(gctx[h * HEAD_DIM : (h + 1) * HEAD_DIM, qs], prob, 1, 0)
                    dk_s[h] += dot_on(qs_s[h, :, qs], grad, 1, 0)
                    dq_s[h, :, qs] += dot_on(packed[D + h * HEAD_DIM : D + (h + 1) * HEAD_DIM, ks], grad, 1, 1)
            return 0

        lax.fori_loop(*key_range(starts, seq, i), inner_block, 0)
        for h in range(HEADS):
            gp[D + h * HEAD_DIM : D + (h + 1) * HEAD_DIM, ks] = dk_s[h].astype(BF)
            gp[2 * D + h * HEAD_DIM : 2 * D + (h + 1) * HEAD_DIM, ks] = dv_s[h].astype(BF)
        return 0

    lax.fori_loop(0, seq // BLOCK_Q, outer, 0)

    def finish(head, unused):
        gp[head_rows(0, head), :] = (dq_s[head] * 0.125).astype(BF)
        return 0

    late[0].wait()
    back.start()
    lax.fori_loop(0, HEADS, finish, 0)
    late[1].wait()
    late[2].wait()
    outs = []

    def leave(step, part):
        rows = pl.ds(step * BLOCK_Q, BLOCK_Q)
        input_grad[rows, :] = (grad_row[rows, :] + part).astype(BF)
        outs.append(
            pltpu.make_async_copy(input_grad.at[rows, :], input_grad_h.at[rows, :], out_sem.at[4 + step])
        )
        outs[-1].start()

    staged(
        seq // BLOCK_Q,
        lambda step: dot_on(gp[:, pl.ds(step * BLOCK_Q, BLOCK_Q)], w[...], 0, 1),
        leave,
    )
    back.wait()
    for out in outs:
        out.wait()


def in_vmem():
    return pl.BlockSpec(memory_space=pltpu.VMEM)


def anywhere():
    return pl.BlockSpec(memory_space=pl.ANY)


def attend(x, w, seg):
    seq = x.shape[0]
    return pl.pallas_call(
        attend_kernel,
        in_specs=[anywhere() for unused in range(3)],
        out_specs=[anywhere() for unused in range(3)],
        out_shape=(
            jax.ShapeDtypeStruct((3 * D, seq), BF),
            jax.ShapeDtypeStruct((D, seq), BF),
            jax.ShapeDtypeStruct((HEADS, 1, seq), F32),
        ),
        scratch_shapes=[
            pltpu.VMEM((seq, D), BF),
            pltpu.VMEM((D, 3 * D), BF),
            pltpu.VMEM((1, seq), jnp.int32),
            pltpu.VMEM((3 * D, seq), BF),
            pltpu.VMEM((D, seq), BF),
            pltpu.VMEM((HEADS, 1, seq), F32),
            pltpu.VMEM((D, seq), BF),
            pltpu.VMEM((HEADS, HEAD_DIM + AUG, seq), BF),
            pltpu.VMEM((HEADS, seq, HEAD_DIM + AUG), BF),
            pltpu.VMEM((HEADS, HEAD_DIM + AUG, seq), BF),
            pltpu.VMEM((HEADS, 8, BLOCK_Q), F32),
            pltpu.VMEM((HEADS, HEAD_DIM + AUG, BLOCK_Q), F32),
            pltpu.SemaphoreType.DMA((2,)),
            pltpu.SemaphoreType.DMA((3,)),
            pltpu.SemaphoreType.DMA((3,)),
            pltpu.SemaphoreType.DMA((2, seq // BLOCK_Q)),
        ],
        name="attend",
        compiler_params=pltpu.CompilerParams(vmem_limit_bytes=60 << 20),
    )(x, w, seg)


def attend_back(packed, ctx, lse, gctx, seg, out, w, grad_row):
    seq = packed.shape[1]
    aug = HEAD_DIM + AUG
    return pl.pallas_call(
        attend_back_kernel,
        in_specs=[anywhere() for unused in range(8)],
        out_specs=[anywhere(), anywhere()],
        out_shape=(jax.ShapeDtypeStruct((seq, D), BF), jax.ShapeDtypeStruct((seq, D), BF)),
        scratch_shapes=[
            pltpu.VMEM((HEADS, 1, seq), F32),
            pltpu.VMEM((1, seq), jnp.int32),
            pltpu.VMEM((3 * D, seq), BF),
            pltpu.VMEM((D, seq), BF),
            pltpu.VMEM((D, seq), BF),
            pltpu.VMEM((3 * D, seq), BF),
            pltpu.VMEM((D, 3 * D), BF),
            pltpu.VMEM((seq, D), F32),
            pltpu.VMEM((seq, D), BF),
            pltpu.VMEM((seq, D), BF),
            pltpu.VMEM((HEADS, HEAD_DIM, seq), BF),
            pltpu.VMEM((HEADS, seq, aug), BF),
            pltpu.VMEM((HEADS, seq, aug), BF),
            pltpu.VMEM((HEADS, aug, seq), BF),
            pltpu.VMEM((HEADS, aug, seq), BF),
            pltpu.VMEM((HEADS, HEAD_DIM, seq), F32),
            pltpu.VMEM((HEADS, HEAD_DIM, BLOCK_Q), F32),
            pltpu.VMEM((HEADS, HEAD_DIM, BLOCK_Q), F32),
            pltpu.SemaphoreType.DMA((HEADS // GROUP + 1, 5)),
            pltpu.SemaphoreType.DMA((4 + seq // BLOCK_Q,)),
        ],
        name="attend_back",
        cost_estimate=pl.CostEstimate(flops=30_000_000_000, bytes_accessed=20_000_000, transcendentals=0),
        compiler_params=pltpu.CompilerParams(vmem_limit_bytes=62 << 20),
    )(packed, ctx, lse, gctx, seg, out, w, grad_row)


def pieces(value):
    high = value.astype(BF)
    return high, (value - high.astype(F32)).astype(BF)


def normalize(values):
    centre = values - jnp.mean(values, axis=-1, keepdims=True)
    factor = lax.rsqrt(jnp.mean(centre * centre, axis=-1, keepdims=True) + 1e-06)
    return centre * factor, factor


def norm_back(scaled, unit_vals, factor):
    return factor * (
        scaled
        - jnp.mean(scaled, axis=-1, keepdims=True)
        - unit_vals * jnp.mean(scaled * unit_vals, axis=-1, keepdims=True)
    )


def gelu_parts(values):
    rising = 0.5 * lax.erf(values * math.sqrt(0.5)) + 0.5
    low = values.astype(BF)
    bell = jnp.exp2(low * low * jnp.asarray(-0.5 * math.log2(math.e), BF))
    steep = low * jnp.asarray(1.0 / math.sqrt(2.0 * math.pi), BF)
    return (values * rising).astype(BF), rising.astype(BF) + steep * bell


def gelu_doubled(values):
    rising = lax.erf(values * math.sqrt(0.5)) + 1.0
    low = values.astype(BF)
    bell = jnp.exp2(low * low * jnp.asarray(-0.5 * math.log2(math.e), BF))
    steep = low * jnp.asarray(2.0 / math.sqrt(2.0 * math.pi), BF)
    return (values * rising).astype(BF), rising.astype(BF) + steep * bell


def fold_rows(values):
    rows, columns = values.shape
    return jnp.sum(values.reshape(rows // 8, 8, columns), axis=0)


def staged(count, product, finish, between=None):
    held = {}
    for step in range(count + 1):
        if between is not None and step == count // 2:
            between()
        if step < count:
            held[step] = product(step)
        if step >= 1:
            finish(step - 1, held.pop(step - 1))


MESH = pl.DeviceIdType.MESH
PLANE = 4
DEPTH = 4
OWN_ROWS = 24
SLABS = 2 * 2 * DEPTH + 2
PLANE_ROWS = 96
CORE_ROWS = 384


def place():
    wide, narrow = lax.axis_index("wide"), lax.axis_index("narrow")
    return wide // 2, lax.rem(wide, 2), narrow // 2, lax.rem(narrow, 2)


def device(z, x, y, core):
    return (z * 2 + x, y * 2 + core)


def plane_mate(step):
    z, x, y, core = place()
    return device(z, jnp.bitwise_xor(x, step // 2), jnp.bitwise_xor(y, step % 2), core)


def depth_mate(step):
    z, x, y, core = place()
    return device(lax.rem(z + step, DEPTH), x, y, core)


def core_mate():
    z, x, y, core = place()
    return device(z, x, y, 1 - core)


def remote(source, target, sems, slot, mate):
    return pltpu.make_async_remote_copy(
        src_ref=source,
        dst_ref=target,
        send_sem=sems.at[0, slot],
        recv_sem=sems.at[1, slot],
        device_id=mate,
        device_id_type=MESH,
    )


def greet(mates):
    barrier = pltpu.get_barrier_semaphore()
    for mate in mates:
        pl.semaphore_signal(barrier, inc=1, device_id=mate, device_id_type=MESH)
    return lambda: pl.semaphore_wait(barrier, len(mates))


class Scatter:
    def __init__(self, which, square, kept, send, near, plane, small_send, small, gathered, sems):
        self.which, self.square, self.kept = which, square, kept
        self.send, self.near, self.plane = send, near, plane
        self.small_send, self.small, self.gathered, self.sems = small_send, small, gathered, sems
        z, x, y, core = place()
        self.z, self.spot, self.core = z, x * 2 + y, core
        self.copies = []

    def rows(self, start, count):
        return pl.ds(pl.multiple_of(start, 8), count)

    def finish(self):
        for copy in self.copies:
            copy.wait()
        self.copies = []

    def go(self, source, target, slot, mate):
        copy = remote(source, target, self.sems, self.which * 16 + slot, mate)
        copy.start()
        self.copies.append(copy)

    def to_core(self):
        self.go(self.send.at[self.which], self.near.at[self.which], 0, core_mate())

    def to_plane(self):
        self.finish()
        for q in range(PLANE):
            rows = pl.ds(q * PLANE_ROWS, PLANE_ROWS)
            total = self.square[rows, :] + self.near[self.which, q].astype(F32)
            self.square[rows, :] = total
            self.send[self.which, q] = total.astype(BF)
        self.kept[self.which] = self.square[self.rows(self.spot * PLANE_ROWS, PLANE_ROWS), :]
        for step in range(1, PLANE):
            spot = jnp.bitwise_xor(self.spot, step)
            self.go(self.send.at[self.which, spot], self.plane.at[self.which, step - 1], step, plane_mate(step))

    def to_depth(self):
        self.finish()
        total = self.kept[self.which]
        for step in range(1, PLANE):
            total = total + self.plane[self.which, step - 1].astype(F32)
        self.kept[self.which] = total
        for k in range(DEPTH):
            self.small_send[self.which, k] = total[k * OWN_ROWS : (k + 1) * OWN_ROWS, :].astype(BF)
        for step in range(1, DEPTH):
            spot = lax.rem(self.z + step, DEPTH)
            self.go(
                self.small_send.at[self.which, spot],
                self.small.at[self.which, step - 1],
                PLANE - 1 + step,
                depth_mate(step),
            )

    def share(self, last=None):
        self.finish()
        total = self.kept[self.which, self.rows(self.z * OWN_ROWS, OWN_ROWS), :]
        for step in range(1, DEPTH):
            total = total + self.small[self.which, step - 1].astype(F32)
        if last is not None:
            high, rest = pieces(total)
            total = dot_on(high, last, 1, 0) + dot_on(rest, last, 1, 0)
        mine = self.gathered.at[self.slab(self.z)]
        mine[...] = total.astype(BF)
        for step in range(1, DEPTH):
            self.go(mine, mine, PLANE + DEPTH - 2 + step, depth_mate(step))

    def slab(self, z):
        return (self.core * 2 + self.which) * DEPTH + z

    def pair(self):
        arriving, self.copies = self.copies, []
        for step in range(DEPTH):
            if step:
                arriving[step - 1].wait()
            spot = lax.rem(self.z - step + DEPTH, DEPTH)
            chunk = self.gathered.at[self.slab(spot)]
            self.go(chunk, chunk, PLANE + 2 * DEPTH - 2 + step, core_mate())


ROWS_AT_ONCE = 256
HIDDEN_AT_ONCE = 512
HIDDEN_ROWS = 512


def middle_kernel(
    joined, x_h, g_h, ctx_h, wo_h, win_h, wout_h, down_h, up_h, wq_h, wk_h, wv_h,
    bias_h, gain_one_h, shift_one_h, gain_two_h, shift_two_h, mask_h,
    out_h, gr_h, gctx_h, v_h, gg_h, sums_h,
    x, g, ctx, wo, win, wout, bank, wq, wk, wv,
    unit_one, unit_two, bottle, guide, total, act, slope, low, factor, mix, score_grads,
    v_s, gg_s, sums_part, vectors, mask, sums_out, in_sem, vector_sem, out_sem, *links,
):
    seq, width = x.shape
    blocks = seq // ROWS_AT_ONCE
    mix_scale = 1.0 / math.sqrt(D)
    vector_loads = [
        pltpu.make_async_copy(source, vectors.at[number, pl.ds(0, width)], vector_sem.at[number])
        for number, source in enumerate((gain_one_h, shift_one_h, gain_two_h, shift_two_h))
    ] + [
        pltpu.make_async_copy(
            bias_h.at[pl.ds(number * 1024, 1024)], vectors.at[4 + number], vector_sem.at[4 + number]
        )
        for number in range(win.shape[1] // 1024)
    ] + [pltpu.make_async_copy(mask_h, mask, vector_sem.at[4 + win.shape[1] // 1024])]
    loads = {}
    names = ("down", "up", "ctx", "wo", "x", "win", "wout", "wq", "wk", "g", "wv")
    sources = (down_h, up_h, ctx_h, wo_h, x_h, win_h, wout_h, wq_h, wk_h, g_h, wv_h)
    targets = (bank.at[0], bank.at[1], ctx, wo, x, win, wout, wq, wk, g, wv)
    gain_one, shift_one, gain_two, shift_two = (vectors.at[number : number + 1, :width] for number in range(4))
    if joined:
        (
            kept, send, near, plane, small_send, small, gathered,
            sums_near, sums_depth, sums_mid, link_sems, bank_sems, sums_sems,
        ) = links
        arrived = greet(
            [core_mate()]
            + [plane_mate(step) for step in range(1, PLANE)]
            + [depth_mate(step) for step in range(1, DEPTH)]
        )
        spot = lax.axis_index("narrow")
        shard = down_h.shape[0]

        own_rows = pl.ds(pl.multiple_of(spot * shard, 16), shard)
        targets = (bank.at[0, own_rows, :], bank.at[1, own_rows, :]) + targets[2:]
    for number, name in enumerate(names):
        loads[name] = pltpu.make_async_copy(sources[number], targets[number], in_sem.at[number])
    for name in names[:5]:
        loads[name].start()
    for load in vector_loads:
        load.start()
    for name in names[5:]:
        loads[name].start()

    def rows_of(step):
        return pl.ds(step * ROWS_AT_ONCE, ROWS_AT_ONCE)

    t_one, t_two, t_three, t_four = (pl.ds(k * width, width) for k in range(4))
    down, up = 0, 1
    column = lax.broadcasted_iota(jnp.int32, (ADAPTERS, width), 1)
    owner = lax.rem(column, ADAPTERS)
    chosen = jnp.where(
        owner == lax.broadcasted_iota(jnp.int32, (ADAPTERS, width), 0), 1.0, 0.0
    ).astype(BF)

    chosen_twice = jnp.concatenate([chosen, chosen], axis=0)

    def per_adapter(values):
        high, rest = pieces(values)
        return dot_on(chosen, high, 1, 1) + dot_on(chosen, rest, 1, 1)

    def per_unit(values):
        return dot_on(jnp.concatenate(pieces(values), axis=0), chosen_twice, 0, 0)

    loads["ctx"].wait()
    loads["wo"].wait()

    def finish_first(step, part):
        rows = rows_of(step)
        if step == 0:
            loads["x"].wait()
            for load in vector_loads:
                load.wait()
        unit, scale = normalize(x[rows, :].astype(F32) + part)
        unit_one[rows, :] = unit
        factor[rows, 0:1] = scale
        low[rows, :] = (unit * gain_one[...] + shift_one[...]).astype(BF)

    if joined:
        arrived()
        loads["down"].wait()
        loads["up"].wait()

        def bank_part(which, index, slot, mate):
            rows = bank.at[which, pl.ds(pl.multiple_of(index * shard, 16), shard), :]
            return remote(rows, rows, bank_sems, slot, mate)

        far_copies = [bank_part(which, spot, which, plane_mate(1)) for which in (down, up)]
        near_copies = [bank_part(which, spot, 2 + which, core_mate()) for which in (down, up)]
        for copy in far_copies + near_copies:
            copy.start()

        def forward(which):
            far_copies[which].wait()
            far_copies[which] = bank_part(which, jnp.bitwise_xor(spot, 2), 4 + which, core_mate())
            far_copies[which].start()

        def whole_bank(which):
            far_copies[which].wait()
            near_copies[which].wait()
    staged(blocks, lambda step: dot_on(ctx[:, rows_of(step)], wo[...], 0, 0), finish_first)

    loads["win"].wait()

    def hidden(chunk, unused):
        columns = pl.ds(pl.multiple_of(chunk * HIDDEN_AT_ONCE, HIDDEN_AT_ONCE), HIDDEN_AT_ONCE)
        per_row = 1024 // HIDDEN_AT_ONCE
        lanes = pl.ds(pl.multiple_of(lax.rem(chunk, per_row) * HIDDEN_AT_ONCE, HIDDEN_AT_ONCE), HIDDEN_AT_ONCE)
        bias = vectors[pl.ds(4 + chunk // per_row, 1), lanes]

        def rows_in(step):
            return pl.ds(step * HIDDEN_ROWS, HIDDEN_ROWS)

        def finish(step, part):
            rows = rows_in(step)
            value, rising = gelu_doubled(part + bias)
            act[rows, columns] = value
            slope[rows, columns] = rising

        staged(seq // HIDDEN_ROWS, lambda step: dot_on(low[rows_in(step), :], win[:, columns], 1, 0), finish)
        return 0

    lax.fori_loop(0, win.shape[1] // HIDDEN_AT_ONCE, hidden, 0)
    loads["wout"].wait()
    if joined:
        forward(down)

    def second(half, unused):
        def rows_in(step):
            start = half * (seq // 2) + step * ROWS_AT_ONCE
            return pl.ds(pl.multiple_of(start, ROWS_AT_ONCE), ROWS_AT_ONCE)

        def finish(step, part):
            rows = rows_in(step)
            unit, scale = normalize(unit_one[rows, :] * gain_one[...] + shift_one[...] + 0.5 * part)
            unit_two[rows, :] = unit
            factor[rows, 1:2] = scale
            low[rows, :] = (unit * gain_two[...] + shift_two[...]).astype(BF)

        staged(blocks // 2, lambda step: dot_on(act[rows_in(step), :], wout[...], 1, 0), finish)
        return 0

    lax.fori_loop(0, 2, second, 0)

    def h_two(rows):
        return unit_two[rows, :] * gain_two[...] + shift_two[...]

    def keep(target, place, size):
        def finish(step, part):
            target[pl.ds(step * size, size), place] = part.astype(BF)

        return finish

    everything = pl.ds(0, width)
    if joined:
        forward(up)
        whole_bank(down)
    else:
        loads["down"].wait()
        loads["up"].wait()

    def finish_down(step, part):
        rows = rows_of(step)
        bottle[rows, :] = part * (0.5 * lax.erf(part * math.sqrt(0.5)) + 0.5)
        act[rows, t_four] = gelu_parts(part)[1]

    staged(blocks, lambda step: dot_on(low[rows_of(step), :], bank[down], 1, 1), finish_down)
    if joined:
        whole_bank(up)
    loads["wk"].wait()
    third = width // 3
    staged(3, lambda step: dot_on(bank[up, pl.ds(step * third, third), :], wk[...], 1, 0), keep(act, t_one, third))
    loads["wq"].wait()
    through = act.at[:width, t_one]
    staged(3, lambda step: dot_on(wq[pl.ds(step * third, third), :], through[...], 1, 1), keep(wk, everything, third))

    def finish_guide(step, part):
        rows = rows_of(step)
        guide[rows, :] = part
        mix[:, rows] = per_adapter(bottle[rows, :] * part)

    staged(blocks, lambda step: dot_on(low[rows_of(step), :], wk[...], 1, 0), finish_guide)
    scores = mix[...] * mix_scale
    shifted = scores - jnp.max(scores, axis=0, keepdims=True)
    exponents = jnp.exp(shifted)
    total_exponent = jnp.sum(exponents, axis=0, keepdims=True)
    weights = exponents / total_exponent
    entropies = -jnp.sum(weights * (shifted - jnp.log(total_exponent)), axis=0, keepdims=True)
    mix[...] = weights

    def finish_mix(step, part):
        rows = rows_of(step)
        act[rows, t_one] = (part * bottle[rows, :]).astype(BF)

    staged(blocks, lambda step: per_unit(mix[:, rows_of(step)]), finish_mix)
    real = mask[...].astype(F32)
    ent = jnp.sum(entropies * real, axis=1, keepdims=True)
    lane = lax.broadcasted_iota(jnp.int32, (1, 1024), 1)
    sums_out[7:8, :] = jnp.where(lane < 128, ent, jnp.sum(real, axis=1, keepdims=True))
    sums_out[3:7, width:] = jnp.zeros((4, 1024 - width), F32)

    def finish_update(step, part):
        rows = rows_of(step)
        x[rows, :] = (h_two(rows) + part).astype(BF)

    staged(blocks, lambda step: dot_on(act[rows_of(step), t_one], bank[up], 1, 0), finish_update)

    loads["g"].wait()

    def over_tokens(left, right, target):
        def product(step):
            return dot_on(left(pl.ds(step * third, third)), right, 0, 0)

        def finish(step, part):
            target[pl.ds(step * third, third), :] = part

        staged(3, product, finish)

    def halves(left, base, right, target, which):
        core = place()[3]

        def product(step):
            start = base + (core if step else 1 - core) * CORE_ROWS
            return dot_on(left[:, pl.ds(pl.multiple_of(start, 128), CORE_ROWS)], right, 0, 0)

        def finish(step, part):
            if step:
                target[...] = part
            else:
                for q in range(PLANE):
                    send[which, q] = part[q * PLANE_ROWS : (q + 1) * PLANE_ROWS, :].astype(BF)

        finish(0, product(0))
        (value_sum, joint_sum)[which].to_core()
        finish(1, product(1))

    if joined:
        value_sum, joint_sum = (
            Scatter(k, v_s, kept, send, near, plane, small_send, small, gathered, link_sems) for k in range(2)
        )
        halves(x, 0, g[...], v_s, 0)
    else:
        over_tokens(lambda cols: x[:, cols], g[...], v_s)
    if not joined:
        v_out = pltpu.make_async_copy(v_s, v_h, out_sem.at[0])
        v_out.start()

    loads["wv"].wait()

    def finish_blend(step, part):
        rows = rows_of(step)
        total[rows, :] = g[rows, :].astype(F32) + part
        act[rows, t_one] = part.astype(BF)

    staged(blocks, lambda step: dot_on(g[rows_of(step), :], wv[...], 1, 1), finish_blend)

    def finish_mixed(step, part):
        rows = rows_of(step)
        act[rows, t_one] = part.astype(BF)
        score_grads[:, rows] = per_adapter(part * bottle[rows, :])

    staged(blocks, lambda step: dot_on(act[rows_of(step), t_one], bank[up], 1, 1), finish_mixed, value_sum.to_plane if joined else None)
    weights = mix[...]
    grad_weights = score_grads[...]
    inner = jnp.sum(grad_weights * weights, axis=0, keepdims=True)
    score_grads[...] = weights * (grad_weights - inner) * mix_scale

    def finish_units(step, part):
        rows = rows_of(step)
        mixed, score_term = part
        grad_bottle = act[rows, t_one].astype(F32) * mixed + score_term * guide[rows, :]
        act[rows, t_three] = (grad_bottle * act[rows, t_four].astype(F32)).astype(BF)
        act[rows, t_one] = (score_term * bottle[rows, :]).astype(BF)

    staged(
        blocks,
        lambda step: (per_unit(mix[:, rows_of(step)]), per_unit(score_grads[:, rows_of(step)])),
        finish_units,
    )
    if joined:
        halves(low, 0, act[:, t_one], v_s, 1)
    else:
        over_tokens(lambda cols: low[:, cols], act[:, t_one], gg_s)
    if not joined:
        gg_out = pltpu.make_async_copy(gg_s, gg_h, out_sem.at[2])
        gg_out.start()
    partial = [jnp.zeros((8, width), F32) for unused in range(4)]

    def finish_two(step, part):
        rows = rows_of(step)
        grad = total[rows, :] + part
        unit = unit_two[rows, :]
        partial[0] = partial[0] + fold_rows(grad * unit)
        partial[1] = partial[1] + fold_rows(grad)
        back = norm_back(grad * gain_two[...], unit, factor[rows, 1:2])
        total[rows, :] = back
        low[rows, :] = (0.5 * back).astype(BF)

    staged(
        blocks,
        lambda step: dot_on(act[rows_of(step), t_three], bank[down], 1, 0)
        + dot_on(act[rows_of(step), t_one], wk[...], 1, 1),
        finish_two,
        joint_sum.to_plane if joined else None,
    )

    if joined:
        value_sum.to_depth()

    def hidden_back(chunk, unused):
        columns = pl.ds(pl.multiple_of(chunk * HIDDEN_AT_ONCE, HIDDEN_AT_ONCE), HIDDEN_AT_ONCE)
        held = [jnp.zeros((8, HIDDEN_AT_ONCE), F32)]

        def rows_in(step):
            return pl.ds(step * HIDDEN_ROWS, HIDDEN_ROWS)

        def finish(step, part):
            rows = rows_in(step)
            grad = (part * slope[rows, columns].astype(F32)).astype(BF)
            act[rows, columns] = grad
            held[0] = held[0] + fold_rows(grad.astype(F32))

        staged(seq // HIDDEN_ROWS, lambda step: dot_on(low[rows_in(step), :], wout[columns, :], 1, 1), finish)
        sums_part[chunk] = held[0]
        return 0

    lax.fori_loop(0, win.shape[1] // HIDDEN_AT_ONCE, hidden_back, 0)
    for number in range(win.shape[1] // HIDDEN_AT_ONCE):
        at, lanes = divmod(number * HIDDEN_AT_ONCE, 1024)
        sums_out[at : at + 1, pl.ds(lanes, HIDDEN_AT_ONCE)] = jnp.sum(sums_part[number], axis=0, keepdims=True)
    sums_out[5:6, :width] = jnp.sum(partial[0], axis=0, keepdims=True)
    sums_out[6:7, :width] = jnp.sum(partial[1], axis=0, keepdims=True)
    if joined:
        value_sum.share()
        joint_sum.to_depth()

    def first_back(half, carried):
        def rows_in(step):
            start = half * (seq // 2) + step * ROWS_AT_ONCE
            return pl.ds(pl.multiple_of(start, ROWS_AT_ONCE), ROWS_AT_ONCE)

        held = list(carried)

        def finish(step, part):
            rows = rows_in(step)
            grad = total[rows, :] + part
            unit = unit_one[rows, :]
            held[0] = held[0] + fold_rows(grad * unit)
            held[1] = held[1] + fold_rows(grad)
            back = norm_back(grad * gain_one[...], unit, factor[rows, 0:1])
            total[rows, :] = back
            low[rows, :] = back.astype(BF)

        staged(blocks // 2, lambda step: dot_on(act[rows_in(step), :], win[...], 1, 1), finish)
        return tuple(held)

    zero = jnp.zeros((8, width), F32)
    gain_sum, shift_sum = lax.fori_loop(0, 2, first_back, (zero, zero))
    sums_out[3:4, :width] = jnp.sum(gain_sum, axis=0, keepdims=True)
    sums_out[4:5, :width] = jnp.sum(shift_sum, axis=0, keepdims=True)
    if joined:
        near_copy = remote(sums_out, sums_near, sums_sems, 0, core_mate())
        near_copy.start()
        value_sum.pair()
        joint_sum.share(bank[up])
    gr_copy = pltpu.make_async_copy(total, gr_h, out_sem.at[3])
    gr_copy.start()

    def finish_ctx(step, part):
        ctx[pl.ds(step * third, third), :] = part.astype(BF)

    staged(3, lambda step: dot_on(wo[pl.ds(step * third, third), :], low[...], 1, 1), finish_ctx)
    gctx_copy = pltpu.make_async_copy(ctx, gctx_h, out_sem.at[4])
    gctx_copy.start()
    if joined:
        near_copy.wait()
        sums_mid[...] = sums_out[...] + sums_near[...]
        depth_copies = [
            remote(sums_mid, sums_depth.at[step - 1], sums_sems, step, depth_mate(step)) for step in range(1, DEPTH)
        ]
        for copy in depth_copies:
            copy.start()
        value_sum.finish()

    def finish_out(step, part):
        rows = rows_of(step)
        x[rows, :] = (h_two(rows) + part).astype(BF)

    staged(blocks, lambda step: dot_on(x[rows_of(step), :], wv[...], 1, 0), finish_out)
    out_copy = pltpu.make_async_copy(x, out_h, out_sem.at[1])
    out_copy.start()
    if joined:
        joint_sum.pair()
        for copy in depth_copies:
            copy.wait()
        rest = sums_mid[...] + sums_depth[0] + sums_depth[1] + sums_depth[2]
        parts = []
        for unused in range(3):
            parts.append(rest.astype(BF).astype(F32))
            rest = rest - parts[-1]
        parts = jnp.concatenate(parts, axis=0).astype(BF)
        gathered[SLABS - 2] = parts[:, :width]
        gathered[SLABS - 1] = jnp.zeros((OWN_ROWS, width), BF)
        gathered[SLABS - 1, :, : 1024 - width] = parts[:, width:]
        joint_sum.finish()
        v_out = pltpu.make_async_copy(gathered, v_h, out_sem.at[0])
        v_out.start()
    else:
        sums_copy = pltpu.make_async_copy(sums_out, sums_h, out_sem.at[5])
        sums_copy.start()
        gg_out.wait()
        sums_copy.wait()
    v_out.wait()
    out_copy.wait()
    gr_copy.wait()
    gctx_copy.wait()


def middle(joined, x, g, ctx, wo, win, wout, down, up, wq, wk, wv, bias, gain_one, shift_one, gain_two, shift_two, mask):
    seq, width = x.shape
    hidden = win.shape[1]
    token_low = pltpu.VMEM((seq, width), BF)
    token_wide = pltpu.VMEM((seq, width), F32)
    square = pltpu.VMEM((width, width), BF)
    sum_square = pltpu.VMEM((CORE_ROWS if joined else width, width), F32)
    links = [
        pltpu.VMEM((2, PLANE_ROWS, width), F32),
        pltpu.VMEM((2, PLANE, PLANE_ROWS, width), BF),
        pltpu.VMEM((2, PLANE, PLANE_ROWS, width), BF),
        pltpu.VMEM((2, PLANE - 1, PLANE_ROWS, width), BF),
        pltpu.VMEM((2, DEPTH, OWN_ROWS, width), BF),
        pltpu.VMEM((2, DEPTH - 1, OWN_ROWS, width), BF),
        pltpu.VMEM((SLABS, OWN_ROWS, width), BF),
        pltpu.VMEM((8, 1024), F32),
        pltpu.VMEM((DEPTH - 1, 8, 1024), F32),
        pltpu.VMEM((8, 1024), F32),
        pltpu.SemaphoreType.DMA((2, 32)),
        pltpu.SemaphoreType.DMA((2, 6)),
        pltpu.SemaphoreType.DMA((2, DEPTH)),
    ]
    return pl.pallas_call(
        functools.partial(middle_kernel, joined),
        in_specs=[anywhere() for unused in range(17)],
        out_specs=[anywhere() for unused in range(6)],
        out_shape=(
            jax.ShapeDtypeStruct((seq, width), BF),
            jax.ShapeDtypeStruct((seq, width), F32),
            jax.ShapeDtypeStruct((width, seq), BF),
            jax.ShapeDtypeStruct((SLABS, OWN_ROWS, width), BF)
            if joined
            else jax.ShapeDtypeStruct((width, width), F32),
            jax.ShapeDtypeStruct((8, 128) if joined else (width, width), F32),
            jax.ShapeDtypeStruct((8, 128 if joined else 1024), F32),
        ),
        scratch_shapes=[
            token_low, token_low, pltpu.VMEM((width, seq), BF),
            square, pltpu.VMEM((width, hidden), BF), pltpu.VMEM((hidden, width), BF),
            pltpu.VMEM((2, width, width), BF), square, square, square,
            token_wide, token_wide, token_wide, token_wide, token_wide,
            pltpu.VMEM((seq, hidden), BF), pltpu.VMEM((seq, hidden), BF), token_low,
            pltpu.VMEM((seq, 2), F32), pltpu.VMEM((ADAPTERS, seq), F32), pltpu.VMEM((ADAPTERS, seq), F32),
            sum_square, pltpu.VMEM((8, 128) if joined else (width, width), F32),
            pltpu.VMEM((hidden // HIDDEN_AT_ONCE, 8, HIDDEN_AT_ONCE), F32),
            pltpu.VMEM((8, 1024), F32), pltpu.VMEM((1, seq), jnp.int32), pltpu.VMEM((8, 1024), F32),
            pltpu.SemaphoreType.DMA((11,)),
            pltpu.SemaphoreType.DMA((8,)), pltpu.SemaphoreType.DMA((6,)),
        ]
        + (links if joined else []),
        name="middle",
        compiler_params=pltpu.CompilerParams(
            vmem_limit_bytes=VMEM_BYTES, **(dict(collective_id=0, has_side_effects=True) if joined else {})
        ),
    )(x, g, ctx, wo, win, wout, down, up, wq, wk, wv, bias, gain_one, shift_one, gain_two, shift_two, mask)

def products_kernel(
    mine_h, first_h, second_h, third_h, wk_h, wq_h,
    value_h, query_h, key_h, bias_h, gain_one_h, shift_one_h, gain_two_h, shift_two_h, entropy,
    sums, held, wk, wq, square, joint, low, in_sem, out_sem,
):
    width = wk.shape[0]
    z, x, y, core = place()
    loads = [
        pltpu.make_async_copy(source, target, in_sem.at[number])
        for number, (source, target) in enumerate(
            [(source, held.at[step]) for step, source in enumerate((mine_h, first_h, second_h, third_h))]
            + [(wk_h, wk), (wq_h, wq)]
        )
    ]
    for load in loads:
        load.start()
    outs = []

    def leave(source, target):
        outs.append(pltpu.make_async_copy(source, target, out_sem.at[len(outs)]))
        outs[-1].start()

    for load in loads[:PLANE]:
        load.wait()

    def unpack(which, target):
        for step in range(PLANE):
            base = jnp.bitwise_xor(x * 2 + y, step) * PLANE_ROWS
            for side in range(2):
                for depth in range(DEPTH):
                    start = pl.multiple_of(base + side * CORE_ROWS + depth * OWN_ROWS, 8)
                    slab = (side * 2 + which) * DEPTH + depth
                    target[pl.ds(start, OWN_ROWS), :] = held[step, slab].astype(F32)

    unpack(0, square.at[0])
    leave(square.at[0], value_h)
    totals = [
        sum(held[step, SLABS - 2 + part].astype(F32) for step in range(PLANE)).reshape(3, 8, width)
        for part in range(2)
    ]
    wide_total, rest_total = ((total[0] + total[1]) + total[2] for total in totals)
    sums[:, :width] = wide_total
    sums[:, width:] = rest_total[:, : 1024 - width]
    for number in range(bias_h.shape[0] // 1024):
        leave(sums.at[number], bias_h.at[pl.ds(number * 1024, 1024)])
    for number, target in enumerate((gain_one_h, shift_one_h, gain_two_h, shift_two_h)):
        leave(sums.at[3 + number, pl.ds(0, width)], target)
    entropy[...] = sums[7:8, 0:1] / sums[7:8, 128:129]
    unpack(1, joint)
    low[...] = joint[...].astype(BF)
    loads[PLANE].wait()
    half = width // 2
    for step in range(2):
        rows = pl.ds(step * half, half)
        square[1, rows, :] = dot_on(low[rows, :], wk[...], 1, 0)
        leave(square.at[1, rows, :], query_h.at[rows, :])
    loads[PLANE + 1].wait()
    for step in range(2):
        rows = pl.ds(step * half, half)
        joint[rows, :] = dot_on(low[:, rows], wq[...], 0, 0)
        leave(joint.at[rows, :], key_h.at[rows, :])
    for out in outs:
        out.wait()


def products(held, wk, wq, hidden):
    width = wk.shape[0]
    square = jax.ShapeDtypeStruct((width, width), F32)
    vector = jax.ShapeDtypeStruct((width,), F32)
    return pl.pallas_call(
        products_kernel,
        in_specs=[anywhere() for unused in range(6)],
        out_specs=[anywhere() for unused in range(8)] + [in_vmem()],
        out_shape=(
            square, square, square, jax.ShapeDtypeStruct((hidden,), F32), vector, vector, vector, vector,
            jax.ShapeDtypeStruct((1, 1), F32),
        ),
        scratch_shapes=[
            pltpu.VMEM((8, 1024), F32),
            pltpu.VMEM((PLANE,) + held[0].shape, BF),
            pltpu.VMEM((width, width), BF),
            pltpu.VMEM((width, width), BF),
            pltpu.VMEM((2, width, width), F32),
            pltpu.VMEM((width, width), F32),
            pltpu.VMEM((width, width), BF),
            pltpu.SemaphoreType.DMA((PLANE + 2,)),
            pltpu.SemaphoreType.DMA((12,)),
        ],
        name="products",
        compiler_params=pltpu.CompilerParams(vmem_limit_bytes=VMEM_BYTES),
    )(*held, wk, wq)


def plane_order(step):
    order = []
    for index in range(32):
        wide, narrow = index // 4, index % 4
        wide, narrow = wide ^ (step // 2), narrow ^ (2 * (step % 2))
        order.append((index, wide * 4 + narrow))
    return order

def per_device(
    joined,
    block_input, segments, real_mask, qkv_weight, attn_out_weight, ffn_in_weight, ffn_bias, ffn_out_weight,
    first_gain, first_shift, second_gain, second_shift, adapter_down, adapter_up,
    joining_query, joining_key, joining_value, cotangent,
):
    row_count, seq_len, width = block_input.shape
    tokens = block_input.reshape(seq_len, width)
    units = adapter_down.shape[2]
    down = jnp.transpose(adapter_down, (2, 1, 0)).reshape(ADAPTERS * units, width)
    up = jnp.transpose(adapter_up, (1, 0, 2)).reshape(ADAPTERS * units, width)
    if not joined:
        down, up = (lax.all_gather(part, "narrow", axis=0, tiled=True) for part in (down, up))
    seg_row = segments.reshape(1, seq_len)
    packed, context, log_total = attend(tokens, qkv_weight, seg_row)
    out, grad_row, grad_context, value_sum, joint_sum, sums = middle(
        joined,
        tokens, cotangent.reshape(seq_len, width), context, attn_out_weight, ffn_in_weight, ffn_out_weight,
        down, up, joining_query, joining_key, joining_value, ffn_bias, first_gain, first_shift,
        second_gain, second_shift, real_mask.reshape(1, seq_len),
    )
    input_grad, out = attend_back(
        packed, context, log_total, grad_context, seg_row, out, qkv_weight, grad_row
    )
    if joined:
        held = [value_sum] + [
            lax.ppermute(value_sum, ("wide", "narrow"), plane_order(step)) for step in range(1, PLANE)
        ]
        value_grad, query_grad, key_grad, bias_grad, gain_one, shift_one, gain_two, shift_two, entropy = products(
            held, joining_key, joining_query, ffn_bias.shape[0]
        )
    else:
        value_grad, joint_sum, sums = lax.psum((value_sum, joint_sum, sums), ("wide", "narrow"))
        high, rest = pieces(joint_sum)
        joint_sum = (dot_on(high, up, 1, 0) + dot_on(rest, up, 1, 0)).astype(BF)
        query_grad = dot_on(joint_sum, joining_key, 1, 0)
        key_grad = dot_on(joint_sum, joining_query, 0, 0)
        bias_grad = sums[:3].reshape(ffn_bias.shape[0])
        gain_one, shift_one, gain_two, shift_two = (sums[number, :width] for number in range(3, 7))
        entropy = sums[7, 0] / sums[7, 128]
    return (
        out.reshape(row_count, seq_len, width),
        input_grad.reshape(row_count, seq_len, width),
        query_grad,
        key_grad,
        value_grad,
        bias_grad,
        gain_one,
        shift_one,
        gain_two,
        shift_two,
        entropy.reshape(()),
    )


def solution(mesh):
    placed = (
        P(("wide", "narrow"), None, None),
        P(("wide", "narrow"), None),
        P(("wide", "narrow"), None),
        P(),
        P(),
        P(),
        P(),
        P(),
        P(),
        P(),
        P(),
        P(),
        P(None, None, "narrow"),
        P(None, "narrow", None),
        P(),
        P(),
        P(),
        P(("wide", "narrow"), None, None),
    )
    joined = mesh.shape["wide"] == 8 and mesh.shape["narrow"] == 4
    return jax.shard_map(
        functools.partial(per_device, joined),
        mesh=mesh,
        in_specs=placed,
        out_specs=(
            P(("wide", "narrow"), None, None),
            P(("wide", "narrow"), None, None),
            P(),
            P(),
            P(),
            P(),
            P(),
            P(),
            P(),
            P(),
            P(),
        ),
        check_vma=False,
    )
```

```python
import math

import jax
import jax.numpy as jnp
import functools

from jax import lax
from jax.experimental import pallas as pl
from jax.experimental.pallas import tpu as pltpu
from jax.sharding import PartitionSpec as P

D = 768
HEADS = 12
HEAD_DIM = 64
ADAPTERS = 16
BOTTLE = 48

AUG = 16
BF = jnp.bfloat16
F32 = jnp.float32
BLOCK_Q = 256
BLOCK_K = 128
UNROLL = 4
VMEM_BYTES = 64 << 20


def dot_on(left_op, right_op, left_dim, right_dim):
    return lax.dot_general(
        left_op,
        right_op,
        (((left_dim,), (right_dim,)), ((), ())),
        preferred_element_type=F32,
    )


def head_rows(part, head):
    return pl.ds(pl.multiple_of(part * D + head * HEAD_DIM, HEAD_DIM), HEAD_DIM)


def doc_starts(seg):
    return [jnp.sum((seg[...] < doc).astype(jnp.int32)) for doc in range(1, 4)]


def key_range(starts, seq, i):
    low, high = jnp.int32(0), jnp.int32(seq)
    for start in starts:
        low = jnp.where(start <= i * BLOCK_K, jnp.maximum(low, start), low)
        high = jnp.where(start >= (i + 1) * BLOCK_K, jnp.minimum(high, start), high)
    return low // BLOCK_K, (high + BLOCK_K - 1) // BLOCK_K


def over_range(starts, seq, i, body):
    low_one, high_one = key_range(starts, seq, 2 * i)
    low_two, high_two = key_range(starts, seq, 2 * i + 1)
    lax.fori_loop(low_one, jnp.minimum(low_two, high_one), body(0, BLOCK_K), 0)
    lax.fori_loop(low_two, high_one, body(0, BLOCK_Q), 0)
    lax.fori_loop(jnp.maximum(low_two, high_one), high_two, body(BLOCK_K, BLOCK_K), 0)


def attend_kernel(
    x_h, w_h, seg_h, packed_h, ctx_h, lse_h,
    x, w, seg, packed, ctx, lse, xt, qa, kt, va, m_s, o_s, in_sem, w_sem, packed_sem, ctx_sem,
):
    seq, width = x.shape

    def w_copy(part):
        columns = pl.ds(pl.multiple_of(part * width, width), width)
        return pltpu.make_async_copy(w_h.at[:, columns], w.at[:, columns], w_sem.at[part])

    def packed_copy(part):
        rows = pl.ds(pl.multiple_of(part * width, width), width)
        return pltpu.make_async_copy(packed.at[rows, :], packed_h.at[rows, :], packed_sem.at[part])

    def ctx_copies(i):
        columns = pl.ds(pl.multiple_of(i * BLOCK_Q, BLOCK_Q), BLOCK_Q)
        return (
            pltpu.make_async_copy(ctx.at[:, columns], ctx_h.at[:, columns], ctx_sem.at[0, i]),
            pltpu.make_async_copy(lse.at[:, :, columns], lse_h.at[:, :, columns], ctx_sem.at[1, i]),
        )

    seg_copy = pltpu.make_async_copy(seg_h, seg, in_sem.at[0])
    x_copy = pltpu.make_async_copy(x_h, x, in_sem.at[1])
    seg_copy.start()
    x_copy.start()
    for part in range(3):
        w_copy(part).start()
    seg_copy.wait()
    starts = doc_starts(seg)
    x_copy.wait()
    xt[...] = x[...].T

    def project(part, unused):
        w_copy(part).wait()
        rows = pl.ds(pl.multiple_of(part * width, width), width)
        packed[rows, :] = dot_on(w[:, rows], xt[...], 0, 0).astype(BF)
        packed_copy(part).start()
        return 0

    lax.fori_loop(0, 3, project, 0)
    row = lax.broadcasted_iota(jnp.int32, (AUG, seq), 0)
    same = row == seg[...]
    aug_q = jnp.where(same, 1.0, 0.0).astype(BF)
    aug_k = jnp.where((row < 4) & (~same), -1e30, 0.0).astype(BF)

    def prepare(head, unused):
        qa[head, :HEAD_DIM, :] = packed[head_rows(0, head), :] * jnp.asarray(0.125, BF)
        qa[head, HEAD_DIM:, :] = aug_q
        kt[head] = jnp.concatenate([packed[head_rows(1, head), :], aug_k], axis=0).T
        va[head, :HEAD_DIM, :] = packed[head_rows(2, head), :]
        va[head, HEAD_DIM:, :] = jnp.ones((AUG, seq), BF)
        return 0

    lax.fori_loop(0, HEADS, prepare, 0, unroll=UNROLL)

    def query_block(i, unused):
        qs = pl.ds(pl.multiple_of(i * BLOCK_Q, BLOCK_Q), BLOCK_Q)
        for h in range(HEADS):
            m_s[h] = jnp.full((8, BLOCK_Q), -1e30, F32)
            o_s[h] = jnp.zeros((HEAD_DIM + AUG, BLOCK_Q), F32)

        def part_block(start, size):
            part_qs = pl.ds(pl.multiple_of(i * BLOCK_Q + start, BLOCK_K), size)
            lanes = pl.ds(start, size)

            def key_block(j, unused):
                ks = pl.ds(pl.multiple_of(j * BLOCK_K, BLOCK_K), BLOCK_K)
                first, second = {}, {}
                lag = 4
                for t in range(HEADS + 2 * lag):
                    if t < HEADS:
                        first[t] = dot_on(kt[t, ks, :], qa[t, :, part_qs], 1, 0)
                    h = t - lag
                    if 0 <= h < HEADS:
                        tile = first.pop(h).reshape(BLOCK_K // 8, 8, size)
                        top = jnp.max(jnp.max(tile, axis=0), axis=0, keepdims=True)
                        old = m_s[h, :, lanes]
                        new = jnp.maximum(old, jnp.broadcast_to(top, (8, size)))
                        m_s[h, :, lanes] = new
                        prob = jnp.exp(tile - new[None]).reshape(BLOCK_K, size).astype(BF)
                        second[h] = (prob, jnp.exp(old - new))
                    h = t - 2 * lag
                    if 0 <= h < HEADS:
                        prob, decay = second.pop(h)
                        rows = HEAD_DIM + AUG
                        kept = (o_s[h, :, lanes].reshape(rows // 8, 8, size) * decay[None]).reshape(rows, size)
                        o_s[h, :, lanes] = kept + dot_on(va[h, :, ks], prob, 1, 0)
                return 0

            return key_block

        over_range(starts, seq, i, part_block)
        for h in range(HEADS):
            total = o_s[h, HEAD_DIM : HEAD_DIM + 1, :]
            ctx[h * HEAD_DIM : (h + 1) * HEAD_DIM, qs] = (o_s[h, :HEAD_DIM, :] * (1.0 / total)).astype(BF)
            lse[h, :, qs] = m_s[h][:1] + jnp.log(total)
        for copy in ctx_copies(i):
            copy.start()
        return 0

    lax.fori_loop(0, seq // BLOCK_Q, query_block, 0)
    for part in range(3):
        packed_copy(part).wait()
    for i in range(seq // BLOCK_Q):
        for copy in ctx_copies(i):
            copy.wait()


GROUP = 4


def attend_back_kernel(
    packed_h, ctx_h, lse_h, gctx_h, seg_h, out_from, w_h, grad_row_h, input_grad_h, out_to,
    lse, seg, packed, ctx, gctx, gp, w, grad_row, bounce, input_grad, qs_s, qt, dt, ka, va, dq_s, dk_s, dv_s, in_sem, out_sem,
):
    width, seq = ctx.shape
    groups = HEADS // GROUP
    group_rows = GROUP * HEAD_DIM
    loads = [
        [
            pltpu.make_async_copy(lse_h, lse, in_sem.at[groups, 0]),
            pltpu.make_async_copy(seg_h, seg, in_sem.at[groups, 1]),
        ]
    ]
    for load in loads[0]:
        load.start()
    for group in range(groups):
        pairs = [(gctx_h, gctx, 0), (ctx_h, ctx, 0)] + [(packed_h, packed, part) for part in range(3)]
        held = []
        for number, (source, target, part) in enumerate(pairs):
            rows = pl.ds(part * width + group * group_rows, group_rows)
            held.append(pltpu.make_async_copy(source.at[rows, :], target.at[rows, :], in_sem.at[group, number]))
            held[-1].start()
        loads.append(held)
    late = [
        pltpu.make_async_copy(source, target, out_sem.at[number])
        for number, (source, target) in enumerate(((out_from, bounce), (w_h, w), (grad_row_h, grad_row)))
    ]
    back = pltpu.make_async_copy(bounce, out_to, out_sem.at[3])

    for load in loads.pop(0):
        load.wait()
    starts = doc_starts(seg)
    row = lax.broadcasted_iota(jnp.int32, (AUG, seq), 0)
    same = row == seg[...]
    aug_q = jnp.where(same, 1.0, 0.0)
    aug_k = jnp.where(row < 4, jnp.where(same, 0.0, -1e30), jnp.where(row < 7, 1.0, 0.0)).astype(BF)
    aug_v = jnp.where(row < 3, 1.0, 0.0).astype(BF)

    def minus_rows(value, base):
        rest = -value
        rows = jnp.zeros((AUG, seq), F32)
        for step in range(3):
            piece = rest.astype(BF).astype(F32)
            rows = jnp.where(row == base + step, jnp.broadcast_to(piece, (AUG, seq)), rows)
            rest = rest - piece
        return rows

    def prepare(head, unused):
        rows = head_rows(0, head)
        scaled = packed[rows, :] * jnp.asarray(0.125, BF)
        qs_s[head] = scaled
        qt[head] = jnp.concatenate([scaled, (aug_q + minus_rows(lse[head], 4)).astype(BF)], axis=0).T
        ka[head, :HEAD_DIM, :] = packed[head_rows(1, head), :]
        ka[head, HEAD_DIM:, :] = aug_k
        va[head, :HEAD_DIM, :] = packed[head_rows(2, head), :]
        va[head, HEAD_DIM:, :] = aug_v
        grad = gctx[rows, :]
        inner = jnp.sum(grad.astype(F32) * ctx[rows, :].astype(F32), axis=0, keepdims=True)
        dt[head] = jnp.concatenate([grad, minus_rows(inner, 0).astype(BF)], axis=0).T
        dq_s[head] = jnp.zeros((HEAD_DIM, seq), F32)
        return 0

    for group in range(groups):
        for load in loads[group]:
            load.wait()
        lax.fori_loop(group * GROUP, (group + 1) * GROUP, prepare, 0, unroll=UNROLL)
    for load in late:
        load.start()

    def outer(i, unused):
        ks = pl.ds(pl.multiple_of(i * BLOCK_Q, BLOCK_Q), BLOCK_Q)
        for h in range(HEADS):
            dk_s[h] = jnp.zeros((HEAD_DIM, BLOCK_Q), F32)
            dv_s[h] = jnp.zeros((HEAD_DIM, BLOCK_Q), F32)

        def part_block(start, size):
            part_ks = pl.ds(pl.multiple_of(i * BLOCK_Q + start, BLOCK_K), size)
            lanes = pl.ds(start, size)

            def inner_block(j, unused):
                qs = pl.ds(pl.multiple_of(j * BLOCK_K, BLOCK_K), BLOCK_K)
                first, second = {}, {}
                lag = 4
                for t in range(HEADS + 2 * lag):
                    if t < HEADS:
                        first[t] = (
                            dot_on(qt[t, qs, :], ka[t, :, part_ks], 1, 0),
                            dot_on(dt[t, qs, :], va[t, :, part_ks], 1, 0),
                        )
                    h = t - lag
                    if 0 <= h < HEADS:
                        logits, grad = first.pop(h)
                        prob = jnp.exp(logits)
                        second[h] = (prob.astype(BF), (prob * grad).astype(BF))
                    h = t - 2 * lag
                    if 0 <= h < HEADS:
                        prob, grad = second.pop(h)
                        dv_s[h, :, lanes] += dot_on(gctx[h * HEAD_DIM : (h + 1) * HEAD_DIM, qs], prob, 1, 0)
                        dk_s[h, :, lanes] += dot_on(qs_s[h, :, qs], grad, 1, 0)
                        dq_s[h, :, qs] += dot_on(packed[D + h * HEAD_DIM : D + (h + 1) * HEAD_DIM, part_ks], grad, 1, 1)
                return 0

            return inner_block

        over_range(starts, seq, i, part_block)
        for h in range(HEADS):
            gp[D + h * HEAD_DIM : D + (h + 1) * HEAD_DIM, ks] = dk_s[h].astype(BF)
            gp[2 * D + h * HEAD_DIM : 2 * D + (h + 1) * HEAD_DIM, ks] = dv_s[h].astype(BF)
        return 0

    lax.fori_loop(0, seq // BLOCK_Q, outer, 0)

    def finish(head, unused):
        gp[head_rows(0, head), :] = (dq_s[head] * 0.125).astype(BF)
        return 0

    late[0].wait()
    back.start()
    lax.fori_loop(0, HEADS, finish, 0)
    late[1].wait()
    late[2].wait()
    outs = []

    def leave(step, part):
        rows = pl.ds(step * BLOCK_Q, BLOCK_Q)
        input_grad[rows, :] = (grad_row[rows, :] + part).astype(BF)
        outs.append(
            pltpu.make_async_copy(input_grad.at[rows, :], input_grad_h.at[rows, :], out_sem.at[4 + step])
        )
        outs[-1].start()

    staged(
        seq // BLOCK_Q,
        lambda step: dot_on(gp[:, pl.ds(step * BLOCK_Q, BLOCK_Q)], w[...], 0, 1),
        leave,
    )
    back.wait()
    for out in outs:
        out.wait()


def in_vmem():
    return pl.BlockSpec(memory_space=pltpu.VMEM)


def anywhere():
    return pl.BlockSpec(memory_space=pl.ANY)


def attend(x, w, seg):
    seq = x.shape[0]
    return pl.pallas_call(
        attend_kernel,
        in_specs=[anywhere() for unused in range(3)],
        out_specs=[anywhere() for unused in range(3)],
        out_shape=(
            jax.ShapeDtypeStruct((3 * D, seq), BF),
            jax.ShapeDtypeStruct((D, seq), BF),
            jax.ShapeDtypeStruct((HEADS, 1, seq), F32),
        ),
        scratch_shapes=[
            pltpu.VMEM((seq, D), BF),
            pltpu.VMEM((D, 3 * D), BF),
            pltpu.VMEM((1, seq), jnp.int32),
            pltpu.VMEM((3 * D, seq), BF),
            pltpu.VMEM((D, seq), BF),
            pltpu.VMEM((HEADS, 1, seq), F32),
            pltpu.VMEM((D, seq), BF),
            pltpu.VMEM((HEADS, HEAD_DIM + AUG, seq), BF),
            pltpu.VMEM((HEADS, seq, HEAD_DIM + AUG), BF),
            pltpu.VMEM((HEADS, HEAD_DIM + AUG, seq), BF),
            pltpu.VMEM((HEADS, 8, BLOCK_Q), F32),
            pltpu.VMEM((HEADS, HEAD_DIM + AUG, BLOCK_Q), F32),
            pltpu.SemaphoreType.DMA((2,)),
            pltpu.SemaphoreType.DMA((3,)),
            pltpu.SemaphoreType.DMA((3,)),
            pltpu.SemaphoreType.DMA((2, seq // BLOCK_Q)),
        ],
        name="attend",
        compiler_params=pltpu.CompilerParams(vmem_limit_bytes=60 << 20),
    )(x, w, seg)


def attend_back(packed, ctx, lse, gctx, seg, out, w, grad_row):
    seq = packed.shape[1]
    aug = HEAD_DIM + AUG
    return pl.pallas_call(
        attend_back_kernel,
        in_specs=[anywhere() for unused in range(8)],
        out_specs=[anywhere(), anywhere()],
        out_shape=(jax.ShapeDtypeStruct((seq, D), BF), jax.ShapeDtypeStruct((seq, D), BF)),
        scratch_shapes=[
            pltpu.VMEM((HEADS, 1, seq), F32),
            pltpu.VMEM((1, seq), jnp.int32),
            pltpu.VMEM((3 * D, seq), BF),
            pltpu.VMEM((D, seq), BF),
            pltpu.VMEM((D, seq), BF),
            pltpu.VMEM((3 * D, seq), BF),
            pltpu.VMEM((D, 3 * D), BF),
            pltpu.VMEM((seq, D), F32),
            pltpu.VMEM((seq, D), BF),
            pltpu.VMEM((seq, D), BF),
            pltpu.VMEM((HEADS, HEAD_DIM, seq), BF),
            pltpu.VMEM((HEADS, seq, aug), BF),
            pltpu.VMEM((HEADS, seq, aug), BF),
            pltpu.VMEM((HEADS, aug, seq), BF),
            pltpu.VMEM((HEADS, aug, seq), BF),
            pltpu.VMEM((HEADS, HEAD_DIM, seq), F32),
            pltpu.VMEM((HEADS, HEAD_DIM, BLOCK_Q), F32),
            pltpu.VMEM((HEADS, HEAD_DIM, BLOCK_Q), F32),
            pltpu.SemaphoreType.DMA((HEADS // GROUP + 1, 5)),
            pltpu.SemaphoreType.DMA((4 + seq // BLOCK_Q,)),
        ],
        name="attend_back",
        cost_estimate=pl.CostEstimate(flops=30_000_000_000, bytes_accessed=20_000_000, transcendentals=0),
        compiler_params=pltpu.CompilerParams(vmem_limit_bytes=62 << 20),
    )(packed, ctx, lse, gctx, seg, out, w, grad_row)


def pieces(value):
    high = value.astype(BF)
    return high, (value - high.astype(F32)).astype(BF)


def normalize(values):
    centre = values - jnp.mean(values, axis=-1, keepdims=True)
    factor = lax.rsqrt(jnp.mean(centre * centre, axis=-1, keepdims=True) + 1e-06)
    return centre * factor, factor


def norm_back(scaled, unit_vals, factor):
    return factor * (
        scaled
        - jnp.mean(scaled, axis=-1, keepdims=True)
        - unit_vals * jnp.mean(scaled * unit_vals, axis=-1, keepdims=True)
    )


def gelu_parts(values):
    rising = 0.5 * lax.erf(values * math.sqrt(0.5)) + 0.5
    low = values.astype(BF)
    bell = jnp.exp2(low * low * jnp.asarray(-0.5 * math.log2(math.e), BF))
    steep = low * jnp.asarray(1.0 / math.sqrt(2.0 * math.pi), BF)
    return (values * rising).astype(BF), rising.astype(BF) + steep * bell


def gelu_doubled(values):
    rising = lax.erf(values * math.sqrt(0.5)) + 1.0
    low = values.astype(BF)
    bell = jnp.exp2(low * low * jnp.asarray(-0.5 * math.log2(math.e), BF))
    steep = low * jnp.asarray(2.0 / math.sqrt(2.0 * math.pi), BF)
    return (values * rising).astype(BF), rising.astype(BF) + steep * bell


def fold_rows(values):
    rows, columns = values.shape
    return jnp.sum(values.reshape(rows // 8, 8, columns), axis=0)


def staged(count, product, finish, between=None):
    held = {}
    for step in range(count + 1):
        if between is not None and step == count // 2:
            between()
        if step < count:
            held[step] = product(step)
        if step >= 1:
            finish(step - 1, held.pop(step - 1))


MESH = pl.DeviceIdType.MESH
PLANE = 4
DEPTH = 4
OWN_ROWS = 24
SLABS = 2 * 2 * DEPTH + 2
PLANE_ROWS = 96
CORE_ROWS = 384


def place():
    wide, narrow = lax.axis_index("wide"), lax.axis_index("narrow")
    return wide // 2, lax.rem(wide, 2), narrow // 2, lax.rem(narrow, 2)


def device(z, x, y, core):
    return (z * 2 + x, y * 2 + core)


def plane_mate(step):
    z, x, y, core = place()
    return device(z, jnp.bitwise_xor(x, step // 2), jnp.bitwise_xor(y, step % 2), core)


def depth_mate(step):
    z, x, y, core = place()
    return device(lax.rem(z + step, DEPTH), x, y, core)


def core_mate():
    z, x, y, core = place()
    return device(z, x, y, 1 - core)


def remote(source, target, sems, slot, mate):
    return pltpu.make_async_remote_copy(
        src_ref=source,
        dst_ref=target,
        send_sem=sems.at[0, slot],
        recv_sem=sems.at[1, slot],
        device_id=mate,
        device_id_type=MESH,
    )


def greet(mates):
    barrier = pltpu.get_barrier_semaphore()
    for mate in mates:
        pl.semaphore_signal(barrier, inc=1, device_id=mate, device_id_type=MESH)
    return lambda: pl.semaphore_wait(barrier, len(mates))


class Scatter:
    def __init__(self, which, square, kept, send, near, plane, small_send, small, gathered, sems):
        self.which, self.square, self.kept = which, square, kept
        self.send, self.near, self.plane = send, near, plane
        self.small_send, self.small, self.gathered, self.sems = small_send, small, gathered, sems
        z, x, y, core = place()
        self.z, self.spot, self.core = z, x * 2 + y, core
        self.copies = []

    def rows(self, start, count):
        return pl.ds(pl.multiple_of(start, 8), count)

    def finish(self):
        for copy in self.copies:
            copy.wait()
        self.copies = []

    def go(self, source, target, slot, mate):
        copy = remote(source, target, self.sems, self.which * 16 + slot, mate)
        copy.start()
        self.copies.append(copy)

    def to_core(self):
        self.go(self.send.at[self.which], self.near.at[self.which], 0, core_mate())

    def to_plane(self):
        self.finish()
        for q in range(PLANE):
            rows = pl.ds(q * PLANE_ROWS, PLANE_ROWS)
            total = self.square[rows, :] + self.near[self.which, q].astype(F32)
            self.square[rows, :] = total
            self.send[self.which, q] = total.astype(BF)
        self.kept[self.which] = self.square[self.rows(self.spot * PLANE_ROWS, PLANE_ROWS), :]
        for step in range(1, PLANE):
            spot = jnp.bitwise_xor(self.spot, step)
            self.go(self.send.at[self.which, spot], self.plane.at[self.which, step - 1], step, plane_mate(step))

    def to_depth(self):
        self.finish()
        total = self.kept[self.which]
        for step in range(1, PLANE):
            total = total + self.plane[self.which, step - 1].astype(F32)
        self.kept[self.which] = total
        for k in range(DEPTH):
            self.small_send[self.which, k] = total[k * OWN_ROWS : (k + 1) * OWN_ROWS, :].astype(BF)
        for step in range(1, DEPTH):
            spot = lax.rem(self.z + step, DEPTH)
            self.go(
                self.small_send.at[self.which, spot],
                self.small.at[self.which, step - 1],
                PLANE - 1 + step,
                depth_mate(step),
            )

    def share(self, last=None):
        self.finish()
        total = self.kept[self.which, self.rows(self.z * OWN_ROWS, OWN_ROWS), :]
        for step in range(1, DEPTH):
            total = total + self.small[self.which, step - 1].astype(F32)
        if last is not None:
            high, rest = pieces(total)
            total = dot_on(high, last, 1, 0) + dot_on(rest, last, 1, 0)
        mine = self.gathered.at[self.slab(self.z)]
        mine[...] = total.astype(BF)
        for step in range(1, DEPTH):
            self.go(mine, mine, PLANE + DEPTH - 2 + step, depth_mate(step))

    def slab(self, z):
        return (self.core * 2 + self.which) * DEPTH + z

    def pair(self):
        arriving, self.copies = self.copies, []
        for step in range(DEPTH):
            if step:
                arriving[step - 1].wait()
            spot = lax.rem(self.z - step + DEPTH, DEPTH)
            chunk = self.gathered.at[self.slab(spot)]
            self.go(chunk, chunk, PLANE + 2 * DEPTH - 2 + step, core_mate())


ROWS_AT_ONCE = 256
HIDDEN_AT_ONCE = 512
HIDDEN_ROWS = 512


def middle_kernel(
    joined, x_h, g_h, ctx_h, wo_h, win_h, wout_h, down_h, up_h, wq_h, wk_h, wv_h,
    bias_h, gain_one_h, shift_one_h, gain_two_h, shift_two_h, mask_h,
    out_h, gr_h, gctx_h, v_h, gg_h, sums_h,
    x, g, ctx, wo, win, wout, bank, wq, wk, wv,
    unit_one, unit_two, bottle, guide, total, act, slope, low, factor, mix, score_grads,
    v_s, gg_s, sums_part, vectors, mask, sums_out, in_sem, vector_sem, out_sem, *links,
):
    seq, width = x.shape
    blocks = seq // ROWS_AT_ONCE
    mix_scale = 1.0 / math.sqrt(D)
    vector_loads = [
        pltpu.make_async_copy(source, vectors.at[number, pl.ds(0, width)], vector_sem.at[number])
        for number, source in enumerate((gain_one_h, shift_one_h, gain_two_h, shift_two_h))
    ] + [
        pltpu.make_async_copy(
            bias_h.at[pl.ds(number * 1024, 1024)], vectors.at[4 + number], vector_sem.at[4 + number]
        )
        for number in range(win.shape[1] // 1024)
    ] + [pltpu.make_async_copy(mask_h, mask, vector_sem.at[4 + win.shape[1] // 1024])]
    loads = {}
    names = ("down", "up", "ctx", "wo", "x", "win", "wout", "wq", "wk", "g", "wv")
    sources = (down_h, up_h, ctx_h, wo_h, x_h, win_h, wout_h, wq_h, wk_h, g_h, wv_h)
    targets = (bank.at[0], bank.at[1], ctx, wo, x, win, wout, wq, wk, g, wv)
    gain_one, shift_one, gain_two, shift_two = (vectors.at[number : number + 1, :width] for number in range(4))
    if joined:
        (
            kept, send, near, plane, small_send, small, gathered,
            sums_near, sums_depth, sums_mid, link_sems, bank_sems, sums_sems,
        ) = links
        arrived = greet(
            [core_mate()]
            + [plane_mate(step) for step in range(1, PLANE)]
            + [depth_mate(step) for step in range(1, DEPTH)]
        )
        spot = lax.axis_index("narrow")
        shard = down_h.shape[0]

        own_rows = pl.ds(pl.multiple_of(spot * shard, 16), shard)
        targets = (bank.at[0, own_rows, :], bank.at[1, own_rows, :]) + targets[2:]
    for number, name in enumerate(names):
        loads[name] = pltpu.make_async_copy(sources[number], targets[number], in_sem.at[number])
    for name in names[:5]:
        loads[name].start()
    for load in vector_loads:
        load.start()
    for name in names[5:]:
        loads[name].start()

    def rows_of(step):
        return pl.ds(step * ROWS_AT_ONCE, ROWS_AT_ONCE)

    t_one, t_two, t_three, t_four = (pl.ds(k * width, width) for k in range(4))
    down, up = 0, 1
    column = lax.broadcasted_iota(jnp.int32, (ADAPTERS, width), 1)
    owner = lax.rem(column, ADAPTERS)
    chosen = jnp.where(
        owner == lax.broadcasted_iota(jnp.int32, (ADAPTERS, width), 0), 1.0, 0.0
    ).astype(BF)

    chosen_twice = jnp.concatenate([chosen, chosen], axis=0)

    def per_adapter(values):
        high, rest = pieces(values)
        return dot_on(chosen, high, 1, 1) + dot_on(chosen, rest, 1, 1)

    def per_unit(values):
        return dot_on(jnp.concatenate(pieces(values), axis=0), chosen_twice, 0, 0)

    loads["ctx"].wait()
    loads["wo"].wait()

    def finish_first(step, part):
        rows = rows_of(step)
        if step == 0:
            loads["x"].wait()
            for load in vector_loads:
                load.wait()
        unit, scale = normalize(x[rows, :].astype(F32) + part)
        unit_one[rows, :] = unit
        factor[rows, 0:1] = scale
        low[rows, :] = (unit * gain_one[...] + shift_one[...]).astype(BF)

    if joined:
        arrived()
        loads["down"].wait()
        loads["up"].wait()

        def bank_part(which, index, slot, mate):
            rows = bank.at[which, pl.ds(pl.multiple_of(index * shard, 16), shard), :]
            return remote(rows, rows, bank_sems, slot, mate)

        far_copies = [bank_part(which, spot, which, plane_mate(1)) for which in (down, up)]
        near_copies = [bank_part(which, spot, 2 + which, core_mate()) for which in (down, up)]
        for copy in far_copies + near_copies:
            copy.start()

        def forward(which):
            far_copies[which].wait()
            far_copies[which] = bank_part(which, jnp.bitwise_xor(spot, 2), 4 + which, core_mate())
            far_copies[which].start()

        def whole_bank(which):
            far_copies[which].wait()
            near_copies[which].wait()
    staged(blocks, lambda step: dot_on(ctx[:, rows_of(step)], wo[...], 0, 0), finish_first)

    loads["win"].wait()

    def hidden(chunk, unused):
        columns = pl.ds(pl.multiple_of(chunk * HIDDEN_AT_ONCE, HIDDEN_AT_ONCE), HIDDEN_AT_ONCE)
        per_row = 1024 // HIDDEN_AT_ONCE
        lanes = pl.ds(pl.multiple_of(lax.rem(chunk, per_row) * HIDDEN_AT_ONCE, HIDDEN_AT_ONCE), HIDDEN_AT_ONCE)
        bias = vectors[pl.ds(4 + chunk // per_row, 1), lanes]

        def rows_in(step):
            return pl.ds(step * HIDDEN_ROWS, HIDDEN_ROWS)

        def finish(step, part):
            rows = rows_in(step)
            value, rising = gelu_doubled(part + bias)
            act[rows, columns] = value
            slope[rows, columns] = rising

        staged(seq // HIDDEN_ROWS, lambda step: dot_on(low[rows_in(step), :], win[:, columns], 1, 0), finish)
        return 0

    lax.fori_loop(0, win.shape[1] // HIDDEN_AT_ONCE, hidden, 0)
    loads["wout"].wait()
    if joined:
        forward(down)

    def second(half, unused):
        def rows_in(step):
            start = half * (seq // 2) + step * ROWS_AT_ONCE
            return pl.ds(pl.multiple_of(start, ROWS_AT_ONCE), ROWS_AT_ONCE)

        def finish(step, part):
            rows = rows_in(step)
            unit, scale = normalize(unit_one[rows, :] * gain_one[...] + shift_one[...] + 0.5 * part)
            unit_two[rows, :] = unit
            factor[rows, 1:2] = scale
            low[rows, :] = (unit * gain_two[...] + shift_two[...]).astype(BF)

        staged(blocks // 2, lambda step: dot_on(act[rows_in(step), :], wout[...], 1, 0), finish)
        return 0

    lax.fori_loop(0, 2, second, 0)

    def h_two(rows):
        return unit_two[rows, :] * gain_two[...] + shift_two[...]

    def keep(target, place, size):
        def finish(step, part):
            target[pl.ds(step * size, size), place] = part.astype(BF)

        return finish

    everything = pl.ds(0, width)
    if joined:
        forward(up)
        whole_bank(down)
    else:
        loads["down"].wait()
        loads["up"].wait()

    def finish_down(step, part):
        rows = rows_of(step)
        bottle[rows, :] = part * (0.5 * lax.erf(part * math.sqrt(0.5)) + 0.5)
        act[rows, t_four] = gelu_parts(part)[1]

    staged(blocks, lambda step: dot_on(low[rows_of(step), :], bank[down], 1, 1), finish_down)
    if joined:
        whole_bank(up)
    loads["wk"].wait()
    third = width // 3
    staged(3, lambda step: dot_on(bank[up, pl.ds(step * third, third), :], wk[...], 1, 0), keep(act, t_one, third))
    loads["wq"].wait()
    through = act.at[:width, t_one]
    staged(3, lambda step: dot_on(wq[pl.ds(step * third, third), :], through[...], 1, 1), keep(wk, everything, third))

    def finish_guide(step, part):
        rows = rows_of(step)
        guide[rows, :] = part
        mix[:, rows] = per_adapter(bottle[rows, :] * part)

    staged(blocks, lambda step: dot_on(low[rows_of(step), :], wk[...], 1, 0), finish_guide)
    scores = mix[...] * mix_scale
    shifted = scores - jnp.max(scores, axis=0, keepdims=True)
    exponents = jnp.exp(shifted)
    total_exponent = jnp.sum(exponents, axis=0, keepdims=True)
    weights = exponents / total_exponent
    entropies = -jnp.sum(weights * (shifted - jnp.log(total_exponent)), axis=0, keepdims=True)
    mix[...] = weights

    def finish_mix(step, part):
        rows = rows_of(step)
        act[rows, t_one] = (part * bottle[rows, :]).astype(BF)

    staged(blocks, lambda step: per_unit(mix[:, rows_of(step)]), finish_mix)
    real = mask[...].astype(F32)
    ent = jnp.sum(entropies * real, axis=1, keepdims=True)
    lane = lax.broadcasted_iota(jnp.int32, (1, 1024), 1)
    sums_out[7:8, :] = jnp.where(lane < 128, ent, jnp.sum(real, axis=1, keepdims=True))
    sums_out[3:7, width:] = jnp.zeros((4, 1024 - width), F32)

    def finish_update(step, part):
        rows = rows_of(step)
        x[rows, :] = (h_two(rows) + part).astype(BF)

    staged(blocks, lambda step: dot_on(act[rows_of(step), t_one], bank[up], 1, 0), finish_update)

    loads["g"].wait()

    def over_tokens(left, right, target):
        def product(step):
            return dot_on(left(pl.ds(step * third, third)), right, 0, 0)

        def finish(step, part):
            target[pl.ds(step * third, third), :] = part

        staged(3, product, finish)

    def halves(left, base, right, target, which):
        core = place()[3]

        def product(step):
            start = base + (core if step else 1 - core) * CORE_ROWS
            return dot_on(left[:, pl.ds(pl.multiple_of(start, 128), CORE_ROWS)], right, 0, 0)

        def finish(step, part):
            if step:
                target[...] = part
            else:
                for q in range(PLANE):
                    send[which, q] = part[q * PLANE_ROWS : (q + 1) * PLANE_ROWS, :].astype(BF)

        finish(0, product(0))
        (value_sum, joint_sum)[which].to_core()
        finish(1, product(1))

    if joined:
        value_sum, joint_sum = (
            Scatter(k, v_s, kept, send, near, plane, small_send, small, gathered, link_sems) for k in range(2)
        )
        halves(x, 0, g[...], v_s, 0)
    else:
        over_tokens(lambda cols: x[:, cols], g[...], v_s)
    if not joined:
        v_out = pltpu.make_async_copy(v_s, v_h, out_sem.at[0])
        v_out.start()

    loads["wv"].wait()

    def finish_blend(step, part):
        rows = rows_of(step)
        total[rows, :] = g[rows, :].astype(F32) + part
        act[rows, t_one] = part.astype(BF)

    staged(blocks, lambda step: dot_on(g[rows_of(step), :], wv[...], 1, 1), finish_blend)

    def finish_mixed(step, part):
        rows = rows_of(step)
        act[rows, t_one] = part.astype(BF)
        score_grads[:, rows] = per_adapter(part * bottle[rows, :])

    staged(blocks, lambda step: dot_on(act[rows_of(step), t_one], bank[up], 1, 1), finish_mixed, value_sum.to_plane if joined else None)
    weights = mix[...]
    grad_weights = score_grads[...]
    inner = jnp.sum(grad_weights * weights, axis=0, keepdims=True)
    score_grads[...] = weights * (grad_weights - inner) * mix_scale

    def finish_units(step, part):
        rows = rows_of(step)
        mixed, score_term = part
        grad_bottle = act[rows, t_one].astype(F32) * mixed + score_term * guide[rows, :]
        act[rows, t_three] = (grad_bottle * act[rows, t_four].astype(F32)).astype(BF)
        act[rows, t_one] = (score_term * bottle[rows, :]).astype(BF)

    staged(
        blocks,
        lambda step: (per_unit(mix[:, rows_of(step)]), per_unit(score_grads[:, rows_of(step)])),
        finish_units,
    )
    if joined:
        halves(low, 0, act[:, t_one], v_s, 1)
    else:
        over_tokens(lambda cols: low[:, cols], act[:, t_one], gg_s)
    if not joined:
        gg_out = pltpu.make_async_copy(gg_s, gg_h, out_sem.at[2])
        gg_out.start()
    partial = [jnp.zeros((8, width), F32) for unused in range(4)]

    def finish_two(step, part):
        rows = rows_of(step)
        grad = total[rows, :] + part
        unit = unit_two[rows, :]
        partial[0] = partial[0] + fold_rows(grad * unit)
        partial[1] = partial[1] + fold_rows(grad)
        back = norm_back(grad * gain_two[...], unit, factor[rows, 1:2])
        total[rows, :] = back
        low[rows, :] = (0.5 * back).astype(BF)

    staged(
        blocks,
        lambda step: dot_on(act[rows_of(step), t_three], bank[down], 1, 0)
        + dot_on(act[rows_of(step), t_one], wk[...], 1, 1),
        finish_two,
        joint_sum.to_plane if joined else None,
    )

    if joined:
        value_sum.to_depth()

    def hidden_back(chunk, unused):
        columns = pl.ds(pl.multiple_of(chunk * HIDDEN_AT_ONCE, HIDDEN_AT_ONCE), HIDDEN_AT_ONCE)
        held = [jnp.zeros((8, HIDDEN_AT_ONCE), F32)]

        def rows_in(step):
            return pl.ds(step * HIDDEN_ROWS, HIDDEN_ROWS)

        def finish(step, part):
            rows = rows_in(step)
            grad = (part * slope[rows, columns].astype(F32)).astype(BF)
            act[rows, columns] = grad
            held[0] = held[0] + fold_rows(grad.astype(F32))

        staged(seq // HIDDEN_ROWS, lambda step: dot_on(low[rows_in(step), :], wout[columns, :], 1, 1), finish)
        sums_part[chunk] = held[0]
        return 0

    lax.fori_loop(0, win.shape[1] // HIDDEN_AT_ONCE, hidden_back, 0)
    for number in range(win.shape[1] // HIDDEN_AT_ONCE):
        at, lanes = divmod(number * HIDDEN_AT_ONCE, 1024)
        sums_out[at : at + 1, pl.ds(lanes, HIDDEN_AT_ONCE)] = jnp.sum(sums_part[number], axis=0, keepdims=True)
    sums_out[5:6, :width] = jnp.sum(partial[0], axis=0, keepdims=True)
    sums_out[6:7, :width] = jnp.sum(partial[1], axis=0, keepdims=True)
    if joined:
        value_sum.share()
        joint_sum.to_depth()

    def first_back(half, carried):
        def rows_in(step):
            start = half * (seq // 2) + step * ROWS_AT_ONCE
            return pl.ds(pl.multiple_of(start, ROWS_AT_ONCE), ROWS_AT_ONCE)

        held = list(carried)

        def finish(step, part):
            rows = rows_in(step)
            grad = total[rows, :] + part
            unit = unit_one[rows, :]
            held[0] = held[0] + fold_rows(grad * unit)
            held[1] = held[1] + fold_rows(grad)
            back = norm_back(grad * gain_one[...], unit, factor[rows, 0:1])
            total[rows, :] = back
            low[rows, :] = back.astype(BF)

        staged(blocks // 2, lambda step: dot_on(act[rows_in(step), :], win[...], 1, 1), finish)
        return tuple(held)

    zero = jnp.zeros((8, width), F32)
    gain_sum, shift_sum = lax.fori_loop(0, 2, first_back, (zero, zero))
    sums_out[3:4, :width] = jnp.sum(gain_sum, axis=0, keepdims=True)
    sums_out[4:5, :width] = jnp.sum(shift_sum, axis=0, keepdims=True)
    if joined:
        near_copy = remote(sums_out, sums_near, sums_sems, 0, core_mate())
        near_copy.start()
        value_sum.pair()
        joint_sum.share(bank[up])
    gr_copy = pltpu.make_async_copy(total, gr_h, out_sem.at[3])
    gr_copy.start()

    def finish_ctx(step, part):
        ctx[pl.ds(step * third, third), :] = part.astype(BF)

    staged(3, lambda step: dot_on(wo[pl.ds(step * third, third), :], low[...], 1, 1), finish_ctx)
    gctx_copy = pltpu.make_async_copy(ctx, gctx_h, out_sem.at[4])
    gctx_copy.start()
    if joined:
        near_copy.wait()
        sums_mid[...] = sums_out[...] + sums_near[...]
        depth_copies = [
            remote(sums_mid, sums_depth.at[step - 1], sums_sems, step, depth_mate(step)) for step in range(1, DEPTH)
        ]
        for copy in depth_copies:
            copy.start()
        value_sum.finish()

    def finish_out(step, part):
        rows = rows_of(step)
        x[rows, :] = (h_two(rows) + part).astype(BF)

    staged(blocks, lambda step: dot_on(x[rows_of(step), :], wv[...], 1, 0), finish_out)
    out_copy = pltpu.make_async_copy(x, out_h, out_sem.at[1])
    out_copy.start()
    if joined:
        joint_sum.pair()
        for copy in depth_copies:
            copy.wait()
        rest = sums_mid[...] + sums_depth[0] + sums_depth[1] + sums_depth[2]
        parts = []
        for unused in range(3):
            parts.append(rest.astype(BF).astype(F32))
            rest = rest - parts[-1]
        parts = jnp.concatenate(parts, axis=0).astype(BF)
        gathered[SLABS - 2] = parts[:, :width]
        gathered[SLABS - 1] = jnp.zeros((OWN_ROWS, width), BF)
        gathered[SLABS - 1, :, : 1024 - width] = parts[:, width:]
        joint_sum.finish()
        v_out = pltpu.make_async_copy(gathered, v_h, out_sem.at[0])
        v_out.start()
    else:
        sums_copy = pltpu.make_async_copy(sums_out, sums_h, out_sem.at[5])
        sums_copy.start()
        gg_out.wait()
        sums_copy.wait()
    v_out.wait()
    out_copy.wait()
    gr_copy.wait()
    gctx_copy.wait()


def middle(joined, x, g, ctx, wo, win, wout, down, up, wq, wk, wv, bias, gain_one, shift_one, gain_two, shift_two, mask):
    seq, width = x.shape
    hidden = win.shape[1]
    token_low = pltpu.VMEM((seq, width), BF)
    token_wide = pltpu.VMEM((seq, width), F32)
    square = pltpu.VMEM((width, width), BF)
    sum_square = pltpu.VMEM((CORE_ROWS if joined else width, width), F32)
    links = [
        pltpu.VMEM((2, PLANE_ROWS, width), F32),
        pltpu.VMEM((2, PLANE, PLANE_ROWS, width), BF),
        pltpu.VMEM((2, PLANE, PLANE_ROWS, width), BF),
        pltpu.VMEM((2, PLANE - 1, PLANE_ROWS, width), BF),
        pltpu.VMEM((2, DEPTH, OWN_ROWS, width), BF),
        pltpu.VMEM((2, DEPTH - 1, OWN_ROWS, width), BF),
        pltpu.VMEM((SLABS, OWN_ROWS, width), BF),
        pltpu.VMEM((8, 1024), F32),
        pltpu.VMEM((DEPTH - 1, 8, 1024), F32),
        pltpu.VMEM((8, 1024), F32),
        pltpu.SemaphoreType.DMA((2, 32)),
        pltpu.SemaphoreType.DMA((2, 6)),
        pltpu.SemaphoreType.DMA((2, DEPTH)),
    ]
    return pl.pallas_call(
        functools.partial(middle_kernel, joined),
        in_specs=[anywhere() for unused in range(17)],
        out_specs=[anywhere() for unused in range(6)],
        out_shape=(
            jax.ShapeDtypeStruct((seq, width), BF),
            jax.ShapeDtypeStruct((seq, width), F32),
            jax.ShapeDtypeStruct((width, seq), BF),
            jax.ShapeDtypeStruct((SLABS, OWN_ROWS, width), BF)
            if joined
            else jax.ShapeDtypeStruct((width, width), F32),
            jax.ShapeDtypeStruct((8, 128) if joined else (width, width), F32),
            jax.ShapeDtypeStruct((8, 128 if joined else 1024), F32),
        ),
        scratch_shapes=[
            token_low, token_low, pltpu.VMEM((width, seq), BF),
            square, pltpu.VMEM((width, hidden), BF), pltpu.VMEM((hidden, width), BF),
            pltpu.VMEM((2, width, width), BF), square, square, square,
            token_wide, token_wide, token_wide, token_wide, token_wide,
            pltpu.VMEM((seq, hidden), BF), pltpu.VMEM((seq, hidden), BF), token_low,
            pltpu.VMEM((seq, 2), F32), pltpu.VMEM((ADAPTERS, seq), F32), pltpu.VMEM((ADAPTERS, seq), F32),
            sum_square, pltpu.VMEM((8, 128) if joined else (width, width), F32),
            pltpu.VMEM((hidden // HIDDEN_AT_ONCE, 8, HIDDEN_AT_ONCE), F32),
            pltpu.VMEM((8, 1024), F32), pltpu.VMEM((1, seq), jnp.int32), pltpu.VMEM((8, 1024), F32),
            pltpu.SemaphoreType.DMA((11,)),
            pltpu.SemaphoreType.DMA((8,)), pltpu.SemaphoreType.DMA((6,)),
        ]
        + (links if joined else []),
        name="middle",
        compiler_params=pltpu.CompilerParams(
            vmem_limit_bytes=VMEM_BYTES, **(dict(collective_id=0, has_side_effects=True) if joined else {})
        ),
    )(x, g, ctx, wo, win, wout, down, up, wq, wk, wv, bias, gain_one, shift_one, gain_two, shift_two, mask)

def products_kernel(
    mine_h, first_h, second_h, third_h, wk_h, wq_h,
    value_h, query_h, key_h, bias_h, gain_one_h, shift_one_h, gain_two_h, shift_two_h, entropy,
    sums, held, wk, wq, square, joint, low, in_sem, out_sem,
):
    width = wk.shape[0]
    z, x, y, core = place()
    loads = [
        pltpu.make_async_copy(source, target, in_sem.at[number])
        for number, (source, target) in enumerate(
            [(source, held.at[step]) for step, source in enumerate((mine_h, first_h, second_h, third_h))]
            + [(wk_h, wk), (wq_h, wq)]
        )
    ]
    for load in loads:
        load.start()
    outs = []

    def leave(source, target):
        outs.append(pltpu.make_async_copy(source, target, out_sem.at[len(outs)]))
        outs[-1].start()

    for load in loads[:PLANE]:
        load.wait()

    def unpack(which, target):
        for step in range(PLANE):
            base = jnp.bitwise_xor(x * 2 + y, step) * PLANE_ROWS
            for side in range(2):
                for depth in range(DEPTH):
                    start = pl.multiple_of(base + side * CORE_ROWS + depth * OWN_ROWS, 8)
                    slab = (side * 2 + which) * DEPTH + depth
                    target[pl.ds(start, OWN_ROWS), :] = held[step, slab].astype(F32)

    unpack(0, square.at[0])
    leave(square.at[0], value_h)
    totals = [
        sum(held[step, SLABS - 2 + part].astype(F32) for step in range(PLANE)).reshape(3, 8, width)
        for part in range(2)
    ]
    wide_total, rest_total = ((total[0] + total[1]) + total[2] for total in totals)
    sums[:, :width] = wide_total
    sums[:, width:] = rest_total[:, : 1024 - width]
    for number in range(bias_h.shape[0] // 1024):
        leave(sums.at[number], bias_h.at[pl.ds(number * 1024, 1024)])
    for number, target in enumerate((gain_one_h, shift_one_h, gain_two_h, shift_two_h)):
        leave(sums.at[3 + number, pl.ds(0, width)], target)
    entropy[...] = sums[7:8, 0:1] / sums[7:8, 128:129]
    unpack(1, joint)
    low[...] = joint[...].astype(BF)
    loads[PLANE].wait()
    half = width // 2
    for step in range(2):
        rows = pl.ds(step * half, half)
        square[1, rows, :] = dot_on(low[rows, :], wk[...], 1, 0)
        leave(square.at[1, rows, :], query_h.at[rows, :])
    loads[PLANE + 1].wait()
    for step in range(2):
        rows = pl.ds(step * half, half)
        joint[rows, :] = dot_on(low[:, rows], wq[...], 0, 0)
        leave(joint.at[rows, :], key_h.at[rows, :])
    for out in outs:
        out.wait()


def products(held, wk, wq, hidden):
    width = wk.shape[0]
    square = jax.ShapeDtypeStruct((width, width), F32)
    vector = jax.ShapeDtypeStruct((width,), F32)
    return pl.pallas_call(
        products_kernel,
        in_specs=[anywhere() for unused in range(6)],
        out_specs=[anywhere() for unused in range(8)] + [in_vmem()],
        out_shape=(
            square, square, square, jax.ShapeDtypeStruct((hidden,), F32), vector, vector, vector, vector,
            jax.ShapeDtypeStruct((1, 1), F32),
        ),
        scratch_shapes=[
            pltpu.VMEM((8, 1024), F32),
            pltpu.VMEM((PLANE,) + held[0].shape, BF),
            pltpu.VMEM((width, width), BF),
            pltpu.VMEM((width, width), BF),
            pltpu.VMEM((2, width, width), F32),
            pltpu.VMEM((width, width), F32),
            pltpu.VMEM((width, width), BF),
            pltpu.SemaphoreType.DMA((PLANE + 2,)),
            pltpu.SemaphoreType.DMA((12,)),
        ],
        name="products",
        compiler_params=pltpu.CompilerParams(vmem_limit_bytes=VMEM_BYTES),
    )(*held, wk, wq)


def plane_order(step):
    order = []
    for index in range(32):
        wide, narrow = index // 4, index % 4
        wide, narrow = wide ^ (step // 2), narrow ^ (2 * (step % 2))
        order.append((index, wide * 4 + narrow))
    return order

def per_device(
    joined,
    block_input, segments, real_mask, qkv_weight, attn_out_weight, ffn_in_weight, ffn_bias, ffn_out_weight,
    first_gain, first_shift, second_gain, second_shift, adapter_down, adapter_up,
    joining_query, joining_key, joining_value, cotangent,
):
    row_count, seq_len, width = block_input.shape
    tokens = block_input.reshape(seq_len, width)
    units = adapter_down.shape[2]
    down = jnp.transpose(adapter_down, (2, 1, 0)).reshape(ADAPTERS * units, width)
    up = jnp.transpose(adapter_up, (1, 0, 2)).reshape(ADAPTERS * units, width)
    if not joined:
        down, up = (lax.all_gather(part, "narrow", axis=0, tiled=True) for part in (down, up))
    seg_row = segments.reshape(1, seq_len)
    packed, context, log_total = attend(tokens, qkv_weight, seg_row)
    out, grad_row, grad_context, value_sum, joint_sum, sums = middle(
        joined,
        tokens, cotangent.reshape(seq_len, width), context, attn_out_weight, ffn_in_weight, ffn_out_weight,
        down, up, joining_query, joining_key, joining_value, ffn_bias, first_gain, first_shift,
        second_gain, second_shift, real_mask.reshape(1, seq_len),
    )
    input_grad, out = attend_back(
        packed, context, log_total, grad_context, seg_row, out, qkv_weight, grad_row
    )
    if joined:
        held = [value_sum] + [
            lax.ppermute(value_sum, ("wide", "narrow"), plane_order(step)) for step in range(1, PLANE)
        ]
        value_grad, query_grad, key_grad, bias_grad, gain_one, shift_one, gain_two, shift_two, entropy = products(
            held, joining_key, joining_query, ffn_bias.shape[0]
        )
    else:
        value_grad, joint_sum, sums = lax.psum((value_sum, joint_sum, sums), ("wide", "narrow"))
        high, rest = pieces(joint_sum)
        joint_sum = (dot_on(high, up, 1, 0) + dot_on(rest, up, 1, 0)).astype(BF)
        query_grad = dot_on(joint_sum, joining_key, 1, 0)
        key_grad = dot_on(joint_sum, joining_query, 0, 0)
        bias_grad = sums[:3].reshape(ffn_bias.shape[0])
        gain_one, shift_one, gain_two, shift_two = (sums[number, :width] for number in range(3, 7))
        entropy = sums[7, 0] / sums[7, 128]
    return (
        out.reshape(row_count, seq_len, width),
        input_grad.reshape(row_count, seq_len, width),
        query_grad,
        key_grad,
        value_grad,
        bias_grad,
        gain_one,
        shift_one,
        gain_two,
        shift_two,
        entropy.reshape(()),
    )


def solution(mesh):
    placed = (
        P(("wide", "narrow"), None, None),
        P(("wide", "narrow"), None),
        P(("wide", "narrow"), None),
        P(),
        P(),
        P(),
        P(),
        P(),
        P(),
        P(),
        P(),
        P(),
        P(None, None, "narrow"),
        P(None, "narrow", None),
        P(),
        P(),
        P(),
        P(("wide", "narrow"), None, None),
    )
    joined = mesh.shape["wide"] == 8 and mesh.shape["narrow"] == 4
    return jax.shard_map(
        functools.partial(per_device, joined),
        mesh=mesh,
        in_specs=placed,
        out_specs=(
            P(("wide", "narrow"), None, None),
            P(("wide", "narrow"), None, None),
            P(),
            P(),
            P(),
            P(),
            P(),
            P(),
            P(),
            P(),
            P(),
        ),
        check_vma=False,
    )
```

```python
import math

import jax
import jax.numpy as jnp
import functools

from jax import lax
from jax.experimental import pallas as pl
from jax.experimental.pallas import tpu as pltpu
from jax.sharding import PartitionSpec as P

D = 768
HEADS = 12
HEAD_DIM = 64
ADAPTERS = 16
BOTTLE = 48

AUG = 16
BF = jnp.bfloat16
F32 = jnp.float32
BLOCK_Q = 256
BLOCK_K = 128
UNROLL = 4
VMEM_BYTES = 64 << 20


def dot_on(left_op, right_op, left_dim, right_dim):
    return lax.dot_general(
        left_op,
        right_op,
        (((left_dim,), (right_dim,)), ((), ())),
        preferred_element_type=F32,
    )


def head_rows(part, head):
    return pl.ds(pl.multiple_of(part * D + head * HEAD_DIM, HEAD_DIM), HEAD_DIM)


def doc_starts(seg):
    return [jnp.sum((seg[...] < doc).astype(jnp.int32)) for doc in range(1, 4)]


def key_range(starts, seq, i):
    low, high = jnp.int32(0), jnp.int32(seq)
    for start in starts:
        low = jnp.where(start <= i * BLOCK_K, jnp.maximum(low, start), low)
        high = jnp.where(start >= (i + 1) * BLOCK_K, jnp.minimum(high, start), high)
    return low // BLOCK_K, (high + BLOCK_K - 1) // BLOCK_K


def over_range(starts, seq, i, body):
    low_one, high_one = key_range(starts, seq, 2 * i)
    low_two, high_two = key_range(starts, seq, 2 * i + 1)
    lax.fori_loop(low_one, jnp.minimum(low_two, high_one), body(0, BLOCK_K), 0)
    lax.fori_loop(low_two, high_one, body(0, BLOCK_Q), 0)
    lax.fori_loop(jnp.maximum(low_two, high_one), high_two, body(BLOCK_K, BLOCK_K), 0)


def attend_kernel(
    x_h, w_h, seg_h, packed_h, ctx_h, lse_h,
    x, w, seg, packed, ctx, lse, xt, qa, kt, va, m_s, o_s, in_sem, w_sem, packed_sem, ctx_sem,
):
    seq, width = x.shape

    def w_copy(part):
        columns = pl.ds(pl.multiple_of(part * width, width), width)
        return pltpu.make_async_copy(w_h.at[:, columns], w.at[:, columns], w_sem.at[part])

    def packed_copy(part):
        rows = pl.ds(pl.multiple_of(part * width, width), width)
        return pltpu.make_async_copy(packed.at[rows, :], packed_h.at[rows, :], packed_sem.at[part])

    def ctx_copies(i):
        columns = pl.ds(pl.multiple_of(i * BLOCK_Q, BLOCK_Q), BLOCK_Q)
        return (
            pltpu.make_async_copy(ctx.at[:, columns], ctx_h.at[:, columns], ctx_sem.at[0, i]),
            pltpu.make_async_copy(lse.at[:, :, columns], lse_h.at[:, :, columns], ctx_sem.at[1, i]),
        )

    seg_copy = pltpu.make_async_copy(seg_h, seg, in_sem.at[0])
    x_copy = pltpu.make_async_copy(x_h, x, in_sem.at[1])
    seg_copy.start()
    x_copy.start()
    for part in range(3):
        w_copy(part).start()
    seg_copy.wait()
    starts = doc_starts(seg)
    x_copy.wait()
    xt[...] = x[...].T

    def project(part, unused):
        w_copy(part).wait()
        rows = pl.ds(pl.multiple_of(part * width, width), width)
        packed[rows, :] = dot_on(w[:, rows], xt[...], 0, 0).astype(BF)
        packed_copy(part).start()
        return 0

    lax.fori_loop(0, 3, project, 0)
    row = lax.broadcasted_iota(jnp.int32, (AUG, seq), 0)
    same = row == seg[...]
    aug_q = jnp.where(same, 1.0, 0.0).astype(BF)
    aug_k = jnp.where((row < 4) & (~same), -1e30, 0.0).astype(BF)

    def prepare(head, unused):
        qa[head, :HEAD_DIM, :] = packed[head_rows(0, head), :] * jnp.asarray(0.125, BF)
        qa[head, HEAD_DIM:, :] = aug_q
        kt[head] = jnp.concatenate([packed[head_rows(1, head), :], aug_k], axis=0).T
        va[head, :HEAD_DIM, :] = packed[head_rows(2, head), :]
        va[head, HEAD_DIM:, :] = jnp.ones((AUG, seq), BF)
        return 0

    lax.fori_loop(0, HEADS, prepare, 0, unroll=UNROLL)

    def query_block(i, unused):
        qs = pl.ds(pl.multiple_of(i * BLOCK_Q, BLOCK_Q), BLOCK_Q)
        for h in range(HEADS):
            m_s[h] = jnp.full((8, BLOCK_Q), -1e30, F32)
            o_s[h] = jnp.zeros((HEAD_DIM + AUG, BLOCK_Q), F32)

        def part_block(start, size):
            part_qs = pl.ds(pl.multiple_of(i * BLOCK_Q + start, BLOCK_K), size)
            lanes = pl.ds(start, size)

            def key_block(j, unused):
                ks = pl.ds(pl.multiple_of(j * BLOCK_K, BLOCK_K), BLOCK_K)
                first, second = {}, {}
                lag = 4
                for t in range(HEADS + 2 * lag):
                    if t < HEADS:
                        first[t] = dot_on(kt[t, ks, :], qa[t, :, part_qs], 1, 0)
                    h = t - lag
                    if 0 <= h < HEADS:
                        tile = first.pop(h).reshape(BLOCK_K // 8, 8, size)
                        top = jnp.max(jnp.max(tile, axis=0), axis=0, keepdims=True)
                        old = m_s[h, :, lanes]
                        new = jnp.maximum(old, jnp.broadcast_to(top, (8, size)))
                        m_s[h, :, lanes] = new
                        prob = jnp.exp(tile - new[None]).reshape(BLOCK_K, size).astype(BF)
                        second[h] = (prob, jnp.exp(old - new))
                    h = t - 2 * lag
                    if 0 <= h < HEADS:
                        prob, decay = second.pop(h)
                        rows = HEAD_DIM + AUG
                        kept = (o_s[h, :, lanes].reshape(rows // 8, 8, size) * decay[None]).reshape(rows, size)
                        o_s[h, :, lanes] = kept + dot_on(va[h, :, ks], prob, 1, 0)
                return 0

            return key_block

        over_range(starts, seq, i, part_block)
        for h in range(HEADS):
            total = o_s[h, HEAD_DIM : HEAD_DIM + 1, :]
            ctx[h * HEAD_DIM : (h + 1) * HEAD_DIM, qs] = (o_s[h, :HEAD_DIM, :] * (1.0 / total)).astype(BF)
            lse[h, :, qs] = m_s[h][:1] + jnp.log(total)
        for copy in ctx_copies(i):
            copy.start()
        return 0

    lax.fori_loop(0, seq // BLOCK_Q, query_block, 0)
    for part in range(3):
        packed_copy(part).wait()
    for i in range(seq // BLOCK_Q):
        for copy in ctx_copies(i):
            copy.wait()


GROUP = 4


def attend_back_kernel(
    packed_h, inner_h, lse_h, gctx_h, seg_h, out_from, w_h, grad_row_h, input_grad_h, out_to,
    lse, seg, packed, inner, gctx, gp, w, grad_row, bounce, input_grad, qs_s, qt, dt, ka, va, dq_s, dk_s, dv_s, in_sem, out_sem,
):
    width, seq = gctx.shape
    groups = HEADS // GROUP
    group_rows = GROUP * HEAD_DIM
    loads = [
        [
            pltpu.make_async_copy(lse_h, lse, in_sem.at[groups, 0]),
            pltpu.make_async_copy(seg_h, seg, in_sem.at[groups, 1]),
            pltpu.make_async_copy(inner_h, inner, in_sem.at[groups, 2]),
        ]
    ]
    for load in loads[0]:
        load.start()
    for group in range(groups):
        pairs = [(gctx_h, gctx, 0)] + [(packed_h, packed, part) for part in range(3)]
        held = []
        for number, (source, target, part) in enumerate(pairs):
            rows = pl.ds(part * width + group * group_rows, group_rows)
            held.append(pltpu.make_async_copy(source.at[rows, :], target.at[rows, :], in_sem.at[group, number]))
            held[-1].start()
        loads.append(held)
    late = [
        pltpu.make_async_copy(source, target, out_sem.at[number])
        for number, (source, target) in enumerate(((out_from, bounce), (w_h, w), (grad_row_h, grad_row)))
    ]
    back = pltpu.make_async_copy(bounce, out_to, out_sem.at[3])

    for load in loads.pop(0):
        load.wait()
    starts = doc_starts(seg)
    row = lax.broadcasted_iota(jnp.int32, (AUG, seq), 0)
    same = row == seg[...]
    aug_q = jnp.where(same, 1.0, 0.0)
    aug_k = jnp.where(row < 4, jnp.where(same, 0.0, -1e30), jnp.where(row < 7, 1.0, 0.0)).astype(BF)
    aug_v = jnp.where(row < 3, 1.0, 0.0).astype(BF)

    def minus_rows(value, base):
        rest = -value
        rows = jnp.zeros((AUG, seq), F32)
        for step in range(3):
            piece = rest.astype(BF).astype(F32)
            rows = jnp.where(row == base + step, jnp.broadcast_to(piece, (AUG, seq)), rows)
            rest = rest - piece
        return rows

    def prepare(head, unused):
        rows = head_rows(0, head)
        scaled = packed[rows, :] * jnp.asarray(0.125, BF)
        qs_s[head] = scaled
        qt[head] = jnp.concatenate([scaled, (aug_q + minus_rows(lse[head], 4)).astype(BF)], axis=0).T
        ka[head, :HEAD_DIM, :] = packed[head_rows(1, head), :]
        ka[head, HEAD_DIM:, :] = aug_k
        va[head, :HEAD_DIM, :] = packed[head_rows(2, head), :]
        va[head, HEAD_DIM:, :] = aug_v
        grad = gctx[rows, :]
        dt[head] = jnp.concatenate([grad, minus_rows(inner[head], 0).astype(BF)], axis=0).T
        dq_s[head] = jnp.zeros((HEAD_DIM, seq), F32)
        return 0

    for group in range(groups):
        for load in loads[group]:
            load.wait()
        lax.fori_loop(group * GROUP, (group + 1) * GROUP, prepare, 0, unroll=UNROLL)
    for load in late:
        load.start()

    def outer(i, unused):
        ks = pl.ds(pl.multiple_of(i * BLOCK_Q, BLOCK_Q), BLOCK_Q)
        for h in range(HEADS):
            dk_s[h] = jnp.zeros((HEAD_DIM, BLOCK_Q), F32)
            dv_s[h] = jnp.zeros((HEAD_DIM, BLOCK_Q), F32)

        def part_block(start, size):
            part_ks = pl.ds(pl.multiple_of(i * BLOCK_Q + start, BLOCK_K), size)
            lanes = pl.ds(start, size)

            def inner_block(j, unused):
                qs = pl.ds(pl.multiple_of(j * BLOCK_K, BLOCK_K), BLOCK_K)
                first, second = {}, {}
                lag = 4
                for t in range(HEADS + 2 * lag):
                    if t < HEADS:
                        first[t] = (
                            dot_on(qt[t, qs, :], ka[t, :, part_ks], 1, 0),
                            dot_on(dt[t, qs, :], va[t, :, part_ks], 1, 0),
                        )
                    h = t - lag
                    if 0 <= h < HEADS:
                        logits, grad = first.pop(h)
                        prob = jnp.exp(logits)
                        second[h] = (prob.astype(BF), (prob * grad).astype(BF))
                    h = t - 2 * lag
                    if 0 <= h < HEADS:
                        prob, grad = second.pop(h)
                        dv_s[h, :, lanes] += dot_on(gctx[h * HEAD_DIM : (h + 1) * HEAD_DIM, qs], prob, 1, 0)
                        dk_s[h, :, lanes] += dot_on(qs_s[h, :, qs], grad, 1, 0)
                        dq_s[h, :, qs] += dot_on(packed[D + h * HEAD_DIM : D + (h + 1) * HEAD_DIM, part_ks], grad, 1, 1)
                return 0

            return inner_block

        over_range(starts, seq, i, part_block)
        for h in range(HEADS):
            gp[D + h * HEAD_DIM : D + (h + 1) * HEAD_DIM, ks] = dk_s[h].astype(BF)
            gp[2 * D + h * HEAD_DIM : 2 * D + (h + 1) * HEAD_DIM, ks] = dv_s[h].astype(BF)
        return 0

    lax.fori_loop(0, seq // BLOCK_Q, outer, 0)

    def finish(head, unused):
        gp[head_rows(0, head), :] = (dq_s[head] * 0.125).astype(BF)
        return 0

    late[0].wait()
    back.start()
    lax.fori_loop(0, HEADS, finish, 0)
    late[1].wait()
    late[2].wait()
    outs = []

    def leave(step, part):
        rows = pl.ds(step * BLOCK_Q, BLOCK_Q)
        input_grad[rows, :] = (grad_row[rows, :] + part).astype(BF)
        outs.append(
            pltpu.make_async_copy(input_grad.at[rows, :], input_grad_h.at[rows, :], out_sem.at[4 + step])
        )
        outs[-1].start()

    staged(
        seq // BLOCK_Q,
        lambda step: dot_on(gp[:, pl.ds(step * BLOCK_Q, BLOCK_Q)], w[...], 0, 1),
        leave,
    )
    back.wait()
    for out in outs:
        out.wait()


def in_vmem():
    return pl.BlockSpec(memory_space=pltpu.VMEM)


def anywhere():
    return pl.BlockSpec(memory_space=pl.ANY)


def attend(x, w, seg):
    seq = x.shape[0]
    return pl.pallas_call(
        attend_kernel,
        in_specs=[anywhere() for unused in range(3)],
        out_specs=[anywhere() for unused in range(3)],
        out_shape=(
            jax.ShapeDtypeStruct((3 * D, seq), BF),
            jax.ShapeDtypeStruct((D, seq), BF),
            jax.ShapeDtypeStruct((HEADS, 1, seq), F32),
        ),
        scratch_shapes=[
            pltpu.VMEM((seq, D), BF),
            pltpu.VMEM((D, 3 * D), BF),
            pltpu.VMEM((1, seq), jnp.int32),
            pltpu.VMEM((3 * D, seq), BF),
            pltpu.VMEM((D, seq), BF),
            pltpu.VMEM((HEADS, 1, seq), F32),
            pltpu.VMEM((D, seq), BF),
            pltpu.VMEM((HEADS, HEAD_DIM + AUG, seq), BF),
            pltpu.VMEM((HEADS, seq, HEAD_DIM + AUG), BF),
            pltpu.VMEM((HEADS, HEAD_DIM + AUG, seq), BF),
            pltpu.VMEM((HEADS, 8, BLOCK_Q), F32),
            pltpu.VMEM((HEADS, HEAD_DIM + AUG, BLOCK_Q), F32),
            pltpu.SemaphoreType.DMA((2,)),
            pltpu.SemaphoreType.DMA((3,)),
            pltpu.SemaphoreType.DMA((3,)),
            pltpu.SemaphoreType.DMA((2, seq // BLOCK_Q)),
        ],
        name="attend",
        compiler_params=pltpu.CompilerParams(vmem_limit_bytes=60 << 20),
    )(x, w, seg)


def attend_back(packed, inner, lse, gctx, seg, out, w, grad_row):
    seq = packed.shape[1]
    aug = HEAD_DIM + AUG
    return pl.pallas_call(
        attend_back_kernel,
        in_specs=[anywhere() for unused in range(8)],
        out_specs=[anywhere(), anywhere()],
        out_shape=(jax.ShapeDtypeStruct((seq, D), BF), jax.ShapeDtypeStruct((seq, D), BF)),
        scratch_shapes=[
            pltpu.VMEM((HEADS, 1, seq), F32),
            pltpu.VMEM((1, seq), jnp.int32),
            pltpu.VMEM((3 * D, seq), BF),
            pltpu.VMEM((HEADS, 1, seq), F32),
            pltpu.VMEM((D, seq), BF),
            pltpu.VMEM((3 * D, seq), BF),
            pltpu.VMEM((D, 3 * D), BF),
            pltpu.VMEM((seq, D), F32),
            pltpu.VMEM((seq, D), BF),
            pltpu.VMEM((seq, D), BF),
            pltpu.VMEM((HEADS, HEAD_DIM, seq), BF),
            pltpu.VMEM((HEADS, seq, aug), BF),
            pltpu.VMEM((HEADS, seq, aug), BF),
            pltpu.VMEM((HEADS, aug, seq), BF),
            pltpu.VMEM((HEADS, aug, seq), BF),
            pltpu.VMEM((HEADS, HEAD_DIM, seq), F32),
            pltpu.VMEM((HEADS, HEAD_DIM, BLOCK_Q), F32),
            pltpu.VMEM((HEADS, HEAD_DIM, BLOCK_Q), F32),
            pltpu.SemaphoreType.DMA((HEADS // GROUP + 1, 5)),
            pltpu.SemaphoreType.DMA((4 + seq // BLOCK_Q,)),
        ],
        name="attend_back",
        cost_estimate=pl.CostEstimate(flops=30_000_000_000, bytes_accessed=20_000_000, transcendentals=0),
        compiler_params=pltpu.CompilerParams(vmem_limit_bytes=62 << 20),
    )(packed, inner, lse, gctx, seg, out, w, grad_row)


def pieces(value):
    high = value.astype(BF)
    return high, (value - high.astype(F32)).astype(BF)


def normalize(values):
    centre = values - jnp.mean(values, axis=-1, keepdims=True)
    factor = lax.rsqrt(jnp.mean(centre * centre, axis=-1, keepdims=True) + 1e-06)
    return centre * factor, factor


def norm_back(scaled, unit_vals, factor):
    return factor * (
        scaled
        - jnp.mean(scaled, axis=-1, keepdims=True)
        - unit_vals * jnp.mean(scaled * unit_vals, axis=-1, keepdims=True)
    )


def gelu_doubled(values):
    rising = lax.erf(values * math.sqrt(0.5)) + 1.0
    low = values.astype(BF)
    bell = jnp.exp2(low * low * jnp.asarray(-0.5 * math.log2(math.e), BF))
    steep = low * jnp.asarray(2.0 / math.sqrt(2.0 * math.pi), BF)
    return (values * rising).astype(BF), rising.astype(BF) + steep * bell


def fold_rows(values):
    rows, columns = values.shape
    return jnp.sum(values.reshape(rows // 8, 8, columns), axis=0)


def staged(count, product, finish, between=None):
    held = {}
    for step in range(count + 1):
        if between is not None and step == count // 2:
            between()
        if step < count:
            held[step] = product(step)
        if step >= 1:
            finish(step - 1, held.pop(step - 1))


MESH = pl.DeviceIdType.MESH
PLANE = 4
DEPTH = 4
OWN_ROWS = 24
SLABS = 2 * 2 * DEPTH + 2
PLANE_ROWS = 96
CORE_ROWS = 384


def place():
    wide, narrow = lax.axis_index("wide"), lax.axis_index("narrow")
    return wide // 2, lax.rem(wide, 2), narrow // 2, lax.rem(narrow, 2)


def device(z, x, y, core):
    return (z * 2 + x, y * 2 + core)


def plane_mate(step):
    z, x, y, core = place()
    return device(z, jnp.bitwise_xor(x, step // 2), jnp.bitwise_xor(y, step % 2), core)


def depth_mate(step):
    z, x, y, core = place()
    return device(lax.rem(z + step, DEPTH), x, y, core)


def core_mate():
    z, x, y, core = place()
    return device(z, x, y, 1 - core)


def remote(source, target, sems, slot, mate):
    return pltpu.make_async_remote_copy(
        src_ref=source,
        dst_ref=target,
        send_sem=sems.at[0, slot],
        recv_sem=sems.at[1, slot],
        device_id=mate,
        device_id_type=MESH,
    )


def greet(mates):
    barrier = pltpu.get_barrier_semaphore()
    for mate in mates:
        pl.semaphore_signal(barrier, inc=1, device_id=mate, device_id_type=MESH)
    return lambda: pl.semaphore_wait(barrier, len(mates))


class Scatter:
    def __init__(self, which, square, kept, send, near, plane, small_send, small, gathered, sems):
        self.which, self.square, self.kept = which, square, kept
        self.send, self.near, self.plane = send, near, plane
        self.small_send, self.small, self.gathered, self.sems = small_send, small, gathered, sems
        z, x, y, core = place()
        self.z, self.spot, self.core = z, x * 2 + y, core
        self.copies = []

    def rows(self, start, count):
        return pl.ds(pl.multiple_of(start, 8), count)

    def finish(self):
        for copy in self.copies:
            copy.wait()
        self.copies = []

    def go(self, source, target, slot, mate):
        copy = remote(source, target, self.sems, self.which * 16 + slot, mate)
        copy.start()
        self.copies.append(copy)

    def to_core(self):
        self.go(self.send.at[self.which], self.near.at[self.which], 0, core_mate())

    def to_plane(self):
        self.finish()
        for q in range(PLANE):
            rows = pl.ds(q * PLANE_ROWS, PLANE_ROWS)
            total = self.square[rows, :] + self.near[self.which, q].astype(F32)
            self.square[rows, :] = total
            self.send[self.which, q] = total.astype(BF)
        self.kept[self.which] = self.square[self.rows(self.spot * PLANE_ROWS, PLANE_ROWS), :]
        for step in range(1, PLANE):
            spot = jnp.bitwise_xor(self.spot, step)
            self.go(self.send.at[self.which, spot], self.plane.at[self.which, step - 1], step, plane_mate(step))

    def to_depth(self):
        self.finish()
        total = self.kept[self.which]
        for step in range(1, PLANE):
            total = total + self.plane[self.which, step - 1].astype(F32)
        self.kept[self.which] = total
        for k in range(DEPTH):
            self.small_send[self.which, k] = total[k * OWN_ROWS : (k + 1) * OWN_ROWS, :].astype(BF)
        for step in range(1, DEPTH):
            spot = lax.rem(self.z + step, DEPTH)
            self.go(
                self.small_send.at[self.which, spot],
                self.small.at[self.which, step - 1],
                PLANE - 1 + step,
                depth_mate(step),
            )

    def share(self, last=None):
        self.finish()
        total = self.kept[self.which, self.rows(self.z * OWN_ROWS, OWN_ROWS), :]
        for step in range(1, DEPTH):
            total = total + self.small[self.which, step - 1].astype(F32)
        if last is not None:
            high, rest = pieces(total)
            total = dot_on(high, last, 1, 0) + dot_on(rest, last, 1, 0)
        mine = self.gathered.at[self.slab(self.z)]
        mine[...] = total.astype(BF)
        for step in range(1, DEPTH):
            self.go(mine, mine, PLANE + DEPTH - 2 + step, depth_mate(step))

    def slab(self, z):
        return (self.core * 2 + self.which) * DEPTH + z

    def pair(self):
        arriving, self.copies = self.copies, []
        for step in range(DEPTH):
            if step:
                arriving[step - 1].wait()
            spot = lax.rem(self.z - step + DEPTH, DEPTH)
            chunk = self.gathered.at[self.slab(spot)]
            self.go(chunk, chunk, PLANE + 2 * DEPTH - 2 + step, core_mate())


ROWS_AT_ONCE = 256
HIDDEN_AT_ONCE = 512
HIDDEN_ROWS = 512


def middle_kernel(
    joined, x_h, g_h, ctx_h, wo_h, win_h, wout_h, down_h, up_h, wq_h, wk_h, wv_h,
    bias_h, gain_one_h, shift_one_h, gain_two_h, shift_two_h, mask_h,
    out_h, gr_h, gctx_h, v_h, gg_h, sums_h, inner_h,
    x, g, ctx, wo, win, wout, bank, wq, wk, wv,
    unit_one, unit_two, bottle, guide, total, act, slope, low, factor, mix, score_grads,
    v_s, gg_s, sums_part, vectors, mask, sums_out, inner, in_sem, vector_sem, out_sem, *links,
):
    seq, width = x.shape
    blocks = seq // ROWS_AT_ONCE
    mix_scale = 1.0 / math.sqrt(D)
    vector_loads = [
        pltpu.make_async_copy(source, vectors.at[number, pl.ds(0, width)], vector_sem.at[number])
        for number, source in enumerate((gain_one_h, shift_one_h, gain_two_h, shift_two_h))
    ] + [
        pltpu.make_async_copy(
            bias_h.at[pl.ds(number * 1024, 1024)], vectors.at[4 + number], vector_sem.at[4 + number]
        )
        for number in range(win.shape[1] // 1024)
    ] + [pltpu.make_async_copy(mask_h, mask, vector_sem.at[4 + win.shape[1] // 1024])]
    loads = {}
    names = ("down", "up", "ctx", "wo", "x", "win", "wout", "wq", "wk", "g", "wv")
    sources = (down_h, up_h, ctx_h, wo_h, x_h, win_h, wout_h, wq_h, wk_h, g_h, wv_h)
    targets = (bank.at[0], bank.at[1], ctx, wo, x, win, wout, wq, wk, g, wv)
    gain_one, shift_one, gain_two, shift_two = (vectors.at[number : number + 1, :width] for number in range(4))
    if joined:
        (
            kept, send, near, plane, small_send, small, gathered,
            sums_near, sums_depth, sums_mid, link_sems, bank_sems, sums_sems,
        ) = links
        arrived = greet(
            [core_mate()]
            + [plane_mate(step) for step in range(1, PLANE)]
            + [depth_mate(step) for step in range(1, DEPTH)]
        )
        spot = lax.axis_index("narrow")
        shard = down_h.shape[0]

        own_rows = pl.ds(pl.multiple_of(spot * shard, 16), shard)
        targets = (bank.at[0, own_rows, :], bank.at[1, own_rows, :]) + targets[2:]
    for number, name in enumerate(names):
        loads[name] = pltpu.make_async_copy(sources[number], targets[number], in_sem.at[number])
    for name in names[:5]:
        loads[name].start()
    for load in vector_loads:
        load.start()
    for name in names[5:]:
        loads[name].start()

    def rows_of(step):
        return pl.ds(step * ROWS_AT_ONCE, ROWS_AT_ONCE)

    t_one, t_two, t_three, t_four = (pl.ds(k * width, width) for k in range(4))
    down, up = 0, 1
    column = lax.broadcasted_iota(jnp.int32, (ADAPTERS, width), 1)
    owner = lax.rem(column, ADAPTERS)
    chosen = jnp.where(
        owner == lax.broadcasted_iota(jnp.int32, (ADAPTERS, width), 0), 1.0, 0.0
    ).astype(BF)

    chosen_twice = jnp.concatenate([chosen, chosen], axis=0)

    def per_adapter(values):
        return dot_on(chosen, values.astype(BF), 1, 1)

    def per_unit(values):
        return dot_on(jnp.concatenate(pieces(values), axis=0), chosen_twice, 0, 0)

    loads["ctx"].wait()
    loads["wo"].wait()

    def finish_first(step, part):
        rows = rows_of(step)
        if step == 0:
            loads["x"].wait()
            for load in vector_loads:
                load.wait()
        unit, scale = normalize(x[rows, :].astype(F32) + part)
        unit_one[rows, :] = unit
        factor[rows, 0:1] = scale
        low[rows, :] = (unit * gain_one[...] + shift_one[...]).astype(BF)

    if joined:
        arrived()
        loads["down"].wait()
        loads["up"].wait()

        def bank_part(which, index, slot, mate):
            rows = bank.at[which, pl.ds(pl.multiple_of(index * shard, 16), shard), :]
            return remote(rows, rows, bank_sems, slot, mate)

        far_copies = [bank_part(which, spot, which, plane_mate(1)) for which in (down, up)]
        near_copies = [bank_part(which, spot, 2 + which, core_mate()) for which in (down, up)]
        for copy in far_copies + near_copies:
            copy.start()

        def forward(which):
            far_copies[which].wait()
            far_copies[which] = bank_part(which, jnp.bitwise_xor(spot, 2), 4 + which, core_mate())
            far_copies[which].start()

        def whole_bank(which):
            far_copies[which].wait()
            near_copies[which].wait()
    staged(blocks, lambda step: dot_on(ctx[:, rows_of(step)], wo[...], 0, 0), finish_first)

    loads["win"].wait()

    def hidden(chunk, unused):
        columns = pl.ds(pl.multiple_of(chunk * HIDDEN_AT_ONCE, HIDDEN_AT_ONCE), HIDDEN_AT_ONCE)
        per_row = 1024 // HIDDEN_AT_ONCE
        lanes = pl.ds(pl.multiple_of(lax.rem(chunk, per_row) * HIDDEN_AT_ONCE, HIDDEN_AT_ONCE), HIDDEN_AT_ONCE)
        bias = vectors[pl.ds(4 + chunk // per_row, 1), lanes]

        def rows_in(step):
            return pl.ds(step * HIDDEN_ROWS, HIDDEN_ROWS)

        def finish(step, part):
            rows = rows_in(step)
            value, rising = gelu_doubled(part + bias)
            act[rows, columns] = value
            slope[rows, columns] = rising

        staged(seq // HIDDEN_ROWS, lambda step: dot_on(low[rows_in(step), :], win[:, columns], 1, 0), finish)
        return 0

    lax.fori_loop(0, win.shape[1] // HIDDEN_AT_ONCE, hidden, 0)
    loads["wout"].wait()
    if joined:
        forward(down)

    def second(half, unused):
        def rows_in(step):
            start = half * (seq // 2) + step * ROWS_AT_ONCE
            return pl.ds(pl.multiple_of(start, ROWS_AT_ONCE), ROWS_AT_ONCE)

        def finish(step, part):
            rows = rows_in(step)
            unit, scale = normalize(unit_one[rows, :] * gain_one[...] + shift_one[...] + 0.5 * part)
            unit_two[rows, :] = unit
            factor[rows, 1:2] = scale
            low[rows, :] = (unit * gain_two[...] + shift_two[...]).astype(BF)

        staged(blocks // 2, lambda step: dot_on(act[rows_in(step), :], wout[...], 1, 0), finish)
        return 0

    lax.fori_loop(0, 2, second, 0)

    def h_two(rows):
        return unit_two[rows, :] * gain_two[...] + shift_two[...]

    def keep(target, place, size):
        def finish(step, part):
            target[pl.ds(step * size, size), place] = part.astype(BF)

        return finish

    everything = pl.ds(0, width)
    if joined:
        forward(up)
        whole_bank(down)
    else:
        loads["down"].wait()
        loads["up"].wait()

    def finish_down(step, part):
        rows = rows_of(step)
        rising = 0.5 * lax.erf(part * math.sqrt(0.5)) + 0.5
        part_low = part.astype(BF)
        bell = jnp.exp2(part_low * part_low * jnp.asarray(-0.5 * math.log2(math.e), BF))
        bottle[rows, :] = part * rising
        act[rows, t_four] = rising.astype(BF) + part_low * jnp.asarray(1.0 / math.sqrt(2.0 * math.pi), BF) * bell

    staged(blocks, lambda step: dot_on(low[rows_of(step), :], bank[down], 1, 1), finish_down)
    if joined:
        whole_bank(up)
    loads["wk"].wait()
    third = width // 3
    staged(3, lambda step: dot_on(bank[up, pl.ds(step * third, third), :], wk[...], 1, 0), keep(act, t_one, third))
    loads["wq"].wait()
    through = act.at[:width, t_one]
    staged(3, lambda step: dot_on(wq[pl.ds(step * third, third), :], through[...], 1, 1), keep(wk, everything, third))

    def finish_guide(step, part):
        rows = rows_of(step)
        guide[rows, :] = part
        mix[:, rows] = per_adapter(bottle[rows, :] * part)

    staged(blocks, lambda step: dot_on(low[rows_of(step), :], wk[...], 1, 0), finish_guide)
    scores = mix[...] * mix_scale
    shifted = scores - jnp.max(scores, axis=0, keepdims=True)
    exponents = jnp.exp(shifted)
    total_exponent = jnp.sum(exponents, axis=0, keepdims=True)
    weights = exponents / total_exponent
    entropies = -jnp.sum(weights * (shifted - jnp.log(total_exponent)), axis=0, keepdims=True)
    mix[...] = weights

    def finish_mix(step, part):
        rows = rows_of(step)
        act[rows, t_one] = (part * bottle[rows, :]).astype(BF)

    staged(blocks, lambda step: per_unit(mix[:, rows_of(step)]), finish_mix)
    real = mask[...].astype(F32)
    ent = jnp.sum(entropies * real, axis=1, keepdims=True)
    lane = lax.broadcasted_iota(jnp.int32, (1, 1024), 1)
    sums_out[7:8, :] = jnp.where(lane < 128, ent, jnp.sum(real, axis=1, keepdims=True))
    sums_out[3:7, width:] = jnp.zeros((4, 1024 - width), F32)

    def finish_update(step, part):
        rows = rows_of(step)
        x[rows, :] = (h_two(rows) + part).astype(BF)

    staged(blocks, lambda step: dot_on(act[rows_of(step), t_one], bank[up], 1, 0), finish_update)

    loads["g"].wait()

    def over_tokens(left, right, target):
        def product(step):
            return dot_on(left(pl.ds(step * third, third)), right, 0, 0)

        def finish(step, part):
            target[pl.ds(step * third, third), :] = part

        staged(3, product, finish)

    def halves(left, base, right, target, which):
        core = place()[3]

        def product(step):
            start = base + (core if step else 1 - core) * CORE_ROWS
            return dot_on(left[:, pl.ds(pl.multiple_of(start, 128), CORE_ROWS)], right, 0, 0)

        def finish(step, part):
            if step:
                target[...] = part
            else:
                for q in range(PLANE):
                    send[which, q] = part[q * PLANE_ROWS : (q + 1) * PLANE_ROWS, :].astype(BF)

        finish(0, product(0))
        (value_sum, joint_sum)[which].to_core()
        finish(1, product(1))

    if joined:
        value_sum, joint_sum = (
            Scatter(k, v_s, kept, send, near, plane, small_send, small, gathered, link_sems) for k in range(2)
        )
        halves(x, 0, g[...], v_s, 0)
    else:
        over_tokens(lambda cols: x[:, cols], g[...], v_s)
    if not joined:
        v_out = pltpu.make_async_copy(v_s, v_h, out_sem.at[0])
        v_out.start()

    loads["wv"].wait()

    def finish_blend(step, part):
        rows = rows_of(step)
        total[rows, :] = g[rows, :].astype(F32) + part
        act[rows, t_one] = part.astype(BF)

    staged(blocks, lambda step: dot_on(g[rows_of(step), :], wv[...], 1, 1), finish_blend)

    def finish_mixed(step, part):
        rows = rows_of(step)
        act[rows, t_one] = part.astype(BF)
        score_grads[:, rows] = per_adapter(part * bottle[rows, :])

    staged(blocks, lambda step: dot_on(act[rows_of(step), t_one], bank[up], 1, 1), finish_mixed, value_sum.to_plane if joined else None)
    weights = mix[...]
    grad_weights = score_grads[...]
    mean_grad = jnp.sum(grad_weights * weights, axis=0, keepdims=True)
    score_grads[...] = weights * (grad_weights - mean_grad) * mix_scale

    def finish_units(step, part):
        rows = rows_of(step)
        mixed, score_term = part
        grad_bottle = act[rows, t_one].astype(F32) * mixed + score_term * guide[rows, :]
        act[rows, t_three] = (grad_bottle * act[rows, t_four].astype(F32)).astype(BF)
        act[rows, t_one] = (score_term * bottle[rows, :]).astype(BF)

    staged(
        blocks,
        lambda step: (per_unit(mix[:, rows_of(step)]), per_unit(score_grads[:, rows_of(step)])),
        finish_units,
    )
    if joined:
        halves(low, 0, act[:, t_one], v_s, 1)
    else:
        over_tokens(lambda cols: low[:, cols], act[:, t_one], gg_s)
    if not joined:
        gg_out = pltpu.make_async_copy(gg_s, gg_h, out_sem.at[2])
        gg_out.start()
    partial = [jnp.zeros((8, width), F32) for unused in range(4)]

    def finish_two(step, part):
        rows = rows_of(step)
        grad = total[rows, :] + part
        unit = unit_two[rows, :]
        partial[0] = partial[0] + fold_rows(grad * unit)
        partial[1] = partial[1] + fold_rows(grad)
        back = norm_back(grad * gain_two[...], unit, factor[rows, 1:2])
        total[rows, :] = back
        low[rows, :] = (0.5 * back).astype(BF)

    staged(
        blocks,
        lambda step: dot_on(act[rows_of(step), t_three], bank[down], 1, 0)
        + dot_on(act[rows_of(step), t_one], wk[...], 1, 1),
        finish_two,
        joint_sum.to_plane if joined else None,
    )

    if joined:
        value_sum.to_depth()

    def hidden_back(chunk, unused):
        columns = pl.ds(pl.multiple_of(chunk * HIDDEN_AT_ONCE, HIDDEN_AT_ONCE), HIDDEN_AT_ONCE)
        held = [jnp.zeros((8, HIDDEN_AT_ONCE), F32)]

        def rows_in(step):
            return pl.ds(step * HIDDEN_ROWS, HIDDEN_ROWS)

        def finish(step, part):
            rows = rows_in(step)
            grad = (part * slope[rows, columns].astype(F32)).astype(BF)
            act[rows, columns] = grad
            held[0] = held[0] + fold_rows(grad.astype(F32))

        staged(seq // HIDDEN_ROWS, lambda step: dot_on(low[rows_in(step), :], wout[columns, :], 1, 1), finish)
        sums_part[chunk] = held[0]
        return 0

    lax.fori_loop(0, win.shape[1] // HIDDEN_AT_ONCE, hidden_back, 0)
    for number in range(win.shape[1] // HIDDEN_AT_ONCE):
        at, lanes = divmod(number * HIDDEN_AT_ONCE, 1024)
        sums_out[at : at + 1, pl.ds(lanes, HIDDEN_AT_ONCE)] = jnp.sum(sums_part[number], axis=0, keepdims=True)
    sums_out[5:6, :width] = jnp.sum(partial[0], axis=0, keepdims=True)
    sums_out[6:7, :width] = jnp.sum(partial[1], axis=0, keepdims=True)
    if joined:
        value_sum.share()
        joint_sum.to_depth()

    def first_back(half, carried):
        def rows_in(step):
            start = half * (seq // 2) + step * ROWS_AT_ONCE
            return pl.ds(pl.multiple_of(start, ROWS_AT_ONCE), ROWS_AT_ONCE)

        held = list(carried)

        def finish(step, part):
            rows = rows_in(step)
            grad = total[rows, :] + part
            unit = unit_one[rows, :]
            held[0] = held[0] + fold_rows(grad * unit)
            held[1] = held[1] + fold_rows(grad)
            back = norm_back(grad * gain_one[...], unit, factor[rows, 0:1])
            total[rows, :] = back
            low[rows, :] = back.astype(BF)

        staged(blocks // 2, lambda step: dot_on(act[rows_in(step), :], win[...], 1, 1), finish)
        return tuple(held)

    zero = jnp.zeros((8, width), F32)
    gain_sum, shift_sum = lax.fori_loop(0, 2, first_back, (zero, zero))
    sums_out[3:4, :width] = jnp.sum(gain_sum, axis=0, keepdims=True)
    sums_out[4:5, :width] = jnp.sum(shift_sum, axis=0, keepdims=True)
    if joined:
        near_copy = remote(sums_out, sums_near, sums_sems, 0, core_mate())
        near_copy.start()
        value_sum.pair()
        joint_sum.share(bank[up])
    gr_copy = pltpu.make_async_copy(total, gr_h, out_sem.at[3])
    gr_copy.start()

    def finish_ctx(step, part):
        grad = part.astype(BF)
        for number in range(third // HEAD_DIM):
            head = step * (third // HEAD_DIM) + number
            value = ctx[head * HEAD_DIM : (head + 1) * HEAD_DIM, :].astype(F32)
            product = grad[number * HEAD_DIM : (number + 1) * HEAD_DIM, :].astype(F32) * value
            inner[head] = jnp.sum(product, axis=0, keepdims=True)
        ctx[pl.ds(step * third, third), :] = grad

    staged(3, lambda step: dot_on(wo[pl.ds(step * third, third), :], low[...], 1, 1), finish_ctx)
    gctx_copy = pltpu.make_async_copy(ctx, gctx_h, out_sem.at[4])
    gctx_copy.start()
    inner_copy = pltpu.make_async_copy(inner, inner_h, out_sem.at[6])
    inner_copy.start()
    if joined:
        near_copy.wait()
        sums_mid[...] = sums_out[...] + sums_near[...]
        depth_copies = [
            remote(sums_mid, sums_depth.at[step - 1], sums_sems, step, depth_mate(step)) for step in range(1, DEPTH)
        ]
        for copy in depth_copies:
            copy.start()
        value_sum.finish()

    def finish_out(step, part):
        rows = rows_of(step)
        x[rows, :] = (h_two(rows) + part).astype(BF)

    staged(blocks, lambda step: dot_on(x[rows_of(step), :], wv[...], 1, 0), finish_out)
    out_copy = pltpu.make_async_copy(x, out_h, out_sem.at[1])
    out_copy.start()
    if joined:
        joint_sum.pair()
        for copy in depth_copies:
            copy.wait()
        rest = sums_mid[...] + sums_depth[0] + sums_depth[1] + sums_depth[2]
        parts = []
        for unused in range(3):
            parts.append(rest.astype(BF).astype(F32))
            rest = rest - parts[-1]
        parts = jnp.concatenate(parts, axis=0).astype(BF)
        gathered[SLABS - 2] = parts[:, :width]
        gathered[SLABS - 1] = jnp.zeros((OWN_ROWS, width), BF)
        gathered[SLABS - 1, :, : 1024 - width] = parts[:, width:]
        joint_sum.finish()
        v_out = pltpu.make_async_copy(gathered, v_h, out_sem.at[0])
        v_out.start()
    else:
        sums_copy = pltpu.make_async_copy(sums_out, sums_h, out_sem.at[5])
        sums_copy.start()
        gg_out.wait()
        sums_copy.wait()
    v_out.wait()
    out_copy.wait()
    gr_copy.wait()
    gctx_copy.wait()
    inner_copy.wait()


def middle(joined, x, g, ctx, wo, win, wout, down, up, wq, wk, wv, bias, gain_one, shift_one, gain_two, shift_two, mask):
    seq, width = x.shape
    hidden = win.shape[1]
    token_low = pltpu.VMEM((seq, width), BF)
    token_wide = pltpu.VMEM((seq, width), F32)
    square = pltpu.VMEM((width, width), BF)
    sum_square = pltpu.VMEM((CORE_ROWS if joined else width, width), F32)
    links = [
        pltpu.VMEM((2, PLANE_ROWS, width), F32),
        pltpu.VMEM((2, PLANE, PLANE_ROWS, width), BF),
        pltpu.VMEM((2, PLANE, PLANE_ROWS, width), BF),
        pltpu.VMEM((2, PLANE - 1, PLANE_ROWS, width), BF),
        pltpu.VMEM((2, DEPTH, OWN_ROWS, width), BF),
        pltpu.VMEM((2, DEPTH - 1, OWN_ROWS, width), BF),
        pltpu.VMEM((SLABS, OWN_ROWS, width), BF),
        pltpu.VMEM((8, 1024), F32),
        pltpu.VMEM((DEPTH - 1, 8, 1024), F32),
        pltpu.VMEM((8, 1024), F32),
        pltpu.SemaphoreType.DMA((2, 32)),
        pltpu.SemaphoreType.DMA((2, 6)),
        pltpu.SemaphoreType.DMA((2, DEPTH)),
    ]
    return pl.pallas_call(
        functools.partial(middle_kernel, joined),
        in_specs=[anywhere() for unused in range(17)],
        out_specs=[anywhere() for unused in range(7)],
        out_shape=(
            jax.ShapeDtypeStruct((seq, width), BF),
            jax.ShapeDtypeStruct((seq, width), F32),
            jax.ShapeDtypeStruct((width, seq), BF),
            jax.ShapeDtypeStruct((SLABS, OWN_ROWS, width), BF)
            if joined
            else jax.ShapeDtypeStruct((width, width), F32),
            jax.ShapeDtypeStruct((8, 128) if joined else (width, width), F32),
            jax.ShapeDtypeStruct((8, 128 if joined else 1024), F32),
            jax.ShapeDtypeStruct((HEADS, 1, seq), F32),
        ),
        scratch_shapes=[
            token_low, token_low, pltpu.VMEM((width, seq), BF),
            square, pltpu.VMEM((width, hidden), BF), pltpu.VMEM((hidden, width), BF),
            pltpu.VMEM((2, width, width), BF), square, square, square,
            token_wide, token_wide, token_wide, token_wide, token_wide,
            pltpu.VMEM((seq, hidden), BF), pltpu.VMEM((seq, hidden), BF), token_low,
            pltpu.VMEM((seq, 2), F32), pltpu.VMEM((ADAPTERS, seq), F32), pltpu.VMEM((ADAPTERS, seq), F32),
            sum_square, pltpu.VMEM((8, 128) if joined else (width, width), F32),
            pltpu.VMEM((hidden // HIDDEN_AT_ONCE, 8, HIDDEN_AT_ONCE), F32),
            pltpu.VMEM((8, 1024), F32), pltpu.VMEM((1, seq), jnp.int32), pltpu.VMEM((8, 1024), F32),
            pltpu.VMEM((HEADS, 1, seq), F32),
            pltpu.SemaphoreType.DMA((11,)),
            pltpu.SemaphoreType.DMA((8,)), pltpu.SemaphoreType.DMA((7,)),
        ]
        + (links if joined else []),
        name="middle",
        compiler_params=pltpu.CompilerParams(
            vmem_limit_bytes=VMEM_BYTES, **(dict(collective_id=0, has_side_effects=True) if joined else {})
        ),
    )(x, g, ctx, wo, win, wout, down, up, wq, wk, wv, bias, gain_one, shift_one, gain_two, shift_two, mask)

def products_kernel(
    mine_h, first_h, second_h, third_h, wk_h, wq_h,
    value_h, query_h, key_h, bias_h, gain_one_h, shift_one_h, gain_two_h, shift_two_h, entropy,
    sums, held, wk, wq, square, joint, low, in_sem, out_sem,
):
    width = wk.shape[0]
    z, x, y, core = place()
    loads = [
        pltpu.make_async_copy(source, target, in_sem.at[number])
        for number, (source, target) in enumerate(
            [(source, held.at[step]) for step, source in enumerate((mine_h, first_h, second_h, third_h))]
            + [(wk_h, wk), (wq_h, wq)]
        )
    ]
    for load in loads:
        load.start()
    outs = []

    def leave(source, target):
        outs.append(pltpu.make_async_copy(source, target, out_sem.at[len(outs)]))
        outs[-1].start()

    for load in loads[:PLANE]:
        load.wait()

    def unpack(which, target):
        for step in range(PLANE):
            base = jnp.bitwise_xor(x * 2 + y, step) * PLANE_ROWS
            for side in range(2):
                for depth in range(DEPTH):
                    start = pl.multiple_of(base + side * CORE_ROWS + depth * OWN_ROWS, 8)
                    slab = (side * 2 + which) * DEPTH + depth
                    target[pl.ds(start, OWN_ROWS), :] = held[step, slab].astype(F32)

    unpack(0, square.at[0])
    leave(square.at[0], value_h)
    totals = [
        sum(held[step, SLABS - 2 + part].astype(F32) for step in range(PLANE)).reshape(3, 8, width)
        for part in range(2)
    ]
    wide_total, rest_total = ((total[0] + total[1]) + total[2] for total in totals)
    sums[:, :width] = wide_total
    sums[:, width:] = rest_total[:, : 1024 - width]
    for number in range(bias_h.shape[0] // 1024):
        leave(sums.at[number], bias_h.at[pl.ds(number * 1024, 1024)])
    for number, target in enumerate((gain_one_h, shift_one_h, gain_two_h, shift_two_h)):
        leave(sums.at[3 + number, pl.ds(0, width)], target)
    entropy[...] = sums[7:8, 0:1] / sums[7:8, 128:129]
    unpack(1, joint)
    low[...] = joint[...].astype(BF)
    loads[PLANE].wait()
    half = width // 2
    for step in range(2):
        rows = pl.ds(step * half, half)
        square[1, rows, :] = dot_on(low[rows, :], wk[...], 1, 0)
        leave(square.at[1, rows, :], query_h.at[rows, :])
    loads[PLANE + 1].wait()
    for step in range(2):
        rows = pl.ds(step * half, half)
        joint[rows, :] = dot_on(low[:, rows], wq[...], 0, 0)
        leave(joint.at[rows, :], key_h.at[rows, :])
    for out in outs:
        out.wait()


def products(held, wk, wq, hidden):
    width = wk.shape[0]
    square = jax.ShapeDtypeStruct((width, width), F32)
    vector = jax.ShapeDtypeStruct((width,), F32)
    return pl.pallas_call(
        products_kernel,
        in_specs=[anywhere() for unused in range(6)],
        out_specs=[anywhere() for unused in range(8)] + [in_vmem()],
        out_shape=(
            square, square, square, jax.ShapeDtypeStruct((hidden,), F32), vector, vector, vector, vector,
            jax.ShapeDtypeStruct((1, 1), F32),
        ),
        scratch_shapes=[
            pltpu.VMEM((8, 1024), F32),
            pltpu.VMEM((PLANE,) + held[0].shape, BF),
            pltpu.VMEM((width, width), BF),
            pltpu.VMEM((width, width), BF),
            pltpu.VMEM((2, width, width), F32),
            pltpu.VMEM((width, width), F32),
            pltpu.VMEM((width, width), BF),
            pltpu.SemaphoreType.DMA((PLANE + 2,)),
            pltpu.SemaphoreType.DMA((12,)),
        ],
        name="products",
        compiler_params=pltpu.CompilerParams(vmem_limit_bytes=VMEM_BYTES),
    )(*held, wk, wq)


def plane_order(step):
    order = []
    for index in range(32):
        wide, narrow = index // 4, index % 4
        wide, narrow = wide ^ (step // 2), narrow ^ (2 * (step % 2))
        order.append((index, wide * 4 + narrow))
    return order

def per_device(
    joined,
    block_input, segments, real_mask, qkv_weight, attn_out_weight, ffn_in_weight, ffn_bias, ffn_out_weight,
    first_gain, first_shift, second_gain, second_shift, adapter_down, adapter_up,
    joining_query, joining_key, joining_value, cotangent,
):
    row_count, seq_len, width = block_input.shape
    tokens = block_input.reshape(seq_len, width)
    units = adapter_down.shape[2]
    down = jnp.transpose(adapter_down, (2, 1, 0)).reshape(ADAPTERS * units, width)
    up = jnp.transpose(adapter_up, (1, 0, 2)).reshape(ADAPTERS * units, width)
    if not joined:
        down, up = (lax.all_gather(part, "narrow", axis=0, tiled=True) for part in (down, up))
    seg_row = segments.reshape(1, seq_len)
    packed, context, log_total = attend(tokens, qkv_weight, seg_row)
    out, grad_row, grad_context, value_sum, joint_sum, sums, inner = middle(
        joined,
        tokens, cotangent.reshape(seq_len, width), context, attn_out_weight, ffn_in_weight, ffn_out_weight,
        down, up, joining_query, joining_key, joining_value, ffn_bias, first_gain, first_shift,
        second_gain, second_shift, real_mask.reshape(1, seq_len),
    )
    input_grad, out = attend_back(
        packed, inner, log_total, grad_context, seg_row, out, qkv_weight, grad_row
    )
    if joined:
        held = [value_sum] + [
            lax.ppermute(value_sum, ("wide", "narrow"), plane_order(step)) for step in range(1, PLANE)
        ]
        value_grad, query_grad, key_grad, bias_grad, gain_one, shift_one, gain_two, shift_two, entropy = products(
            held, joining_key, joining_query, ffn_bias.shape[0]
        )
    else:
        value_grad, joint_sum, sums = lax.psum((value_sum, joint_sum, sums), ("wide", "narrow"))
        high, rest = pieces(joint_sum)
        joint_sum = (dot_on(high, up, 1, 0) + dot_on(rest, up, 1, 0)).astype(BF)
        query_grad = dot_on(joint_sum, joining_key, 1, 0)
        key_grad = dot_on(joint_sum, joining_query, 0, 0)
        bias_grad = sums[:3].reshape(ffn_bias.shape[0])
        gain_one, shift_one, gain_two, shift_two = (sums[number, :width] for number in range(3, 7))
        entropy = sums[7, 0] / sums[7, 128]
    return (
        out.reshape(row_count, seq_len, width),
        input_grad.reshape(row_count, seq_len, width),
        query_grad,
        key_grad,
        value_grad,
        bias_grad,
        gain_one,
        shift_one,
        gain_two,
        shift_two,
        entropy.reshape(()),
    )


def solution(mesh):
    placed = (
        P(("wide", "narrow"), None, None),
        P(("wide", "narrow"), None),
        P(("wide", "narrow"), None),
        P(),
        P(),
        P(),
        P(),
        P(),
        P(),
        P(),
        P(),
        P(),
        P(None, None, "narrow"),
        P(None, "narrow", None),
        P(),
        P(),
        P(),
        P(("wide", "narrow"), None, None),
    )
    joined = mesh.shape["wide"] == 8 and mesh.shape["narrow"] == 4
    return jax.shard_map(
        functools.partial(per_device, joined),
        mesh=mesh,
        in_specs=placed,
        out_specs=(
            P(("wide", "narrow"), None, None),
            P(("wide", "narrow"), None, None),
            P(),
            P(),
            P(),
            P(),
            P(),
            P(),
            P(),
            P(),
            P(),
        ),
        check_vma=False,
    )
```
